32 devices in a mesh: cuts: 2 (over y), group: 16 (over z, x, core).
Axes of the slice: x: 2, y: 2, z: 4, core: 2. Of those that a mesh axis runs over, the one named last changes fastest.
Arguments:
- queries: bfloat16 [8192, 2048], P(('cuts', 'group')), may hold values from -6 to 6
- keys: bfloat16 [8192, 2048], P(('cuts', 'group')), may hold values from -6 to 6
- values: bfloat16 [8192, 2048], P(('cuts', 'group')), may hold values from -6 to 6
- window: int32 [64], P(('cuts', 'group')), may hold values from 1 to 2
- summary_index: int32 [64, 16], P(('cuts', 'group')), may hold values from 0 to 63, as said below
Outputs:
- attended: bfloat16 [8192, 2048], P(('cuts', 'group'))
The draws below stay inside these ranges and needn't reach their ends.
Inputs may be any that keep to these rules, and one draw needn't show every extreme that they name: `summary_index`: entry j of every row names one of the blocks j * 4 to (j + 1) * 4 - 1.
All inputs are finite; a program needn't handle non-finite values.
Results may differ from the reference program's by a relative error of at most 0.001.
The reference program's roundings to bfloat16 on the way count: a program that leaves them out, or rounds other values in their place, can miss the bound.
Values may be sent and summed in bfloat16 or wider, within the bound.
A program may use at most 64 MiB of HBM per device.

```python
import jax
import jax.numpy as jnp
from jax import lax

D = 2048
HEADS = 16
HEAD = 128
BLOCK = 128
WMAX = 2
SUMMARY = 16
NB = 64
STRIDE = 4
SEQ = 8192


def draw_pair(key):
    base_key = jax.random.fold_in(key, 7001)
    query_key, key_key = jax.random.split(base_key, 2)
    complete_shape = (NB, BLOCK, HEADS, HEAD)
    query_base = jnp.clip(jax.random.normal(query_key, complete_shape, jnp.float32), -6.0, 6.0)
    key_base = jnp.clip(jax.random.normal(key_key, complete_shape, jnp.float32), -6.0, 6.0)
    return (query_base.reshape(SEQ, D), key_base.reshape(SEQ, D))


def draw_queries(key, part):
    return draw_pair(key)[0].astype(jnp.bfloat16)


def draw_keys(key, part):
    return draw_pair(key)[1].astype(jnp.bfloat16)


def draw_summary_index(key, part):
    stride_key = jax.random.fold_in(key, 9103)
    offsets = jax.random.randint(stride_key, (NB, SUMMARY), 0, STRIDE, dtype=jnp.int32)
    return offsets + STRIDE * jnp.arange(SUMMARY, dtype=jnp.int32)[None, :]


def plant(entries, key, smallest, high):
    longest = entries.shape.index(max(entries.shape))
    spots = []
    for shift in (0, 1):
        where = [jax.random.randint(jax.random.fold_in(key, axis), (), 0, length) for axis, length in enumerate(entries.shape)]
        where[longest] = (where[longest] + shift) % entries.shape[longest]
        spots.append(tuple(where))
    return entries.at[spots[0]].set(smallest).at[spots[1]].set(high)


def level_of(own_key, dims, cuts, smallest, largest):
    def one(position, blocks):
        draws = jax.random.uniform(jax.random.fold_in(jax.random.fold_in(own_key, 6), position), (blocks,), jnp.float32, smallest / len(cuts), largest / len(cuts))
        return jnp.repeat(jnp.exp(draws), dims[position] // blocks).reshape((-1,) + (1,) * (len(dims) - position - 1))

    loudness = one(*cuts[0])
    for cut in cuts[1:]:
        loudness = loudness * one(*cut)
    return loudness


def scatter_about(rng, dims, scale, reach, cuts=(), held_as=jnp.bfloat16):
    values = scale * jax.random.normal(rng, dims, jnp.float32)
    if cuts:
        values = values * level_of(rng, dims, cuts, -0.22, 0.18)
    return jnp.clip(values, -reach, reach).astype(held_as)


def setup_inputs(seed: int = 0) -> dict:
    seeds = jax.random.split(jax.random.key(seed), 6)
    return {
        "queries": draw_queries(jax.random.fold_in(seeds[5], 71), 0),
        "keys": draw_keys(jax.random.fold_in(seeds[5], 71), 0),
        "values": scatter_about(seeds[2], (SEQ, D), 1.0, 6.0, ((0, 32),)),
        "window": plant(jax.random.randint(seeds[3], (NB,), 1, WMAX + 1), jax.random.fold_in(seeds[3], 1), 1, WMAX).astype(jnp.int32),
        "summary_index": draw_summary_index(jax.random.fold_in(seeds[5], 71), 0),
    }


def reference(queries, keys, values, window, summary_index):
    width = queries.shape[1]
    pooled_keys = (lax.optimization_barrier(jnp.sum(keys.reshape(NB, BLOCK, width), axis=1, dtype=jnp.float32)) / jnp.sqrt(jnp.float32(BLOCK))).astype(jnp.bfloat16)
    pooled_values = (lax.optimization_barrier(jnp.sum(values.reshape(NB, BLOCK, width), axis=1, dtype=jnp.float32)) / jnp.float32(BLOCK)).astype(jnp.bfloat16)
    zeros = jnp.zeros((WMAX * BLOCK, width), jnp.bfloat16)
    keys_padded = jnp.concatenate([zeros, keys, zeros], axis=0)
    values_padded = jnp.concatenate([zeros, values, zeros], axis=0)
    span = 2 * WMAX + 1
    scale = 1.0 / jnp.sqrt(jnp.float32(HEAD))

    def one_block(block):
        start = (block * BLOCK).astype(jnp.int32)
        query_rows = lax.dynamic_slice_in_dim(queries, start, BLOCK, 0).reshape(BLOCK, HEADS, HEAD).astype(jnp.float32)
        key_rows = lax.dynamic_slice_in_dim(keys_padded, start, span * BLOCK, 0).reshape(span * BLOCK, HEADS, HEAD).astype(jnp.float32)
        value_rows = lax.dynamic_slice_in_dim(values_padded, start, span * BLOCK, 0).reshape(span * BLOCK, HEADS, HEAD).astype(jnp.float32)
        chosen = summary_index[block]
        summary_keys = pooled_keys[chosen].reshape(SUMMARY, HEADS, HEAD).astype(jnp.float32)
        sum_values = pooled_values[chosen].reshape(SUMMARY, HEADS, HEAD).astype(jnp.float32)
        neighbour = block - WMAX + jnp.arange(span, dtype=jnp.int32)
        allowed = (jnp.abs(neighbour - block) <= window[block]) & (neighbour >= 0) & (neighbour < NB)
        allowed = jnp.repeat(allowed, BLOCK)
        local_scores = jnp.einsum('qhd,khd->hqk', query_rows, key_rows) * scale
        local_scores = jnp.where(allowed[None, None, :], local_scores, -1e+30)
        far_scores = jnp.einsum('qhd,khd->hqk', query_rows, summary_keys) * scale
        top = jnp.maximum(lax.optimization_barrier(jnp.max(local_scores, axis=2)), lax.optimization_barrier(jnp.max(far_scores, axis=2)))
        local_weights = jnp.exp(local_scores - top[:, :, None])
        far_weights = jnp.exp(far_scores - top[:, :, None])
        total = lax.optimization_barrier(jnp.sum(local_weights, axis=2)) + lax.optimization_barrier(jnp.sum(far_weights, axis=2))
        local_rounded = local_weights.astype(jnp.bfloat16).astype(jnp.float32)
        distant_rounded = far_weights.astype(jnp.bfloat16).astype(jnp.float32)
        mixed = jnp.einsum('hqk,khd->hqd', local_rounded, value_rows) + jnp.einsum('hqk,khd->hqd', distant_rounded, sum_values)
        mixed = mixed / total[:, :, None]
        return jnp.transpose(mixed, (1, 0, 2)).reshape(BLOCK, width).astype(jnp.bfloat16)
    attended = lax.map(one_block, jnp.arange(NB, dtype=jnp.int32))
    return attended.reshape(NB * BLOCK, width)
```

```python
import functools

import jax
import jax.numpy as jnp
from jax import lax
from jax.experimental import pallas as pl
from jax.experimental.pallas import tpu as pltpu
from jax.sharding import PartitionSpec as P

HEAD = 128
BLOCK = 128
REACH = 2
CHUNK_HEADS = 2
SEATS = 4
MESH = pl.DeviceIdType.MESH


def kernel(
    cuts, group,
    q_hbm, k_hbm, v_hbm, window_hbm, index_hbm, out_ref,
    qbuf, kbuf, vbuf, relay, window_ref, index_ref, own, pool, far, wbuf, fwbuf, inv,
    local_sem, k_send, k_recv, v_send, v_recv, fast_send, fast_recv,
    relay_send, relay_recv, own_send, own_recv, core_send, core_recv,
    up_send, up_recv, down_send, down_recv,
    right_send, right_recv, left_send, left_recv, go_sem,
):
    count = cuts * group
    rows, width = q_hbm.shape
    blocks = rows // BLOCK
    heads = width // HEAD
    halo = REACH * BLOCK
    span = (2 * REACH + 1) * BLOCK
    chunk = CHUNK_HEADS * HEAD
    chunks = width // chunk
    listed = index_ref.shape[1]
    levels = group // SEATS
    top = levels - 1

    cut = lax.axis_index("cuts")
    spot = lax.axis_index("group")
    me = cut * group + spot
    seat = lax.rem(spot, SEATS)
    level = spot // SEATS
    odd = lax.rem(seat, 2) == 1
    hub = (seat == 1) | (seat == 2)
    below, above = level > 0, level < top
    before, after = cut > 0, cut < cuts - 1

    fast_peer = jnp.where(odd, me - 1, me + 1)
    slow_peer = jnp.where(odd, me + 1, me - 1)
    has_slow = (slow_peer >= 0) & (slow_peer < count)
    across = jnp.where(seat < 2, me + 2, me - 2)

    lent = jnp.where(
        seat == 3,
        jnp.where(above, (top - level) * chunks // levels, chunks),
        jnp.where(
            seat == 0, jnp.where(below, level * chunks // levels, chunks), 0
        ),
    )
    lent = jnp.where(has_slow, lent, 0)
    lend_peer = jnp.where(
        seat == 3,
        jnp.where(above, me - 2, me + SEATS),
        jnp.where(below, me + 2, me - SEATS),
    )
    relay_up = (seat == 1) & above
    relay_down = (seat == 2) & below
    ends_after = (seat == 3) & (level == top) & after
    ends_before = (seat == 0) & (level == 0) & before
    relay_after = (seat == 3) & (level == 0) & before
    relay_before = (seat == 0) & (level == top) & after
    borrowed = jnp.where(
        relay_up,
        (top - level) * chunks // levels,
        jnp.where(
            relay_down,
            level * chunks // levels,
            jnp.where(relay_after | relay_before, chunks, 0),
        ),
    )
    relay_peer = jnp.where(
        relay_up | relay_before, me + (SEATS - 1), me - (SEATS - 1)
    )

    loads = [
        pltpu.make_async_copy(k_hbm, kbuf.at[pl.ds(halo, rows)], local_sem.at[0]),
        pltpu.make_async_copy(v_hbm, vbuf.at[pl.ds(halo, rows)], local_sem.at[1]),
        pltpu.make_async_copy(q_hbm, qbuf, local_sem.at[2]),
        pltpu.make_async_copy(window_hbm, window_ref, local_sem.at[3]),
        pltpu.make_async_copy(index_hbm, index_ref, local_sem.at[4]),
    ]
    for load in loads:
        load.start()

    def place(device):
        return (device // group, lax.rem(device, group))

    barrier = pltpu.get_barrier_semaphore()

    def greet(device, present=None):
        def signal():
            pl.semaphore_signal(
                barrier, inc=1, device_id=place(device), device_id_type=MESH
            )

        if present is None:
            signal()
        else:
            pl.when(present)(signal)

    greet(fast_peer)
    greet(slow_peer, has_slow)
    greet(across, hub)
    greet(me - SEATS, (hub & below) | relay_after)
    greet(me + SEATS, (hub & above) | relay_before)
    greet(me - group, hub & before)
    greet(me + group, hub & after)
    greet(me - (SEATS - 1), ((seat == 0) & below) | ends_after)
    greet(me + (SEATS - 1), ((seat == 3) & above) | ends_before)
    expected = 1
    for present in (
        has_slow, ~hub, hub & below, hub & above, hub & before, hub & after,
        relay_up, relay_down, relay_after, relay_before, ends_after, ends_before,
    ):
        expected = expected + jnp.where(present, 1, 0)

    def remote(source, target, send, recv, device):
        return pltpu.make_async_remote_copy(
            src_ref=source, dst_ref=target, send_sem=send, recv_sem=recv,
            device_id=place(device), device_id_type=MESH,
        )

    def columns_of(step):
        return pl.ds(pl.multiple_of(step * chunk, chunk), chunk)

    edge = halo + rows
    slow_from = pl.ds(pl.multiple_of(jnp.where(odd, rows, halo), BLOCK), halo)
    slow_to = pl.ds(pl.multiple_of(jnp.where(odd, 0, edge), BLOCK), halo)
    fast_from = pl.ds(pl.multiple_of(jnp.where(odd, halo, rows), BLOCK), halo)
    fast_to = pl.ds(pl.multiple_of(jnp.where(odd, edge, 0), BLOCK), halo)
    relay_to = pl.ds(
        pl.multiple_of(jnp.where(relay_up | relay_after, 0, edge), BLOCK), halo
    )

    def slow_copy(buffer, send, recv, step):
        columns = columns_of(step)
        return remote(
            buffer.at[slow_from, columns], buffer.at[slow_to, columns],
            send.at[step], recv.at[step], slow_peer,
        )

    def fast_copy(buffer, part):
        return remote(
            buffer.at[fast_from], buffer.at[fast_to],
            fast_send.at[part], fast_recv.at[part], fast_peer,
        )

    def lend_copy(step):
        return remote(
            vbuf.at[slow_from, columns_of(step)], relay.at[step],
            v_send.at[step], relay_recv.at[step], lend_peer,
        )

    def relay_copy(step):
        return remote(
            relay.at[step], vbuf.at[relay_to, columns_of(step)],
            relay_send.at[step], v_recv.at[step], relay_peer,
        )

    def own_copy(place_of, device):
        return remote(
            own, pool.at[me], own_send.at[place_of], own_recv.at[place_of], device
        )

    def quad_copy(owner, item, send, recv, device):
        held = pool.at[pl.ds(owner * group + item * SEATS, SEATS)]
        return remote(held, held, send, recv, device)

    def up_copy(item):
        return quad_copy(cut, item, up_send.at[item], up_recv.at[item], me + SEATS)

    def down_copy(item):
        return quad_copy(cut, item, down_send.at[item], down_recv.at[item], me - SEATS)

    def right_copy(owner, item):
        return quad_copy(
            owner, item, right_send.at[owner, item], right_recv.at[owner, item], me + group
        )

    def left_copy(owner, item):
        return quad_copy(
            owner, item, left_send.at[owner, item], left_recv.at[owner, item], me - group
        )

    def core_copy(owner, item):
        return quad_copy(
            owner, item, core_send.at[owner, item], core_recv.at[owner, item], fast_peer
        )

    ones = jnp.ones((heads, BLOCK), jnp.bfloat16)
    row = lax.broadcasted_iota(jnp.int32, (heads, HEAD), 0)
    for part, (buffer, divisor) in enumerate(
        ((kbuf, jnp.sqrt(jnp.float32(BLOCK))), (vbuf, jnp.float32(BLOCK)))
    ):
        loads[part].wait()
        for block in range(blocks):
            pooled = jnp.zeros((heads, HEAD), jnp.float32)
            sums = jnp.dot(
                ones,
                buffer[halo + block * BLOCK : halo + (block + 1) * BLOCK, :],
                preferred_element_type=jnp.float32,
            )
            for head in range(heads):
                pooled = jnp.where(
                    row == head, sums[:, head * HEAD : (head + 1) * HEAD], pooled
                )
            own[part, block] = (pooled / divisor).astype(jnp.bfloat16)
    pl.semaphore_wait(barrier, expected)

    @pl.when(hub)
    def _():
        own_copy(0, slow_peer).start()

    @pl.when(~hub)
    def _():
        own_copy(1, across).start()
        own_copy(2, fast_peer).start()

    def send_slow():
        @pl.when(has_slow)
        def _():
            @pl.loop(0, chunks)
            def _(step):
                slow_copy(kbuf, k_send, k_recv, step).start()

            @pl.loop(lent, chunks)
            def _(step):
                slow_copy(vbuf, v_send, v_recv, step).start()

    @pl.loop(0, lent)
    def _(step):
        lend_copy(step).start()

    pl.when(hub)(send_slow)
    fast_copy(kbuf, 0).start()
    fast_copy(vbuf, 1).start()

    @pl.when(me == 0)
    def _():
        kbuf[pl.ds(0, halo), :] = jnp.zeros((halo, width), kbuf.dtype)
        vbuf[pl.ds(0, halo), :] = jnp.zeros((halo, width), vbuf.dtype)

    @pl.when(me == count - 1)
    def _():
        kbuf[pl.ds(edge, halo), :] = jnp.zeros((halo, width), kbuf.dtype)
        vbuf[pl.ds(edge, halo), :] = jnp.zeros((halo, width), vbuf.dtype)

    def spread(item):
        @pl.when(after)
        def _():
            right_copy(cut, item).start()

        @pl.when(before)
        def _():
            left_copy(cut, item).start()

        core_copy(cut, item).start()

    @pl.when(hub)
    def _():
        pool[me] = own[...]
        own_copy(0, slow_peer).wait_recv()
        own_copy(1, across).wait_recv()
        own_copy(2, fast_peer).wait_recv()

        @pl.when(above)
        def _():
            up_copy(level).start()

        @pl.when(below)
        def _():
            down_copy(level).start()

        @pl.when(relay_up | relay_down)
        def _():
            pl.semaphore_signal(
                go_sem, inc=1, device_id=place(relay_peer), device_id_type=MESH
            )

        spread(level)

        @pl.loop(1, levels)
        def _(hop):
            @pl.when(level >= hop)
            def _():
                up_copy(level - hop).wait_recv()

                @pl.when(above)
                def _():
                    up_copy(level - hop).start()

                spread(level - hop)

            @pl.when(level + hop < levels)
            def _():
                down_copy(level + hop).wait_recv()

                @pl.when(below)
                def _():
                    down_copy(level + hop).start()

                spread(level + hop)

        @pl.loop(1, cuts)
        def _(hop):
            @pl.loop(0, levels)
            def _(item):
                @pl.when(cut >= hop)
                def _():
                    right_copy(cut - hop, item).wait_recv()

                    @pl.when(after)
                    def _():
                        right_copy(cut - hop, item).start()

                    core_copy(cut - hop, item).start()

                @pl.when(cut + hop < cuts)
                def _():
                    left_copy(cut + hop, item).wait_recv()

                    @pl.when(before)
                    def _():
                        left_copy(cut + hop, item).start()

                    core_copy(cut + hop, item).start()

    @pl.when(~hub)
    def _():
        @pl.when(((seat == 3) & above) | ((seat == 0) & below))
        def _():
            pl.semaphore_wait(go_sem, 1)

        send_slow()

        @pl.loop(0, borrowed)
        def _(step):
            lend_copy(step).wait_recv()
            relay_copy(step).start()

        @pl.loop(0, cuts)
        def _(owner):
            @pl.loop(0, levels)
            def _(item):
                core_copy(owner, item).wait_recv()

    for load in loads[2:]:
        load.wait()

    for part in range(2):
        for block in range(blocks):
            for entry in range(listed):
                name = index_ref[block, entry]
                tile = pool[name // blocks, part, lax.rem(name, blocks)]
                far[part, block, pl.ds(entry * heads, heads), :] = tile.astype(jnp.float32)

    scale = 1.0 / jnp.sqrt(jnp.float32(HEAD))
    contract = (((1,), (1,)), ((), ()))
    total_blocks = count * blocks

    def far_rows(part, block, head):
        return far[part, block, pl.ds(head, listed, stride=heads), :].astype(jnp.bfloat16)

    fast_copy(kbuf, 0).wait_recv()

    @pl.loop(0, chunks)
    def _(step):
        @pl.when(has_slow)
        def _():
            slow_copy(kbuf, k_send, k_recv, step).wait_recv()

        for inner in range(CHUNK_HEADS):
            head = step * CHUNK_HEADS + inner
            columns = pl.ds(pl.multiple_of(head * HEAD, HEAD), HEAD)
            for block in range(blocks):
                query = qbuf[block * BLOCK : (block + 1) * BLOCK, columns]
                near_keys = kbuf[pl.ds(block * BLOCK, span), columns]
                scores = lax.dot_general(
                    query, near_keys, contract, preferred_element_type=jnp.float32
                )
                far_scores = lax.dot_general(
                    query, far_rows(0, block, head), contract,
                    preferred_element_type=jnp.float32,
                )
                own = me * blocks + block
                pieces = []
                for place_of in range(2 * REACH + 1):
                    offset = place_of - REACH
                    piece = scores[:, place_of * BLOCK : (place_of + 1) * BLOCK]
                    if offset:
                        other = own + offset
                        allowed = (
                            (window_ref[block] >= abs(offset))
                            & (other >= 0)
                            & (other < total_blocks)
                        )
                        piece = jnp.where(allowed, piece, -1e30)
                    pieces.append(piece)
                tallest = functools.reduce(jnp.maximum, pieces)
                top = jnp.maximum(
                    jnp.max(tallest, axis=1, keepdims=True),
                    jnp.max(far_scores, axis=1, keepdims=True),
                )
                weights = [jnp.exp((piece - top) * scale) for piece in pieces]
                far_weights = jnp.exp((far_scores - top) * scale)
                total = jnp.sum(
                    functools.reduce(jnp.add, weights), axis=1, keepdims=True
                ) + jnp.sum(far_weights, axis=1, keepdims=True)
                for place_of, weight in enumerate(weights):
                    wbuf[head, block, :, place_of * BLOCK : (place_of + 1) * BLOCK] = (
                        weight.astype(jnp.bfloat16)
                    )
                fwbuf[head, block] = far_weights.astype(jnp.bfloat16)
                inv[head, block] = 1.0 / total

        @pl.when(hub & (step < borrowed))
        def _():
            lend_copy(step).wait_recv()
            relay_copy(step).start()

    fast_copy(vbuf, 1).wait_recv()

    @pl.loop(0, chunks)
    def _(step):
        @pl.when(has_slow)
        def _():
            slow_copy(kbuf, k_send, k_recv, step).wait_send()
            slow_copy(vbuf, v_send, v_recv, step).wait_recv()

        for inner in range(CHUNK_HEADS):
            head = step * CHUNK_HEADS + inner
            columns = pl.ds(pl.multiple_of(head * HEAD, HEAD), HEAD)
            for block in range(blocks):
                near_values = vbuf[pl.ds(block * BLOCK, span), columns]
                mixed = jnp.dot(
                    wbuf[head, block], near_values, preferred_element_type=jnp.float32
                ) + jnp.dot(
                    fwbuf[head, block], far_rows(1, block, head),
                    preferred_element_type=jnp.float32,
                )
                out_ref[block * BLOCK : (block + 1) * BLOCK, columns] = (
                    mixed * inv[head, block]
                ).astype(out_ref.dtype)

    fast_copy(kbuf, 0).wait_send()
    fast_copy(vbuf, 1).wait_send()

    @pl.when(~hub)
    def _():
        own_copy(1, across).wait_send()
        own_copy(2, fast_peer).wait_send()

    @pl.when(hub)
    def _():
        own_copy(0, slow_peer).wait_send()

        @pl.when(above)
        def _():
            @pl.loop(0, level + 1)
            def _(item):
                up_copy(item).wait_send()

        @pl.when(below)
        def _():
            @pl.loop(level, levels)
            def _(item):
                down_copy(item).wait_send()

        @pl.loop(0, levels)
        def _(item):
            @pl.loop(0, cuts)
            def _(owner):
                core_copy(owner, item).wait_send()

            @pl.when(after)
            def _():
                @pl.loop(0, cut + 1)
                def _(owner):
                    right_copy(owner, item).wait_send()

            @pl.when(before)
            def _():
                @pl.loop(cut, cuts)
                def _(owner):
                    left_copy(owner, item).wait_send()

    @pl.loop(0, borrowed)
    def _(step):
        relay_copy(step).wait_send()

    @pl.when(has_slow)
    def _():
        @pl.loop(0, chunks)
        def _(step):
            slow_copy(vbuf, v_send, v_recv, step).wait_send()


def shards(cuts, group, queries, keys, values, window, summary_index):
    rows, width = queries.shape
    blocks = rows // BLOCK
    heads = width // HEAD
    listed = summary_index.shape[1]
    count = cuts * group
    levels = group // SEATS
    chunk = CHUNK_HEADS * HEAD
    chunks = width // chunk
    halo = REACH * BLOCK
    held = rows + 2 * halo
    span = (2 * REACH + 1) * BLOCK
    dma = pltpu.SemaphoreType.DMA
    return pl.pallas_call(
        functools.partial(kernel, cuts, group),
        out_shape=jax.ShapeDtypeStruct((rows, width), jnp.bfloat16),
        in_specs=[pl.BlockSpec(memory_space=pltpu.HBM)] * 5,
        out_specs=pl.BlockSpec(memory_space=pltpu.VMEM),
        scratch_shapes=[
            pltpu.VMEM((rows, width), jnp.bfloat16),
            pltpu.VMEM((held, width), jnp.bfloat16),
            pltpu.VMEM((held, width), jnp.bfloat16),
            pltpu.VMEM((chunks, halo, chunk), jnp.bfloat16),
            pltpu.SMEM(window.shape, jnp.int32),
            pltpu.SMEM(summary_index.shape, jnp.int32),
            pltpu.VMEM((2, blocks, heads, HEAD), jnp.bfloat16),
            pltpu.VMEM((count, 2, blocks, heads, HEAD), jnp.bfloat16),
            pltpu.VMEM((2, blocks, listed * heads, HEAD), jnp.float32),
            pltpu.VMEM((heads, blocks, BLOCK, span), jnp.bfloat16),
            pltpu.VMEM((heads, blocks, BLOCK, listed), jnp.bfloat16),
            pltpu.VMEM((heads, blocks, BLOCK, 1), jnp.float32),
            dma((5,)),
            *[dma((chunks,))] * 4,
            *[dma((2,))] * 2,
            *[dma((chunks,))] * 2,
            *[dma((3,))] * 2,
            *[dma((cuts, levels))] * 2,
            *[dma((levels,))] * 4,
            *[dma((cuts, levels))] * 4,
            pltpu.SemaphoreType.REGULAR,
        ],
        compiler_params=pltpu.CompilerParams(
            collective_id=0, has_side_effects=True, vmem_limit_bytes=48 * 1024 * 1024
        ),
    )(
        *(
            pltpu.with_memory_space_constraint(operand, pltpu.HBM)
            for operand in (queries, keys, values, window, summary_index)
        )
    )


def solution(mesh):
    return jax.shard_map(
        functools.partial(shards, mesh.shape["cuts"], mesh.shape["group"]),
        mesh=mesh,
        in_specs=(
            P(("cuts", "group"), None),
            P(("cuts", "group"), None),
            P(("cuts", "group"), None),
            P(("cuts", "group")),
            P(("cuts", "group"), None),
        ),
        out_specs=P(("cuts", "group"), None),
        check_vma=False,
    )
```

```python
import functools

import jax
import jax.numpy as jnp
from jax import lax
from jax.experimental import pallas as pl
from jax.experimental.pallas import tpu as pltpu
from jax.sharding import PartitionSpec as P

HEAD = 128
BLOCK = 128
REACH = 2
CHUNK_HEADS = 2
SEATS = 4
MESH = pl.DeviceIdType.MESH


def pieces_of(chunks, most):
    if most == 2:
        lengths = [chunks // 2, chunks - chunks // 2]
    else:
        rest = chunks - 2
        lengths = [rest - rest // 2, rest // 2, 1, 1]
    pieces, start = [], 0
    for length in lengths:
        if length:
            pieces.append((start, length))
            start += length
    return pieces


def kernel(
    cuts, group,
    q_hbm, k_hbm, v_hbm, window_hbm, index_hbm, out_ref,
    qbuf, kbuf, vbuf, relay, window_ref, index_ref, own, pool, far, wbuf, fwbuf, inv,
    local_sem, k_send, k_recv, v_send, v_recv, fast_send, fast_recv,
    relay_send, relay_recv, own_send, own_recv, core_send, core_recv,
    up_send, up_recv, down_send, down_recv,
    right_send, right_recv, left_send, left_recv, go_sem,
):
    count = cuts * group
    rows, width = q_hbm.shape
    blocks = rows // BLOCK
    heads = width // HEAD
    halo = REACH * BLOCK
    span = (2 * REACH + 1) * BLOCK
    chunk = CHUNK_HEADS * HEAD
    chunks = width // chunk
    listed = index_ref.shape[1]
    levels = group // SEATS
    top = levels - 1

    cut = lax.axis_index("cuts")
    spot = lax.axis_index("group")
    me = cut * group + spot
    seat = lax.rem(spot, SEATS)
    level = spot // SEATS
    odd = lax.rem(seat, 2) == 1
    hub = (seat == 1) | (seat == 2)
    below, above = level > 0, level < top
    before, after = cut > 0, cut < cuts - 1

    fast_peer = jnp.where(odd, me - 1, me + 1)
    slow_peer = jnp.where(odd, me + 1, me - 1)
    has_slow = (slow_peer >= 0) & (slow_peer < count)
    across = jnp.where(seat < 2, me + 2, me - 2)

    lent = jnp.where(
        seat == 3,
        jnp.where(above, (top - level) * chunks // levels, chunks),
        jnp.where(
            seat == 0, jnp.where(below, level * chunks // levels, chunks), 0
        ),
    )
    lent = jnp.where(has_slow, lent, 0)
    lend_peer = jnp.where(
        seat == 3,
        jnp.where(above, me - 2, me + SEATS),
        jnp.where(below, me + 2, me - SEATS),
    )
    relay_up = (seat == 1) & above
    relay_down = (seat == 2) & below
    ends_after = (seat == 3) & (level == top) & after
    ends_before = (seat == 0) & (level == 0) & before
    relay_after = (seat == 3) & (level == 0) & before
    relay_before = (seat == 0) & (level == top) & after
    borrowed = jnp.where(
        relay_up,
        (top - level) * chunks // levels,
        jnp.where(
            relay_down,
            level * chunks // levels,
            jnp.where(relay_after | relay_before, chunks, 0),
        ),
    )
    relay_peer = jnp.where(
        relay_up | relay_before, me + (SEATS - 1), me - (SEATS - 1)
    )

    def place(device):
        return (device // group, lax.rem(device, group))

    barrier = pltpu.get_barrier_semaphore()

    def greet(device, present=None):
        def signal():
            pl.semaphore_signal(
                barrier, inc=1, device_id=place(device), device_id_type=MESH
            )

        if present is None:
            signal()
        else:
            pl.when(present)(signal)

    greet(fast_peer)
    greet(slow_peer, has_slow)
    greet(across, hub)
    greet(me - SEATS, (hub & below) | relay_after)
    greet(me + SEATS, (hub & above) | relay_before)
    greet(me - group, hub & before)
    greet(me + group, hub & after)
    greet(me - (SEATS - 1), ((seat == 0) & below) | ends_after)
    greet(me + (SEATS - 1), ((seat == 3) & above) | ends_before)
    expected = 1
    for present in (
        has_slow, ~hub, hub & below, hub & above, hub & before, hub & after,
        relay_up, relay_down, relay_after, relay_before, ends_after, ends_before,
    ):
        expected = expected + jnp.where(present, 1, 0)

    loads = [
        pltpu.make_async_copy(k_hbm, kbuf.at[pl.ds(halo, rows)], local_sem.at[0]),
        pltpu.make_async_copy(v_hbm, vbuf.at[pl.ds(halo, rows)], local_sem.at[1]),
        pltpu.make_async_copy(q_hbm, qbuf, local_sem.at[2]),
        pltpu.make_async_copy(window_hbm, window_ref, local_sem.at[3]),
        pltpu.make_async_copy(index_hbm, index_ref, local_sem.at[4]),
    ]
    for load in loads:
        load.start()

    def remote(source, target, send, recv, device):
        return pltpu.make_async_remote_copy(
            src_ref=source, dst_ref=target, send_sem=send, recv_sem=recv,
            device_id=place(device), device_id_type=MESH,
        )

    def columns_of(step):
        return pl.ds(pl.multiple_of(step * chunk, chunk), chunk)

    key_pieces = pieces_of(chunks, 2)
    value_pieces = pieces_of(chunks, 4)
    edge = halo + rows
    slow_from = pl.ds(pl.multiple_of(jnp.where(odd, rows, halo), BLOCK), halo)
    slow_to = pl.ds(pl.multiple_of(jnp.where(odd, 0, edge), BLOCK), halo)
    fast_from = pl.ds(pl.multiple_of(jnp.where(odd, halo, rows), BLOCK), halo)
    fast_to = pl.ds(pl.multiple_of(jnp.where(odd, edge, 0), BLOCK), halo)
    relay_to = pl.ds(
        pl.multiple_of(jnp.where(relay_up | relay_after, 0, edge), BLOCK), halo
    )

    def slow_copy(buffer, send, recv, step, length=1):
        columns = pl.ds(pl.multiple_of(step * chunk, chunk), length * chunk)
        return remote(
            buffer.at[slow_from, columns], buffer.at[slow_to, columns],
            send.at[step], recv.at[step], slow_peer,
        )

    def fast_copy(buffer, part):
        return remote(
            buffer.at[fast_from], buffer.at[fast_to],
            fast_send.at[part], fast_recv.at[part], fast_peer,
        )

    def lend_copy(step):
        return remote(
            vbuf.at[slow_from, columns_of(step)], relay.at[step],
            v_send.at[step], relay_recv.at[step], lend_peer,
        )

    def relay_copy(step):
        return remote(
            relay.at[step], vbuf.at[relay_to, columns_of(step)],
            relay_send.at[step], v_recv.at[step], relay_peer,
        )

    def own_copy(place_of, device):
        return remote(
            own, pool.at[me], own_send.at[place_of], own_recv.at[place_of], device
        )

    def quad_copy(owner, item, send, recv, device):
        held = pool.at[pl.ds(owner * group + item * SEATS, SEATS)]
        return remote(held, held, send, recv, device)

    def up_copy(item):
        return quad_copy(cut, item, up_send.at[item], up_recv.at[item], me + SEATS)

    def down_copy(item):
        return quad_copy(cut, item, down_send.at[item], down_recv.at[item], me - SEATS)

    def right_copy(owner, item):
        return quad_copy(
            owner, item, right_send.at[owner, item], right_recv.at[owner, item], me + group
        )

    def left_copy(owner, item):
        return quad_copy(
            owner, item, left_send.at[owner, item], left_recv.at[owner, item], me - group
        )

    def core_copy(owner, item):
        return quad_copy(
            owner, item, core_send.at[owner, item], core_recv.at[owner, item], fast_peer
        )

    ones = jnp.ones((heads, BLOCK), jnp.bfloat16)
    row = lax.broadcasted_iota(jnp.int32, (heads, HEAD), 0)
    for part, (buffer, divisor) in enumerate(
        ((kbuf, jnp.sqrt(jnp.float32(BLOCK))), (vbuf, jnp.float32(BLOCK)))
    ):
        loads[part].wait()
        for block in range(blocks):
            pooled = jnp.zeros((heads, HEAD), jnp.float32)
            sums = jnp.dot(
                ones,
                buffer[halo + block * BLOCK : halo + (block + 1) * BLOCK, :],
                preferred_element_type=jnp.float32,
            )
            for head in range(heads):
                pooled = jnp.where(
                    row == head, sums[:, head * HEAD : (head + 1) * HEAD], pooled
                )
            own[part, block] = (pooled / divisor).astype(jnp.bfloat16)
    pl.semaphore_wait(barrier, expected)

    @pl.when(hub)
    def _():
        own_copy(0, slow_peer).start()

    @pl.when(~hub)
    def _():
        own_copy(1, across).start()
        own_copy(2, fast_peer).start()

    def send_slow(whole):
        @pl.when(has_slow)
        def _():
            for start, length in key_pieces:
                slow_copy(kbuf, k_send, k_recv, start, length).start()

            if whole:
                for start, length in value_pieces:
                    slow_copy(vbuf, v_send, v_recv, start, length).start()
            else:
                @pl.loop(lent, chunks)
                def _(step):
                    slow_copy(vbuf, v_send, v_recv, step).start()

    @pl.loop(0, lent)
    def _(step):
        lend_copy(step).start()

    pl.when(hub)(lambda: send_slow(True))
    fast_copy(kbuf, 0).start()
    fast_copy(vbuf, 1).start()

    @pl.when(me == 0)
    def _():
        kbuf[pl.ds(0, halo), :] = jnp.zeros((halo, width), kbuf.dtype)
        vbuf[pl.ds(0, halo), :] = jnp.zeros((halo, width), vbuf.dtype)

    @pl.when(me == count - 1)
    def _():
        kbuf[pl.ds(edge, halo), :] = jnp.zeros((halo, width), kbuf.dtype)
        vbuf[pl.ds(edge, halo), :] = jnp.zeros((halo, width), vbuf.dtype)

    def spread(item):
        @pl.when(after)
        def _():
            right_copy(cut, item).start()

        @pl.when(before)
        def _():
            left_copy(cut, item).start()

        core_copy(cut, item).start()

    @pl.when(hub)
    def _():
        pool[me] = own[...]
        own_copy(0, slow_peer).wait_recv()
        own_copy(1, across).wait_recv()
        own_copy(2, fast_peer).wait_recv()

        @pl.when(above)
        def _():
            up_copy(level).start()

        @pl.when(below)
        def _():
            down_copy(level).start()

        @pl.when(relay_up | relay_down)
        def _():
            pl.semaphore_signal(
                go_sem, inc=1, device_id=place(relay_peer), device_id_type=MESH
            )

        spread(level)

        @pl.loop(1, levels)
        def _(hop):
            @pl.when(level >= hop)
            def _():
                up_copy(level - hop).wait_recv()

                @pl.when(above)
                def _():
                    up_copy(level - hop).start()

                spread(level - hop)

            @pl.when(level + hop < levels)
            def _():
                down_copy(level + hop).wait_recv()

                @pl.when(below)
                def _():
                    down_copy(level + hop).start()

                spread(level + hop)

        @pl.loop(1, cuts)
        def _(hop):
            @pl.loop(0, levels)
            def _(item):
                @pl.when(cut >= hop)
                def _():
                    right_copy(cut - hop, item).wait_recv()

                    @pl.when(after)
                    def _():
                        right_copy(cut - hop, item).start()

                    core_copy(cut - hop, item).start()

                @pl.when(cut + hop < cuts)
                def _():
                    left_copy(cut + hop, item).wait_recv()

                    @pl.when(before)
                    def _():
                        left_copy(cut + hop, item).start()

                    core_copy(cut + hop, item).start()

    @pl.when(~hub)
    def _():
        @pl.when(((seat == 3) & above) | ((seat == 0) & below))
        def _():
            pl.semaphore_wait(go_sem, 1)

        send_slow(False)

        @pl.loop(0, borrowed)
        def _(step):
            lend_copy(step).wait_recv()
            relay_copy(step).start()

        @pl.loop(0, cuts)
        def _(owner):
            @pl.loop(0, levels)
            def _(item):
                core_copy(owner, item).wait_recv()

    for load in loads[2:]:
        load.wait()

    for part in range(2):
        for block in range(blocks):
            for entry in range(listed):
                name = index_ref[block, entry]
                tile = pool[name // blocks, part, lax.rem(name, blocks)]
                far[part, block, pl.ds(entry * heads, heads), :] = tile.astype(jnp.float32)

    scale = 1.0 / jnp.sqrt(jnp.float32(HEAD))
    contract = (((1,), (1,)), ((), ()))
    total_blocks = count * blocks

    def far_rows(part, block, head):
        return far[part, block, pl.ds(head, listed, stride=heads), :].astype(jnp.bfloat16)

    fast_copy(kbuf, 0).wait_recv()

    @pl.loop(0, chunks)
    def _(step):
        for start, length in key_pieces:
            @pl.when(has_slow & (step == start))
            def _():
                slow_copy(kbuf, k_send, k_recv, start, length).wait_recv()

        for inner in range(CHUNK_HEADS):
            head = step * CHUNK_HEADS + inner
            columns = pl.ds(pl.multiple_of(head * HEAD, HEAD), HEAD)
            for block in range(blocks):
                query = qbuf[block * BLOCK : (block + 1) * BLOCK, columns]
                near_keys = kbuf[pl.ds(block * BLOCK, span), columns]
                scores = lax.dot_general(
                    query, near_keys, contract, preferred_element_type=jnp.float32
                )
                far_scores = lax.dot_general(
                    query, far_rows(0, block, head), contract,
                    preferred_element_type=jnp.float32,
                )
                own = me * blocks + block
                pieces = []
                for place_of in range(2 * REACH + 1):
                    offset = place_of - REACH
                    piece = scores[:, place_of * BLOCK : (place_of + 1) * BLOCK]
                    if offset:
                        other = own + offset
                        allowed = (
                            (window_ref[block] >= abs(offset))
                            & (other >= 0)
                            & (other < total_blocks)
                        )
                        piece = jnp.where(allowed, piece, -1e30)
                    pieces.append(piece)
                tallest = functools.reduce(jnp.maximum, pieces)
                top = jnp.maximum(
                    jnp.max(tallest, axis=1, keepdims=True),
                    jnp.max(far_scores, axis=1, keepdims=True),
                )
                weights = [jnp.exp((piece - top) * scale) for piece in pieces]
                far_weights = jnp.exp((far_scores - top) * scale)
                total = jnp.sum(
                    functools.reduce(jnp.add, weights), axis=1, keepdims=True
                ) + jnp.sum(far_weights, axis=1, keepdims=True)
                for place_of, weight in enumerate(weights):
                    wbuf[head, block, :, place_of * BLOCK : (place_of + 1) * BLOCK] = (
                        weight.astype(jnp.bfloat16)
                    )
                fwbuf[head, block] = far_weights.astype(jnp.bfloat16)
                inv[head, block] = 1.0 / total

        @pl.when(hub & (step < borrowed))
        def _():
            lend_copy(step).wait_recv()
            relay_copy(step).start()

    fast_copy(kbuf, 0).wait_send()
    fast_copy(vbuf, 1).wait_send()

    @pl.when(~hub)
    def _():
        own_copy(1, across).wait_send()
        own_copy(2, fast_peer).wait_send()

    @pl.when(hub)
    def _():
        own_copy(0, slow_peer).wait_send()

        @pl.when(above)
        def _():
            @pl.loop(0, level + 1)
            def _(item):
                up_copy(item).wait_send()

        @pl.when(below)
        def _():
            @pl.loop(level, levels)
            def _(item):
                down_copy(item).wait_send()

        @pl.loop(0, levels)
        def _(item):
            @pl.loop(0, cuts)
            def _(owner):
                core_copy(owner, item).wait_send()

            @pl.when(after)
            def _():
                @pl.loop(0, cut + 1)
                def _(owner):
                    right_copy(owner, item).wait_send()

            @pl.when(before)
            def _():
                @pl.loop(cut, cuts)
                def _(owner):
                    left_copy(owner, item).wait_send()

    fast_copy(vbuf, 1).wait_recv()

    @pl.loop(0, chunks)
    def _(step):
        for start, length in value_pieces:
            @pl.when(hub & has_slow & (step == start))
            def _():
                slow_copy(vbuf, v_send, v_recv, start, length).wait_recv()

        @pl.when(~hub & has_slow)
        def _():
            slow_copy(vbuf, v_send, v_recv, step).wait_recv()

        for inner in range(CHUNK_HEADS):
            head = step * CHUNK_HEADS + inner
            columns = pl.ds(pl.multiple_of(head * HEAD, HEAD), HEAD)
            for block in range(blocks):
                near_values = vbuf[pl.ds(block * BLOCK, span), columns]
                mixed = jnp.dot(
                    wbuf[head, block], near_values, preferred_element_type=jnp.float32
                ) + jnp.dot(
                    fwbuf[head, block], far_rows(1, block, head),
                    preferred_element_type=jnp.float32,
                )
                out_ref[block * BLOCK : (block + 1) * BLOCK, columns] = (
                    mixed * inv[head, block]
                ).astype(out_ref.dtype)

    @pl.loop(0, borrowed)
    def _(step):
        relay_copy(step).wait_send()

    @pl.when(has_slow)
    def _():
        for start, length in key_pieces:
            slow_copy(kbuf, k_send, k_recv, start, length).wait_send()

    @pl.when(hub & has_slow)
    def _():
        for start, length in value_pieces:
            slow_copy(vbuf, v_send, v_recv, start, length).wait_send()

    @pl.when(~hub & has_slow)
    def _():
        @pl.loop(0, chunks)
        def _(step):
            slow_copy(vbuf, v_send, v_recv, step).wait_send()


def shards(cuts, group, queries, keys, values, window, summary_index):
    rows, width = queries.shape
    blocks = rows // BLOCK
    heads = width // HEAD
    listed = summary_index.shape[1]
    count = cuts * group
    levels = group // SEATS
    chunk = CHUNK_HEADS * HEAD
    chunks = width // chunk
    halo = REACH * BLOCK
    held = rows + 2 * halo
    span = (2 * REACH + 1) * BLOCK
    dma = pltpu.SemaphoreType.DMA
    return pl.pallas_call(
        functools.partial(kernel, cuts, group),
        out_shape=jax.ShapeDtypeStruct((rows, width), jnp.bfloat16),
        in_specs=[pl.BlockSpec(memory_space=pltpu.HBM)] * 5,
        out_specs=pl.BlockSpec(memory_space=pltpu.VMEM),
        scratch_shapes=[
            pltpu.VMEM((rows, width), jnp.bfloat16),
            pltpu.VMEM((held, width), jnp.bfloat16),
            pltpu.VMEM((held, width), jnp.bfloat16),
            pltpu.VMEM((chunks, halo, chunk), jnp.bfloat16),
            pltpu.SMEM(window.shape, jnp.int32),
            pltpu.SMEM(summary_index.shape, jnp.int32),
            pltpu.VMEM((2, blocks, heads, HEAD), jnp.bfloat16),
            pltpu.VMEM((count, 2, blocks, heads, HEAD), jnp.bfloat16),
            pltpu.VMEM((2, blocks, listed * heads, HEAD), jnp.float32),
            pltpu.VMEM((heads, blocks, BLOCK, span), jnp.bfloat16),
            pltpu.VMEM((heads, blocks, BLOCK, listed), jnp.bfloat16),
            pltpu.VMEM((heads, blocks, BLOCK, 1), jnp.float32),
            dma((5,)),
            *[dma((chunks,))] * 4,
            *[dma((2,))] * 2,
            *[dma((chunks,))] * 2,
            *[dma((3,))] * 2,
            *[dma((cuts, levels))] * 2,
            *[dma((levels,))] * 4,
            *[dma((cuts, levels))] * 4,
            pltpu.SemaphoreType.REGULAR,
        ],
        compiler_params=pltpu.CompilerParams(
            collective_id=0, has_side_effects=True, vmem_limit_bytes=48 * 1024 * 1024
        ),
    )(
        *(
            pltpu.with_memory_space_constraint(operand, pltpu.HBM)
            for operand in (queries, keys, values, window, summary_index)
        )
    )


def solution(mesh):
    return jax.shard_map(
        functools.partial(shards, mesh.shape["cuts"], mesh.shape["group"]),
        mesh=mesh,
        in_specs=(
            P(("cuts", "group"), None),
            P(("cuts", "group"), None),
            P(("cuts", "group"), None),
            P(("cuts", "group")),
            P(("cuts", "group"), None),
        ),
        out_specs=P(("cuts", "group"), None),
        check_vma=False,
    )
```

```python
import functools

import jax
import jax.numpy as jnp
from jax import lax
from jax.experimental import pallas as pl
from jax.experimental.pallas import tpu as pltpu
from jax.sharding import PartitionSpec as P

HEAD = 128
BLOCK = 128
REACH = 2
CHUNK_HEADS = 2
SEATS = 4
MESH = pl.DeviceIdType.MESH


def pieces_of(chunks, most):
    if most == 2:
        lengths = [1, chunks // 2 - 1, chunks - chunks // 2]
    else:
        rest = chunks - 2
        lengths = [rest - rest // 2, rest // 2, 1, 1]
    pieces, start = [], 0
    for length in lengths:
        if length:
            pieces.append((start, length))
            start += length
    return pieces


def kernel(
    cuts, group,
    q_hbm, k_hbm, v_hbm, window_hbm, index_hbm, out_ref,
    qbuf, kbuf, vbuf, relay, window_ref, index_ref, own, pool, far, wbuf, fwbuf, inv,
    local_sem, k_send, k_recv, v_send, v_recv, fast_send, fast_recv,
    relay_send, relay_recv, own_send, own_recv, core_send, core_recv,
    up_send, up_recv, down_send, down_recv,
    right_send, right_recv, left_send, left_recv, go_sem, far_sem,
):
    count = cuts * group
    rows, width = q_hbm.shape
    blocks = rows // BLOCK
    heads = width // HEAD
    halo = REACH * BLOCK
    span = (2 * REACH + 1) * BLOCK
    chunk = CHUNK_HEADS * HEAD
    chunks = width // chunk
    listed = index_ref.shape[1]
    levels = group // SEATS
    top = levels - 1

    cut = lax.axis_index("cuts")
    spot = lax.axis_index("group")
    me = cut * group + spot
    seat = lax.rem(spot, SEATS)
    level = spot // SEATS
    odd = lax.rem(seat, 2) == 1
    hub = (seat == 1) | (seat == 2)
    below, above = level > 0, level < top
    before, after = cut > 0, cut < cuts - 1

    fast_peer = jnp.where(odd, me - 1, me + 1)
    slow_peer = jnp.where(odd, me + 1, me - 1)
    has_slow = (slow_peer >= 0) & (slow_peer < count)
    across = jnp.where(seat < 2, me + 2, me - 2)

    lent = jnp.where(
        seat == 3,
        jnp.where(above, (top - level) * chunks // levels, chunks),
        jnp.where(
            seat == 0, jnp.where(below, level * chunks // levels, chunks), 0
        ),
    )
    lent = jnp.where(has_slow, lent, 0)
    lend_peer = jnp.where(
        seat == 3,
        jnp.where(above, me - 2, me + SEATS),
        jnp.where(below, me + 2, me - SEATS),
    )
    relay_up = (seat == 1) & above
    relay_down = (seat == 2) & below
    ends_after = (seat == 3) & (level == top) & after
    ends_before = (seat == 0) & (level == 0) & before
    relay_after = (seat == 3) & (level == 0) & before
    relay_before = (seat == 0) & (level == top) & after
    borrowed = jnp.where(
        relay_up,
        (top - level) * chunks // levels,
        jnp.where(
            relay_down,
            level * chunks // levels,
            jnp.where(relay_after | relay_before, chunks, 0),
        ),
    )
    relay_peer = jnp.where(
        relay_up | relay_before, me + (SEATS - 1), me - (SEATS - 1)
    )

    def place(device):
        return (device // group, lax.rem(device, group))

    barrier = pltpu.get_barrier_semaphore()

    def greet(device, present=None):
        def signal():
            pl.semaphore_signal(
                barrier, inc=1, device_id=place(device), device_id_type=MESH
            )

        if present is None:
            signal()
        else:
            pl.when(present)(signal)

    greet(slow_peer, has_slow)
    greet(fast_peer)
    greet(across, hub)
    greet(fast_peer - SEATS, hub & below)
    greet(fast_peer + SEATS, hub & above)
    greet(fast_peer - group, hub & before)
    greet(fast_peer + group, hub & after)
    greet(me - SEATS, relay_after)
    greet(me + SEATS, relay_before)
    greet(me - SEATS, (seat == 0) & below)
    greet(me + SEATS, (seat == 3) & above)
    greet(me - (SEATS - 1), ends_after)
    greet(me + (SEATS - 1), ends_before)
    expected = 1
    for present in (
        has_slow, ~hub, ~hub & below, ~hub & above, ~hub & before, ~hub & after,
        (seat == 0) & above, (seat == 3) & below,
        relay_after, relay_before, ends_after, ends_before,
    ):
        expected = expected + jnp.where(present, 1, 0)

    loads = [
        pltpu.make_async_copy(k_hbm, kbuf.at[pl.ds(halo, rows)], local_sem.at[0]),
        pltpu.make_async_copy(v_hbm, vbuf.at[pl.ds(halo, rows)], local_sem.at[1]),
        pltpu.make_async_copy(q_hbm, qbuf, local_sem.at[2]),
        pltpu.make_async_copy(window_hbm, window_ref, local_sem.at[3]),
        pltpu.make_async_copy(index_hbm, index_ref, local_sem.at[4]),
    ]
    for load in loads:
        load.start()

    def remote(source, target, send, recv, device):
        return pltpu.make_async_remote_copy(
            src_ref=source, dst_ref=target, send_sem=send, recv_sem=recv,
            device_id=place(device), device_id_type=MESH,
        )

    def columns_of(step):
        return pl.ds(pl.multiple_of(step * chunk, chunk), chunk)

    key_pieces = pieces_of(chunks, 2)
    value_pieces = pieces_of(chunks, 4)
    edge = halo + rows
    slow_from = pl.ds(pl.multiple_of(jnp.where(odd, rows, halo), BLOCK), halo)
    first_from = pl.ds(pl.multiple_of(jnp.where(odd, rows - halo, 0), BLOCK), halo)
    slow_to = pl.ds(pl.multiple_of(jnp.where(odd, 0, edge), BLOCK), halo)
    fast_from = pl.ds(pl.multiple_of(jnp.where(odd, halo, rows), BLOCK), halo)
    fast_to = pl.ds(pl.multiple_of(jnp.where(odd, edge, 0), BLOCK), halo)
    relay_to = pl.ds(
        pl.multiple_of(jnp.where(relay_up | relay_after, 0, edge), BLOCK), halo
    )

    def slow_copy(buffer, send, recv, step, length=1):
        columns = pl.ds(pl.multiple_of(step * chunk, chunk), length * chunk)
        return remote(
            buffer.at[slow_from, columns], buffer.at[slow_to, columns],
            send.at[step], recv.at[step], slow_peer,
        )

    def fast_copy(buffer, part):
        return remote(
            buffer.at[fast_from], buffer.at[fast_to],
            fast_send.at[part], fast_recv.at[part], fast_peer,
        )

    def lend_copy(step):
        return remote(
            vbuf.at[slow_from, columns_of(step)], relay.at[step],
            v_send.at[step], relay_recv.at[step], lend_peer,
        )

    def relay_copy(step):
        return remote(
            relay.at[step], vbuf.at[relay_to, columns_of(step)],
            relay_send.at[step], v_recv.at[step], relay_peer,
        )

    def own_copy(place_of, device):
        return remote(
            own, pool.at[me], own_send.at[place_of], own_recv.at[place_of], device
        )

    def quad_copy(owner, item, send, recv, device):
        held = pool.at[pl.ds(owner * group + item * SEATS, SEATS)]
        return remote(held, held, send, recv, device)

    def up_copy(item):
        return quad_copy(cut, item, up_send.at[item], up_recv.at[item], me + SEATS)

    def down_copy(item):
        return quad_copy(cut, item, down_send.at[item], down_recv.at[item], me - SEATS)

    def right_copy(owner, item):
        return quad_copy(
            owner, item, right_send.at[owner, item], right_recv.at[owner, item], me + group
        )

    def left_copy(owner, item):
        return quad_copy(
            owner, item, left_send.at[owner, item], left_recv.at[owner, item], me - group
        )

    def core_copy(owner, item):
        return quad_copy(
            owner, item, core_send.at[owner, item], core_recv.at[owner, item], fast_peer
        )

    def first_copy():
        length = key_pieces[0][1] * chunk
        return remote(
            k_hbm.at[first_from, pl.ds(0, length)], kbuf.at[slow_to, pl.ds(0, length)],
            k_send.at[0], k_recv.at[0], slow_peer,
        )

    @pl.when(hub)
    def _():
        pl.semaphore_wait(barrier, expected)

        @pl.when(has_slow)
        def _():
            first_copy().start()

    ones = jnp.ones((heads, BLOCK), jnp.bfloat16)
    row = lax.broadcasted_iota(jnp.int32, (heads, HEAD), 0)
    for part, (buffer, divisor) in enumerate(
        ((kbuf, jnp.sqrt(jnp.float32(BLOCK))), (vbuf, jnp.float32(BLOCK)))
    ):
        loads[part].wait()
        for block in range(blocks):
            pooled = jnp.zeros((heads, HEAD), jnp.float32)
            sums = jnp.dot(
                ones,
                buffer[halo + block * BLOCK : halo + (block + 1) * BLOCK, :],
                preferred_element_type=jnp.float32,
            )
            for head in range(heads):
                pooled = jnp.where(
                    row == head, sums[:, head * HEAD : (head + 1) * HEAD], pooled
                )
            own[part, block] = (pooled / divisor).astype(jnp.bfloat16)
    @pl.when(~hub)
    def _():
        pl.semaphore_wait(barrier, expected)

    @pl.when(hub)
    def _():
        own_copy(0, slow_peer).start()

    @pl.when(~hub)
    def _():
        own_copy(1, across).start()
        own_copy(2, fast_peer).start()
        pl.semaphore_signal(
            far_sem, inc=1, device_id=place(fast_peer), device_id_type=MESH
        )

    def send_slow(whole):
        @pl.when(has_slow)
        def _():
            for start, length in key_pieces[1 if whole else 0 :]:
                slow_copy(kbuf, k_send, k_recv, start, length).start()

            if whole:
                for start, length in value_pieces:
                    slow_copy(vbuf, v_send, v_recv, start, length).start()
            else:
                @pl.loop(lent, chunks)
                def _(step):
                    slow_copy(vbuf, v_send, v_recv, step).start()

    @pl.loop(0, lent)
    def _(step):
        lend_copy(step).start()

    pl.when(hub)(lambda: send_slow(True))
    fast_copy(kbuf, 0).start()
    fast_copy(vbuf, 1).start()

    @pl.when(me == 0)
    def _():
        kbuf[pl.ds(0, halo), :] = jnp.zeros((halo, width), kbuf.dtype)
        vbuf[pl.ds(0, halo), :] = jnp.zeros((halo, width), vbuf.dtype)

    @pl.when(me == count - 1)
    def _():
        kbuf[pl.ds(edge, halo), :] = jnp.zeros((halo, width), kbuf.dtype)
        vbuf[pl.ds(edge, halo), :] = jnp.zeros((halo, width), vbuf.dtype)

    def spread(item):
        @pl.when(after)
        def _():
            right_copy(cut, item).start()

        @pl.when(before)
        def _():
            left_copy(cut, item).start()

        core_copy(cut, item).start()

    @pl.when(hub)
    def _():
        pool[me] = own[...]
        own_copy(0, slow_peer).wait_recv()
        own_copy(1, across).wait_recv()
        own_copy(2, fast_peer).wait_recv()
        pl.semaphore_wait(far_sem, 1)

        @pl.when(above)
        def _():
            up_copy(level).start()

        @pl.when(below)
        def _():
            down_copy(level).start()

        @pl.when(relay_up | relay_down)
        def _():
            pl.semaphore_signal(
                go_sem, inc=1, device_id=place(relay_peer), device_id_type=MESH
            )

        spread(level)

        @pl.loop(1, levels)
        def _(hop):
            @pl.when(level >= hop)
            def _():
                up_copy(level - hop).wait_recv()

                @pl.when(above)
                def _():
                    up_copy(level - hop).start()

                spread(level - hop)

            @pl.when(level + hop < levels)
            def _():
                down_copy(level + hop).wait_recv()

                @pl.when(below)
                def _():
                    down_copy(level + hop).start()

                spread(level + hop)

        @pl.loop(1, cuts)
        def _(hop):
            @pl.loop(0, levels)
            def _(item):
                @pl.when(cut >= hop)
                def _():
                    right_copy(cut - hop, item).wait_recv()

                    @pl.when(after)
                    def _():
                        right_copy(cut - hop, item).start()

                    core_copy(cut - hop, item).start()

                @pl.when(cut + hop < cuts)
                def _():
                    left_copy(cut + hop, item).wait_recv()

                    @pl.when(before)
                    def _():
                        left_copy(cut + hop, item).start()

                    core_copy(cut + hop, item).start()

    @pl.when(~hub)
    def _():
        @pl.when(((seat == 3) & above) | ((seat == 0) & below))
        def _():
            pl.semaphore_wait(go_sem, 1)

        @pl.when(ends_after | ends_before)
        def _():
            @pl.loop(0, chunks)
            def _(step):
                lend_copy(step).wait_send()

        send_slow(False)

        @pl.loop(0, borrowed)
        def _(step):
            lend_copy(step).wait_recv()
            relay_copy(step).start()

        @pl.loop(0, cuts)
        def _(owner):
            @pl.loop(0, levels)
            def _(item):
                core_copy(owner, item).wait_recv()

    for load in loads[2:]:
        load.wait()

    for part in range(2):
        for block in range(blocks):
            for entry in range(listed):
                name = index_ref[block, entry]
                tile = pool[name // blocks, part, lax.rem(name, blocks)]
                far[part, block, pl.ds(entry * heads, heads), :] = tile.astype(jnp.float32)

    scale = 1.0 / jnp.sqrt(jnp.float32(HEAD))
    contract = (((1,), (1,)), ((), ()))
    total_blocks = count * blocks

    def far_rows(part, block, head):
        return far[part, block, pl.ds(head, listed, stride=heads), :].astype(jnp.bfloat16)

    fast_copy(kbuf, 0).wait_recv()

    @pl.loop(0, chunks)
    def _(step):
        for start, length in key_pieces:
            @pl.when(has_slow & (step == start))
            def _():
                slow_copy(kbuf, k_send, k_recv, start, length).wait_recv()

        for inner in range(CHUNK_HEADS):
            head = step * CHUNK_HEADS + inner
            columns = pl.ds(pl.multiple_of(head * HEAD, HEAD), HEAD)
            for block in range(blocks):
                query = qbuf[block * BLOCK : (block + 1) * BLOCK, columns]
                near_keys = kbuf[pl.ds(block * BLOCK, span), columns]
                scores = lax.dot_general(
                    query, near_keys, contract, preferred_element_type=jnp.float32
                )
                far_scores = lax.dot_general(
                    query, far_rows(0, block, head), contract,
                    preferred_element_type=jnp.float32,
                )
                own = me * blocks + block
                pieces = []
                for place_of in range(2 * REACH + 1):
                    offset = place_of - REACH
                    piece = scores[:, place_of * BLOCK : (place_of + 1) * BLOCK]
                    if offset:
                        other = own + offset
                        allowed = (
                            (window_ref[block] >= abs(offset))
                            & (other >= 0)
                            & (other < total_blocks)
                        )
                        piece = jnp.where(allowed, piece, -1e30)
                    pieces.append(piece)
                tallest = functools.reduce(jnp.maximum, pieces)
                top = jnp.maximum(
                    jnp.max(tallest, axis=1, keepdims=True),
                    jnp.max(far_scores, axis=1, keepdims=True),
                )
                weights = [jnp.exp((piece - top) * scale) for piece in pieces]
                far_weights = jnp.exp((far_scores - top) * scale)
                total = jnp.sum(
                    functools.reduce(jnp.add, weights), axis=1, keepdims=True
                ) + jnp.sum(far_weights, axis=1, keepdims=True)
                for place_of, weight in enumerate(weights):
                    wbuf[head, block, :, place_of * BLOCK : (place_of + 1) * BLOCK] = (
                        weight.astype(jnp.bfloat16)
                    )
                fwbuf[head, block] = far_weights.astype(jnp.bfloat16)
                inv[head, block] = 1.0 / total

        @pl.when(hub & (step < borrowed))
        def _():
            lend_copy(step).wait_recv()
            relay_copy(step).start()

    fast_copy(kbuf, 0).wait_send()
    fast_copy(vbuf, 1).wait_send()

    @pl.when(~hub)
    def _():
        own_copy(1, across).wait_send()
        own_copy(2, fast_peer).wait_send()

    @pl.when(hub)
    def _():
        own_copy(0, slow_peer).wait_send()

        @pl.when(above)
        def _():
            @pl.loop(0, level + 1)
            def _(item):
                up_copy(item).wait_send()

        @pl.when(below)
        def _():
            @pl.loop(level, levels)
            def _(item):
                down_copy(item).wait_send()

        @pl.loop(0, levels)
        def _(item):
            @pl.loop(0, cuts)
            def _(owner):
                core_copy(owner, item).wait_send()

            @pl.when(after)
            def _():
                @pl.loop(0, cut + 1)
                def _(owner):
                    right_copy(owner, item).wait_send()

            @pl.when(before)
            def _():
                @pl.loop(cut, cuts)
                def _(owner):
                    left_copy(owner, item).wait_send()

    fast_copy(vbuf, 1).wait_recv()

    @pl.loop(0, chunks)
    def _(step):
        for start, length in value_pieces:
            @pl.when(hub & has_slow & (step == start))
            def _():
                slow_copy(vbuf, v_send, v_recv, start, length).wait_recv()

        @pl.when(~hub & has_slow)
        def _():
            slow_copy(vbuf, v_send, v_recv, step).wait_recv()

        for inner in range(CHUNK_HEADS):
            head = step * CHUNK_HEADS + inner
            columns = pl.ds(pl.multiple_of(head * HEAD, HEAD), HEAD)
            for block in range(blocks):
                near_values = vbuf[pl.ds(block * BLOCK, span), columns]
                mixed = jnp.dot(
                    wbuf[head, block], near_values, preferred_element_type=jnp.float32
                ) + jnp.dot(
                    fwbuf[head, block], far_rows(1, block, head),
                    preferred_element_type=jnp.float32,
                )
                out_ref[block * BLOCK : (block + 1) * BLOCK, columns] = (
                    mixed * inv[head, block]
                ).astype(out_ref.dtype)

    @pl.loop(0, borrowed)
    def _(step):
        relay_copy(step).wait_send()

    @pl.when(has_slow)
    def _():
        for start, length in key_pieces:
            slow_copy(kbuf, k_send, k_recv, start, length).wait_send()

    @pl.when(hub & has_slow)
    def _():
        for start, length in value_pieces:
            slow_copy(vbuf, v_send, v_recv, start, length).wait_send()

    @pl.when(~hub & has_slow & ~(ends_after | ends_before))
    def _():
        @pl.loop(0, chunks)
        def _(step):
            slow_copy(vbuf, v_send, v_recv, step).wait_send()


def shards(cuts, group, queries, keys, values, window, summary_index):
    rows, width = queries.shape
    blocks = rows // BLOCK
    heads = width // HEAD
    listed = summary_index.shape[1]
    count = cuts * group
    levels = group // SEATS
    chunk = CHUNK_HEADS * HEAD
    chunks = width // chunk
    halo = REACH * BLOCK
    held = rows + 2 * halo
    span = (2 * REACH + 1) * BLOCK
    dma = pltpu.SemaphoreType.DMA
    return pl.pallas_call(
        functools.partial(kernel, cuts, group),
        out_shape=jax.ShapeDtypeStruct((rows, width), jnp.bfloat16),
        in_specs=[pl.BlockSpec(memory_space=pltpu.HBM)] * 5,
        out_specs=pl.BlockSpec(memory_space=pltpu.VMEM),
        scratch_shapes=[
            pltpu.VMEM((rows, width), jnp.bfloat16),
            pltpu.VMEM((held, width), jnp.bfloat16),
            pltpu.VMEM((held, width), jnp.bfloat16),
            pltpu.VMEM((chunks, halo, chunk), jnp.bfloat16),
            pltpu.SMEM(window.shape, jnp.int32),
            pltpu.SMEM(summary_index.shape, jnp.int32),
            pltpu.VMEM((2, blocks, heads, HEAD), jnp.bfloat16),
            pltpu.VMEM((count, 2, blocks, heads, HEAD), jnp.bfloat16),
            pltpu.VMEM((2, blocks, listed * heads, HEAD), jnp.float32),
            pltpu.VMEM((heads, blocks, BLOCK, span), jnp.bfloat16),
            pltpu.VMEM((heads, blocks, BLOCK, listed), jnp.bfloat16),
            pltpu.VMEM((heads, blocks, BLOCK, 1), jnp.float32),
            dma((5,)),
            *[dma((chunks,))] * 4,
            *[dma((2,))] * 2,
            *[dma((chunks,))] * 2,
            *[dma((3,))] * 2,
            *[dma((cuts, levels))] * 2,
            *[dma((levels,))] * 4,
            *[dma((cuts, levels))] * 4,
            *[pltpu.SemaphoreType.REGULAR] * 2,
        ],
        compiler_params=pltpu.CompilerParams(
            collective_id=0, has_side_effects=True, vmem_limit_bytes=48 * 1024 * 1024
        ),
    )(
        *(
            pltpu.with_memory_space_constraint(operand, pltpu.HBM)
            for operand in (queries, keys, values, window, summary_index)
        )
    )


def solution(mesh):
    return jax.shard_map(
        functools.partial(shards, mesh.shape["cuts"], mesh.shape["group"]),
        mesh=mesh,
        in_specs=(
            P(("cuts", "group"), None),
            P(("cuts", "group"), None),
            P(("cuts", "group"), None),
            P(("cuts", "group")),
            P(("cuts", "group"), None),
        ),
        out_specs=P(("cuts", "group"), None),
        check_vma=False,
    )
```

```python
import functools

import jax
import jax.numpy as jnp
from jax import lax
from jax.experimental import pallas as pl
from jax.experimental.pallas import tpu as pltpu
from jax.sharding import PartitionSpec as P

HEAD = 128
BLOCK = 128
REACH = 2
CHUNK_HEADS = 2
SEATS = 4
QUARTERS = 4
MESH = pl.DeviceIdType.MESH


def pieces_of(chunks, most):
    if most == 2:
        lengths = [1, chunks // 2 - 1, chunks - chunks // 2]
    else:
        rest = chunks - 2
        lengths = [rest - rest // 2, rest // 2, 1, 1]
    pieces, start = [], 0
    for length in lengths:
        if length:
            pieces.append((start, length))
            start += length
    return pieces


def kernel(
    cuts, group,
    q_hbm, k_hbm, v_hbm, window_hbm, index_hbm, out_ref,
    qbuf, kbuf, vbuf, relay, window_ref, index_ref, own, pool, far, wbuf, fwbuf, inv,
    local_sem, k_send, k_recv, v_send, v_recv, fast_send, fast_recv,
    relay_send, relay_recv, part_send, part_recv, pass_send, own_send, own_recv, core_send, core_recv,
    up_send, up_recv, down_send, down_recv,
    right_send, right_recv, left_send, left_recv, go_sem, far_sem,
):
    count = cuts * group
    rows, width = q_hbm.shape
    blocks = rows // BLOCK
    heads = width // HEAD
    halo = REACH * BLOCK
    span = (2 * REACH + 1) * BLOCK
    chunk = CHUNK_HEADS * HEAD
    chunks = width // chunk
    listed = index_ref.shape[1]
    levels = group // SEATS
    top = levels - 1

    cut = lax.axis_index("cuts")
    spot = lax.axis_index("group")
    me = cut * group + spot
    seat = lax.rem(spot, SEATS)
    level = spot // SEATS
    odd = lax.rem(seat, 2) == 1
    hub = (seat == 1) | (seat == 2)
    below, above = level > 0, level < top
    before, after = cut > 0, cut < cuts - 1

    fast_peer = jnp.where(odd, me - 1, me + 1)
    slow_peer = jnp.where(odd, me + 1, me - 1)
    has_slow = (slow_peer >= 0) & (slow_peer < count)
    across = jnp.where(seat < 2, me + 2, me - 2)

    trim = jnp.where(cut == 0, jnp.maximum(2 - level, 0), 0)
    upward = jnp.maximum((top - level) * chunks * QUARTERS // levels - trim, 0)
    downward = level * chunks // levels * QUARTERS
    quarters = jnp.where(
        seat == 3,
        jnp.where(above, upward, chunks * QUARTERS),
        jnp.where(seat == 0, jnp.where(below, downward, chunks * QUARTERS), 0),
    )
    quarters = jnp.where(has_slow, quarters, 0)
    lent = quarters // QUARTERS
    rest = quarters - lent * QUARTERS
    lend_peer = jnp.where(
        seat == 3,
        jnp.where(above, me - 2, me + SEATS),
        jnp.where(below, me + 2, me - SEATS),
    )
    relay_up = (seat == 1) & above
    relay_down = (seat == 2) & below
    ends_after = (seat == 3) & (level == top) & after
    ends_before = (seat == 0) & (level == 0) & before
    relay_after = (seat == 3) & (level == 0) & before
    relay_before = (seat == 0) & (level == top) & after
    taken = jnp.where(
        relay_up,
        upward,
        jnp.where(
            relay_down,
            downward,
            jnp.where(relay_after | relay_before, chunks * QUARTERS, 0),
        ),
    )
    borrowed = taken // QUARTERS
    passed = taken - borrowed * QUARTERS
    relay_peer = jnp.where(
        relay_up | relay_before, me + (SEATS - 1), me - (SEATS - 1)
    )

    def place(device):
        return (device // group, lax.rem(device, group))

    barrier = pltpu.get_barrier_semaphore()

    def greet(device, present=None):
        def signal():
            pl.semaphore_signal(
                barrier, inc=1, device_id=place(device), device_id_type=MESH
            )

        if present is None:
            signal()
        else:
            pl.when(present)(signal)

    greet(slow_peer, has_slow)
    greet(fast_peer)
    greet(across, hub)
    greet(fast_peer - SEATS, hub & below)
    greet(fast_peer + SEATS, hub & above)
    greet(fast_peer - group, hub & before)
    greet(fast_peer + group, hub & after)
    greet(me - SEATS, relay_after)
    greet(me + SEATS, relay_before)
    greet(me - SEATS, (seat == 0) & below)
    greet(me + SEATS, (seat == 3) & above)
    greet(me - (SEATS - 1), ends_after)
    greet(me + (SEATS - 1), ends_before)
    expected = 1
    for present in (
        has_slow, ~hub, ~hub & below, ~hub & above, ~hub & before, ~hub & after,
        (seat == 0) & above, (seat == 3) & below,
        relay_after, relay_before, ends_after, ends_before,
    ):
        expected = expected + jnp.where(present, 1, 0)

    loads = [
        pltpu.make_async_copy(k_hbm, kbuf.at[pl.ds(halo, rows)], local_sem.at[0]),
        pltpu.make_async_copy(v_hbm, vbuf.at[pl.ds(halo, rows)], local_sem.at[1]),
        pltpu.make_async_copy(q_hbm, qbuf, local_sem.at[2]),
        pltpu.make_async_copy(window_hbm, window_ref, local_sem.at[3]),
        pltpu.make_async_copy(index_hbm, index_ref, local_sem.at[4]),
    ]
    for load in loads:
        load.start()

    def remote(source, target, send, recv, device):
        return pltpu.make_async_remote_copy(
            src_ref=source, dst_ref=target, send_sem=send, recv_sem=recv,
            device_id=place(device), device_id_type=MESH,
        )

    def columns_of(step):
        return pl.ds(pl.multiple_of(step * chunk, chunk), chunk)

    key_pieces = pieces_of(chunks, 2)
    value_pieces = pieces_of(chunks, 4)
    edge = halo + rows
    slow_from = pl.ds(pl.multiple_of(jnp.where(odd, rows, halo), BLOCK), halo)
    first_from = pl.ds(pl.multiple_of(jnp.where(odd, rows - halo, 0), BLOCK), halo)
    slow_to = pl.ds(pl.multiple_of(jnp.where(odd, 0, edge), BLOCK), halo)
    fast_from = pl.ds(pl.multiple_of(jnp.where(odd, halo, rows), BLOCK), halo)
    fast_to = pl.ds(pl.multiple_of(jnp.where(odd, edge, 0), BLOCK), halo)
    relay_to = pl.ds(
        pl.multiple_of(jnp.where(relay_up | relay_after, 0, edge), BLOCK), halo
    )

    def slow_copy(buffer, send, recv, step, length=1):
        columns = pl.ds(pl.multiple_of(step * chunk, chunk), length * chunk)
        return remote(
            buffer.at[slow_from, columns], buffer.at[slow_to, columns],
            send.at[step], recv.at[step], slow_peer,
        )

    piece = halo // QUARTERS

    def rows_of(start, number):
        return pl.ds(pl.multiple_of(start + number * piece, piece), piece)

    def slow_part(number):
        return remote(
            vbuf.at[rows_of(jnp.where(odd, rows, halo), number), columns_of(lent)],
            vbuf.at[rows_of(jnp.where(odd, 0, edge), number), columns_of(lent)],
            part_send.at[number], v_recv.at[lent], slow_peer,
        )

    def lend_part(number):
        return remote(
            vbuf.at[rows_of(jnp.where(odd, rows, halo), number), columns_of(lent)],
            relay.at[lent, rows_of(0, number)],
            part_send.at[number], part_recv.at[number], lend_peer,
        )

    def relay_part(number):
        return remote(
            relay.at[borrowed, rows_of(0, number)],
            vbuf.at[
                rows_of(jnp.where(relay_up | relay_after, 0, edge), number),
                columns_of(borrowed),
            ],
            pass_send.at[number], v_recv.at[borrowed], relay_peer,
        )

    def take_part(number):
        return remote(
            vbuf.at[rows_of(halo, number), columns_of(borrowed)],
            relay.at[borrowed, rows_of(0, number)],
            part_send.at[number], part_recv.at[number], lend_peer,
        )

    def fast_copy(buffer, part):
        return remote(
            buffer.at[fast_from], buffer.at[fast_to],
            fast_send.at[part], fast_recv.at[part], fast_peer,
        )

    def lend_copy(step):
        return remote(
            vbuf.at[slow_from, columns_of(step)], relay.at[step],
            v_send.at[step], relay_recv.at[step], lend_peer,
        )

    def relay_copy(step):
        return remote(
            relay.at[step], vbuf.at[relay_to, columns_of(step)],
            relay_send.at[step], v_recv.at[step], relay_peer,
        )

    def own_copy(place_of, device):
        return remote(
            own, pool.at[me], own_send.at[place_of], own_recv.at[place_of], device
        )

    def quad_copy(owner, item, send, recv, device):
        held = pool.at[pl.ds(owner * group + item * SEATS, SEATS)]
        return remote(held, held, send, recv, device)

    def up_copy(item):
        return quad_copy(cut, item, up_send.at[item], up_recv.at[item], me + SEATS)

    def down_copy(item):
        return quad_copy(cut, item, down_send.at[item], down_recv.at[item], me - SEATS)

    def right_copy(owner, item):
        return quad_copy(
            owner, item, right_send.at[owner, item], right_recv.at[owner, item], me + group
        )

    def left_copy(owner, item):
        return quad_copy(
            owner, item, left_send.at[owner, item], left_recv.at[owner, item], me - group
        )

    def core_copy(owner, item):
        return quad_copy(
            owner, item, core_send.at[owner, item], core_recv.at[owner, item], fast_peer
        )

    def first_copy():
        length = key_pieces[0][1] * chunk
        return remote(
            k_hbm.at[first_from, pl.ds(0, length)], kbuf.at[slow_to, pl.ds(0, length)],
            k_send.at[0], k_recv.at[0], slow_peer,
        )

    @pl.when(hub)
    def _():
        pl.semaphore_wait(barrier, expected)

        @pl.when(has_slow)
        def _():
            first_copy().start()

    ones = jnp.ones((heads, BLOCK), jnp.bfloat16)
    row = lax.broadcasted_iota(jnp.int32, (heads, HEAD), 0)
    for part, (buffer, divisor) in enumerate(
        ((kbuf, jnp.sqrt(jnp.float32(BLOCK))), (vbuf, jnp.float32(BLOCK)))
    ):
        loads[part].wait()
        for block in range(blocks):
            pooled = jnp.zeros((heads, HEAD), jnp.float32)
            sums = jnp.dot(
                ones,
                buffer[halo + block * BLOCK : halo + (block + 1) * BLOCK, :],
                preferred_element_type=jnp.float32,
            )
            for head in range(heads):
                pooled = jnp.where(
                    row == head, sums[:, head * HEAD : (head + 1) * HEAD], pooled
                )
            own[part, block] = (pooled / divisor).astype(jnp.bfloat16)
    @pl.when(~hub)
    def _():
        pl.semaphore_wait(barrier, expected)

    @pl.when(hub)
    def _():
        own_copy(0, slow_peer).start()

    @pl.when(~hub)
    def _():
        own_copy(1, across).start()
        own_copy(2, fast_peer).start()
        pl.semaphore_signal(
            far_sem, inc=1, device_id=place(fast_peer), device_id_type=MESH
        )

    def send_slow(whole):
        @pl.when(has_slow)
        def _():
            for start, length in key_pieces[1 if whole else 0 :]:
                slow_copy(kbuf, k_send, k_recv, start, length).start()

            if whole:
                for start, length in value_pieces:
                    slow_copy(vbuf, v_send, v_recv, start, length).start()
            else:
                @pl.when(rest > 0)
                def _():
                    @pl.loop(rest, QUARTERS)
                    def _(number):
                        slow_part(number).start()

                @pl.loop(lent + jnp.where(rest > 0, 1, 0), chunks)
                def _(step):
                    slow_copy(vbuf, v_send, v_recv, step).start()

    @pl.loop(0, lent)
    def _(step):
        lend_copy(step).start()

    @pl.loop(0, rest)
    def _(number):
        lend_part(number).start()

    pl.when(hub)(lambda: send_slow(True))
    fast_copy(kbuf, 0).start()
    fast_copy(vbuf, 1).start()

    @pl.when(me == 0)
    def _():
        kbuf[pl.ds(0, halo), :] = jnp.zeros((halo, width), kbuf.dtype)
        vbuf[pl.ds(0, halo), :] = jnp.zeros((halo, width), vbuf.dtype)

    @pl.when(me == count - 1)
    def _():
        kbuf[pl.ds(edge, halo), :] = jnp.zeros((halo, width), kbuf.dtype)
        vbuf[pl.ds(edge, halo), :] = jnp.zeros((halo, width), vbuf.dtype)

    def spread(item):
        @pl.when(after)
        def _():
            right_copy(cut, item).start()

        @pl.when(before)
        def _():
            left_copy(cut, item).start()

        core_copy(cut, item).start()

    @pl.when(hub)
    def _():
        pool[me] = own[...]
        own_copy(0, slow_peer).wait_recv()
        own_copy(1, across).wait_recv()
        own_copy(2, fast_peer).wait_recv()
        pl.semaphore_wait(far_sem, 1)

        @pl.when(above)
        def _():
            up_copy(level).start()

        @pl.when(below)
        def _():
            down_copy(level).start()

        @pl.when(relay_up | relay_down)
        def _():
            pl.semaphore_signal(
                go_sem, inc=1, device_id=place(relay_peer), device_id_type=MESH
            )

        spread(level)

        @pl.loop(1, levels)
        def _(hop):
            @pl.when(level >= hop)
            def _():
                up_copy(level - hop).wait_recv()

                @pl.when(above)
                def _():
                    up_copy(level - hop).start()

                spread(level - hop)

            @pl.when(level + hop < levels)
            def _():
                down_copy(level + hop).wait_recv()

                @pl.when(below)
                def _():
                    down_copy(level + hop).start()

                spread(level + hop)

        @pl.loop(1, cuts)
        def _(hop):
            @pl.loop(0, levels)
            def _(item):
                @pl.when(cut >= hop)
                def _():
                    right_copy(cut - hop, item).wait_recv()

                    @pl.when(after)
                    def _():
                        right_copy(cut - hop, item).start()

                    core_copy(cut - hop, item).start()

                @pl.when(cut + hop < cuts)
                def _():
                    left_copy(cut + hop, item).wait_recv()

                    @pl.when(before)
                    def _():
                        left_copy(cut + hop, item).start()

                    core_copy(cut + hop, item).start()

    @pl.when(~hub)
    def _():
        @pl.when(((seat == 3) & above) | ((seat == 0) & below))
        def _():
            pl.semaphore_wait(go_sem, 1)

        @pl.when(ends_after | ends_before)
        def _():
            @pl.loop(0, chunks)
            def _(step):
                lend_copy(step).wait_send()

        send_slow(False)

        @pl.loop(0, borrowed)
        def _(step):
            lend_copy(step).wait_recv()
            relay_copy(step).start()

        @pl.loop(0, cuts)
        def _(owner):
            @pl.loop(0, levels)
            def _(item):
                core_copy(owner, item).wait_recv()

    for load in loads[2:]:
        load.wait()

    for part in range(2):
        for block in range(blocks):
            for entry in range(listed):
                name = index_ref[block, entry]
                tile = pool[name // blocks, part, lax.rem(name, blocks)]
                far[part, block, pl.ds(entry * heads, heads), :] = tile.astype(jnp.float32)

    scale = 1.0 / jnp.sqrt(jnp.float32(HEAD))
    contract = (((1,), (1,)), ((), ()))
    total_blocks = count * blocks

    def far_rows(part, block, head):
        return far[part, block, pl.ds(head, listed, stride=heads), :].astype(jnp.bfloat16)

    fast_copy(kbuf, 0).wait_recv()

    @pl.loop(0, chunks)
    def _(step):
        for start, length in key_pieces:
            @pl.when(has_slow & (step == start))
            def _():
                slow_copy(kbuf, k_send, k_recv, start, length).wait_recv()

        for inner in range(CHUNK_HEADS):
            head = step * CHUNK_HEADS + inner
            columns = pl.ds(pl.multiple_of(head * HEAD, HEAD), HEAD)
            for block in range(blocks):
                query = qbuf[block * BLOCK : (block + 1) * BLOCK, columns]
                near_keys = kbuf[pl.ds(block * BLOCK, span), columns]
                scores = lax.dot_general(
                    query, near_keys, contract, preferred_element_type=jnp.float32
                )
                far_scores = lax.dot_general(
                    query, far_rows(0, block, head), contract,
                    preferred_element_type=jnp.float32,
                )
                own = me * blocks + block
                pieces = []
                for place_of in range(2 * REACH + 1):
                    offset = place_of - REACH
                    piece = scores[:, place_of * BLOCK : (place_of + 1) * BLOCK]
                    if offset:
                        other = own + offset
                        allowed = (
                            (window_ref[block] >= abs(offset))
                            & (other >= 0)
                            & (other < total_blocks)
                        )
                        piece = jnp.where(allowed, piece, -1e30)
                    pieces.append(piece)
                tallest = functools.reduce(jnp.maximum, pieces)
                top = jnp.maximum(
                    jnp.max(tallest, axis=1, keepdims=True),
                    jnp.max(far_scores, axis=1, keepdims=True),
                )
                weights = [jnp.exp((piece - top) * scale) for piece in pieces]
                far_weights = jnp.exp((far_scores - top) * scale)
                total = jnp.sum(
                    functools.reduce(jnp.add, weights), axis=1, keepdims=True
                ) + jnp.sum(far_weights, axis=1, keepdims=True)
                for place_of, weight in enumerate(weights):
                    wbuf[head, block, :, place_of * BLOCK : (place_of + 1) * BLOCK] = (
                        weight.astype(jnp.bfloat16)
                    )
                fwbuf[head, block] = far_weights.astype(jnp.bfloat16)
                inv[head, block] = 1.0 / total

        @pl.when(hub & (step < borrowed))
        def _():
            lend_copy(step).wait_recv()
            relay_copy(step).start()

        @pl.when(hub & (step == borrowed))
        def _():
            @pl.loop(0, passed)
            def _(number):
                take_part(number).wait_recv()
                relay_part(number).start()

    fast_copy(kbuf, 0).wait_send()
    fast_copy(vbuf, 1).wait_send()

    @pl.when(~hub)
    def _():
        own_copy(1, across).wait_send()
        own_copy(2, fast_peer).wait_send()

    @pl.when(hub)
    def _():
        own_copy(0, slow_peer).wait_send()

        @pl.when(above)
        def _():
            @pl.loop(0, level + 1)
            def _(item):
                up_copy(item).wait_send()

        @pl.when(below)
        def _():
            @pl.loop(level, levels)
            def _(item):
                down_copy(item).wait_send()

        @pl.loop(0, levels)
        def _(item):
            @pl.loop(0, cuts)
            def _(owner):
                core_copy(owner, item).wait_send()

            @pl.when(after)
            def _():
                @pl.loop(0, cut + 1)
                def _(owner):
                    right_copy(owner, item).wait_send()

            @pl.when(before)
            def _():
                @pl.loop(cut, cuts)
                def _(owner):
                    left_copy(owner, item).wait_send()

    fast_copy(vbuf, 1).wait_recv()

    @pl.loop(0, chunks)
    def _(step):
        @pl.when(has_slow & (step == chunks - 1))
        def _():
            for start, length in key_pieces:
                slow_copy(kbuf, k_send, k_recv, start, length).wait_send()

        @pl.when(hub & (step == chunks - 1))
        def _():
            @pl.loop(0, borrowed)
            def _(item):
                relay_copy(item).wait_send()

            @pl.loop(0, passed)
            def _(number):
                relay_part(number).wait_send()

        for start, length in value_pieces:
            @pl.when(hub & has_slow & (step == start))
            def _():
                slow_copy(vbuf, v_send, v_recv, start, length).wait_recv()

        @pl.when(~hub & has_slow)
        def _():
            slow_copy(vbuf, v_send, v_recv, step).wait_recv()

        for inner in range(CHUNK_HEADS):
            head = step * CHUNK_HEADS + inner
            columns = pl.ds(pl.multiple_of(head * HEAD, HEAD), HEAD)
            for block in range(blocks):
                near_values = vbuf[pl.ds(block * BLOCK, span), columns]
                mixed = jnp.dot(
                    wbuf[head, block], near_values, preferred_element_type=jnp.float32
                ) + jnp.dot(
                    fwbuf[head, block], far_rows(1, block, head),
                    preferred_element_type=jnp.float32,
                )
                out_ref[block * BLOCK : (block + 1) * BLOCK, columns] = (
                    mixed * inv[head, block]
                ).astype(out_ref.dtype)

    @pl.when(~hub)
    def _():
        @pl.loop(0, borrowed)
        def _(step):
            relay_copy(step).wait_send()

    @pl.when(hub & has_slow)
    def _():
        for start, length in value_pieces:
            slow_copy(vbuf, v_send, v_recv, start, length).wait_send()

    @pl.when(~hub & has_slow & ~(ends_after | ends_before))
    def _():
        @pl.loop(0, lent)
        def _(step):
            slow_copy(vbuf, v_send, v_recv, step).wait_send()

        @pl.when(rest > 0)
        def _():
            @pl.loop(0, QUARTERS)
            def _(number):
                slow_part(number).wait_send()

        @pl.loop(lent + jnp.where(rest > 0, 1, 0), chunks)
        def _(step):
            slow_copy(vbuf, v_send, v_recv, step).wait_send()


def shards(cuts, group, queries, keys, values, window, summary_index):
    rows, width = queries.shape
    blocks = rows // BLOCK
    heads = width // HEAD
    listed = summary_index.shape[1]
    count = cuts * group
    levels = group // SEATS
    chunk = CHUNK_HEADS * HEAD
    chunks = width // chunk
    halo = REACH * BLOCK
    held = rows + 2 * halo
    span = (2 * REACH + 1) * BLOCK
    dma = pltpu.SemaphoreType.DMA
    return pl.pallas_call(
        functools.partial(kernel, cuts, group),
        out_shape=jax.ShapeDtypeStruct((rows, width), jnp.bfloat16),
        in_specs=[pl.BlockSpec(memory_space=pltpu.HBM)] * 5,
        out_specs=pl.BlockSpec(memory_space=pltpu.VMEM),
        scratch_shapes=[
            pltpu.VMEM((rows, width), jnp.bfloat16),
            pltpu.VMEM((held, width), jnp.bfloat16),
            pltpu.VMEM((held, width), jnp.bfloat16),
            pltpu.VMEM((chunks, halo, chunk), jnp.bfloat16),
            pltpu.SMEM(window.shape, jnp.int32),
            pltpu.SMEM(summary_index.shape, jnp.int32),
            pltpu.VMEM((2, blocks, heads, HEAD), jnp.bfloat16),
            pltpu.VMEM((count, 2, blocks, heads, HEAD), jnp.bfloat16),
            pltpu.VMEM((2, blocks, listed * heads, HEAD), jnp.float32),
            pltpu.VMEM((heads, blocks, BLOCK, span), jnp.bfloat16),
            pltpu.VMEM((heads, blocks, BLOCK, listed), jnp.bfloat16),
            pltpu.VMEM((heads, blocks, BLOCK, 1), jnp.float32),
            dma((5,)),
            *[dma((chunks,))] * 4,
            *[dma((2,))] * 2,
            *[dma((chunks,))] * 2,
            *[dma((QUARTERS,))] * 3,
            *[dma((3,))] * 2,
            *[dma((cuts, levels))] * 2,
            *[dma((levels,))] * 4,
            *[dma((cuts, levels))] * 4,
            *[pltpu.SemaphoreType.REGULAR] * 2,
        ],
        compiler_params=pltpu.CompilerParams(
            collective_id=0, has_side_effects=True, vmem_limit_bytes=48 * 1024 * 1024
        ),
    )(
        *(
            pltpu.with_memory_space_constraint(operand, pltpu.HBM)
            for operand in (queries, keys, values, window, summary_index)
        )
    )


def solution(mesh):
    return jax.shard_map(
        functools.partial(shards, mesh.shape["cuts"], mesh.shape["group"]),
        mesh=mesh,
        in_specs=(
            P(("cuts", "group"), None),
            P(("cuts", "group"), None),
            P(("cuts", "group"), None),
            P(("cuts", "group")),
            P(("cuts", "group"), None),
        ),
        out_specs=P(("cuts", "group"), None),
        check_vma=False,
    )
```

```python
import functools

import jax
import jax.numpy as jnp
from jax import lax
from jax.experimental import pallas as pl
from jax.experimental.pallas import tpu as pltpu
from jax.sharding import PartitionSpec as P

HEAD = 128
BLOCK = 128
REACH = 2
CHUNK_HEADS = 2
SEATS = 4
QUARTERS = 4
MESH = pl.DeviceIdType.MESH


def pieces_of(chunks, most):
    if most == 2:
        lengths = [1, chunks // 2 - 1, chunks - chunks // 2]
    else:
        rest = chunks - 2
        lengths = [rest - rest // 2, rest // 2, 1, 1]
    pieces, start = [], 0
    for length in lengths:
        if length:
            pieces.append((start, length))
            start += length
    return pieces


def kernel(
    cuts, group,
    q_hbm, k_hbm, v_hbm, window_hbm, index_hbm, out_ref,
    qbuf, kbuf, vbuf, relay, window_ref, index_ref, own, pool, far, wbuf, fwbuf, inv, early,
    local_sem, k_send, k_recv, v_send, v_recv, fast_send, fast_recv,
    relay_send, relay_recv, part_send, part_recv, pass_send, own_send, own_recv, core_send, core_recv,
    level_send, level_recv,
    right_send, right_recv, left_send, left_recv, go_sem, far_sem,
):
    count = cuts * group
    rows, width = q_hbm.shape
    blocks = rows // BLOCK
    heads = width // HEAD
    halo = REACH * BLOCK
    span = (2 * REACH + 1) * BLOCK
    chunk = CHUNK_HEADS * HEAD
    chunks = width // chunk
    listed = index_ref.shape[1]
    levels = group // SEATS
    top = levels - 1

    cut = lax.axis_index("cuts")
    spot = lax.axis_index("group")
    me = cut * group + spot
    seat = lax.rem(spot, SEATS)
    level = spot // SEATS
    odd = lax.rem(seat, 2) == 1
    hub = (seat == 1) | (seat == 2)
    below, above = level > 0, level < top
    before, after = cut > 0, cut < cuts - 1

    fast_peer = jnp.where(odd, me - 1, me + 1)
    slow_peer = jnp.where(odd, me + 1, me - 1)
    has_slow = (slow_peer >= 0) & (slow_peer < count)
    across = jnp.where(seat < 2, me + 2, me - 2)

    trim = jnp.where(cut == 0, jnp.maximum(2 - level, 0), 0)
    upward = jnp.maximum((top - level) * chunks * QUARTERS // levels - trim, 0)
    downward = level * chunks // levels * QUARTERS
    quarters = jnp.where(
        seat == 3,
        jnp.where(above, upward, chunks * QUARTERS),
        jnp.where(seat == 0, jnp.where(below, downward, chunks * QUARTERS), 0),
    )
    quarters = jnp.where(has_slow, quarters, 0)
    lent = quarters // QUARTERS
    rest = quarters - lent * QUARTERS
    lend_peer = jnp.where(
        seat == 3,
        jnp.where(above, me - 2, me + SEATS),
        jnp.where(below, me + 2, me - SEATS),
    )
    relay_up = (seat == 1) & above
    relay_down = (seat == 2) & below
    ends_after = (seat == 3) & (level == top) & after
    ends_before = (seat == 0) & (level == 0) & before
    relay_after = (seat == 3) & (level == 0) & before
    relay_before = (seat == 0) & (level == top) & after
    taken = jnp.where(
        relay_up,
        upward,
        jnp.where(
            relay_down,
            downward,
            jnp.where(relay_after | relay_before, chunks * QUARTERS, 0),
        ),
    )
    borrowed = taken // QUARTERS
    passed = taken - borrowed * QUARTERS
    relay_peer = jnp.where(
        relay_up | relay_before, me + (SEATS - 1), me - (SEATS - 1)
    )

    def place(device):
        return (device // group, lax.rem(device, group))

    barrier = pltpu.get_barrier_semaphore()

    def greet(device, present=None):
        def signal():
            pl.semaphore_signal(
                barrier, inc=1, device_id=place(device), device_id_type=MESH
            )

        if present is None:
            signal()
        else:
            pl.when(present)(signal)

    greet(slow_peer, has_slow)
    greet(fast_peer)
    greet(across, hub)
    @pl.when(hub)
    def _():
        @pl.loop(1, levels)
        def _(hop):
            greet(cut * group + lax.rem(fast_peer - cut * group + hop * SEATS, group))

    greet(fast_peer - group, hub & before)
    greet(fast_peer + group, hub & after)
    greet(me - SEATS, relay_after)
    greet(me + SEATS, relay_before)
    greet(me - SEATS, (seat == 0) & below)
    greet(me + SEATS, (seat == 3) & above)
    greet(me - (SEATS - 1), ends_after)
    greet(me + (SEATS - 1), ends_before)
    expected = 1 + jnp.where(hub, 0, levels - 1)
    for present in (
        has_slow, ~hub, ~hub & before, ~hub & after,
        (seat == 0) & above, (seat == 3) & below,
        relay_after, relay_before, ends_after, ends_before,
    ):
        expected = expected + jnp.where(present, 1, 0)

    loads = [
        pltpu.make_async_copy(k_hbm, kbuf.at[pl.ds(halo, rows)], local_sem.at[0]),
        pltpu.make_async_copy(v_hbm, vbuf.at[pl.ds(halo, rows)], local_sem.at[1]),
        pltpu.make_async_copy(q_hbm, qbuf, local_sem.at[2]),
        pltpu.make_async_copy(window_hbm, window_ref, local_sem.at[3]),
        pltpu.make_async_copy(index_hbm, index_ref, local_sem.at[4]),
    ]
    for load in loads:
        load.start()

    def remote(source, target, send, recv, device):
        return pltpu.make_async_remote_copy(
            src_ref=source, dst_ref=target, send_sem=send, recv_sem=recv,
            device_id=place(device), device_id_type=MESH,
        )

    def columns_of(step):
        return pl.ds(pl.multiple_of(step * chunk, chunk), chunk)

    key_pieces = pieces_of(chunks, 2)
    value_pieces = pieces_of(chunks, 4)
    edge = halo + rows
    slow_from = pl.ds(pl.multiple_of(jnp.where(odd, rows, halo), BLOCK), halo)
    first_from = pl.ds(pl.multiple_of(jnp.where(odd, rows - halo, 0), BLOCK), halo)
    slow_to = pl.ds(pl.multiple_of(jnp.where(odd, 0, edge), BLOCK), halo)
    fast_from = pl.ds(pl.multiple_of(jnp.where(odd, halo, rows), BLOCK), halo)
    fast_to = pl.ds(pl.multiple_of(jnp.where(odd, edge, 0), BLOCK), halo)
    relay_to = pl.ds(
        pl.multiple_of(jnp.where(relay_up | relay_after, 0, edge), BLOCK), halo
    )

    def slow_copy(buffer, send, recv, step, length=1):
        columns = pl.ds(pl.multiple_of(step * chunk, chunk), length * chunk)
        return remote(
            buffer.at[slow_from, columns], buffer.at[slow_to, columns],
            send.at[step], recv.at[step], slow_peer,
        )

    piece = halo // QUARTERS

    def rows_of(start, number):
        return pl.ds(pl.multiple_of(start + number * piece, piece), piece)

    def slow_part(number):
        return remote(
            vbuf.at[rows_of(jnp.where(odd, rows, halo), number), columns_of(lent)],
            vbuf.at[rows_of(jnp.where(odd, 0, edge), number), columns_of(lent)],
            part_send.at[number], v_recv.at[lent], slow_peer,
        )

    def lend_part(number):
        return remote(
            vbuf.at[rows_of(jnp.where(odd, rows, halo), number), columns_of(lent)],
            relay.at[lent, rows_of(0, number)],
            part_send.at[number], part_recv.at[number], lend_peer,
        )

    def relay_part(number):
        return remote(
            relay.at[borrowed, rows_of(0, number)],
            vbuf.at[
                rows_of(jnp.where(relay_up | relay_after, 0, edge), number),
                columns_of(borrowed),
            ],
            pass_send.at[number], v_recv.at[borrowed], relay_peer,
        )

    def take_part(number):
        return remote(
            vbuf.at[rows_of(halo, number), columns_of(borrowed)],
            relay.at[borrowed, rows_of(0, number)],
            part_send.at[number], part_recv.at[number], lend_peer,
        )

    def fast_copy(buffer, part):
        return remote(
            buffer.at[fast_from], buffer.at[fast_to],
            fast_send.at[part], fast_recv.at[part], fast_peer,
        )

    def lend_copy(step):
        return remote(
            vbuf.at[slow_from, columns_of(step)], relay.at[step],
            v_send.at[step], relay_recv.at[step], lend_peer,
        )

    def relay_copy(step):
        return remote(
            relay.at[step], vbuf.at[relay_to, columns_of(step)],
            relay_send.at[step], v_recv.at[step], relay_peer,
        )

    def own_copy(place_of, device):
        return remote(
            own, pool.at[me], own_send.at[place_of], own_recv.at[place_of], device
        )

    def quad_copy(owner, item, send, recv, device):
        held = pool.at[pl.ds(owner * group + item * SEATS, SEATS)]
        return remote(held, held, send, recv, device)

    def level_copy(hop):
        return quad_copy(
            cut, level, level_send.at[hop], level_recv.at[hop],
            cut * group + lax.rem(spot + hop * SEATS, group),
        )

    def right_copy(owner, item):
        return quad_copy(
            owner, item, right_send.at[owner, item], right_recv.at[owner, item], me + group
        )

    def left_copy(owner, item):
        return quad_copy(
            owner, item, left_send.at[owner, item], left_recv.at[owner, item], me - group
        )

    def core_copy(owner, item):
        return quad_copy(
            owner, item, core_send.at[owner, item], core_recv.at[owner, item], fast_peer
        )

    def first_copy():
        length = key_pieces[0][1] * chunk
        return remote(
            k_hbm.at[first_from, pl.ds(0, length)], kbuf.at[slow_to, pl.ds(0, length)],
            k_send.at[0], k_recv.at[0], slow_peer,
        )

    @pl.when(hub)
    def _():
        pl.semaphore_wait(barrier, expected)

        @pl.when(has_slow)
        def _():
            first_copy().start()

    ones = jnp.ones((heads, BLOCK), jnp.bfloat16)
    row = lax.broadcasted_iota(jnp.int32, (heads, HEAD), 0)
    for part, (buffer, divisor) in enumerate(
        ((kbuf, jnp.sqrt(jnp.float32(BLOCK))), (vbuf, jnp.float32(BLOCK)))
    ):
        loads[part].wait()
        for block in range(blocks):
            pooled = jnp.zeros((heads, HEAD), jnp.float32)
            sums = jnp.dot(
                ones,
                buffer[halo + block * BLOCK : halo + (block + 1) * BLOCK, :],
                preferred_element_type=jnp.float32,
            )
            for head in range(heads):
                pooled = jnp.where(
                    row == head, sums[:, head * HEAD : (head + 1) * HEAD], pooled
                )
            own[part, block] = (pooled / divisor).astype(jnp.bfloat16)
    @pl.when(~hub)
    def _():
        pl.semaphore_wait(barrier, expected)

    @pl.when(hub)
    def _():
        own_copy(0, slow_peer).start()

    @pl.when(~hub)
    def _():
        own_copy(1, across).start()
        own_copy(2, fast_peer).start()
        pl.semaphore_signal(
            far_sem, inc=1, device_id=place(fast_peer), device_id_type=MESH
        )

    def send_slow(whole):
        @pl.when(has_slow)
        def _():
            for start, length in key_pieces[1 if whole else 0 :]:
                slow_copy(kbuf, k_send, k_recv, start, length).start()

            if whole:
                for start, length in value_pieces:
                    slow_copy(vbuf, v_send, v_recv, start, length).start()
            else:
                @pl.when(rest > 0)
                def _():
                    @pl.loop(rest, QUARTERS)
                    def _(number):
                        slow_part(number).start()

                @pl.loop(lent + jnp.where(rest > 0, 1, 0), chunks)
                def _(step):
                    slow_copy(vbuf, v_send, v_recv, step).start()

    @pl.loop(0, lent)
    def _(step):
        lend_copy(step).start()

    @pl.loop(0, rest)
    def _(number):
        lend_part(number).start()

    pl.when(hub)(lambda: send_slow(True))
    fast_copy(kbuf, 0).start()
    fast_copy(vbuf, 1).start()

    @pl.when(me == 0)
    def _():
        kbuf[pl.ds(0, halo), :] = jnp.zeros((halo, width), kbuf.dtype)
        vbuf[pl.ds(0, halo), :] = jnp.zeros((halo, width), vbuf.dtype)

    @pl.when(me == count - 1)
    def _():
        kbuf[pl.ds(edge, halo), :] = jnp.zeros((halo, width), kbuf.dtype)
        vbuf[pl.ds(edge, halo), :] = jnp.zeros((halo, width), vbuf.dtype)

    def spread(item):
        @pl.when(after)
        def _():
            right_copy(cut, item).start()

        @pl.when(before)
        def _():
            left_copy(cut, item).start()

        core_copy(cut, item).start()

    @pl.when(hub)
    def _():
        pool[me] = own[...]
        own_copy(0, slow_peer).wait_recv()
        own_copy(1, across).wait_recv()
        own_copy(2, fast_peer).wait_recv()
        pl.semaphore_wait(far_sem, 1)

        @pl.loop(1, levels)
        def _(hop):
            level_copy(hop).start()

        @pl.when(relay_up | relay_down)
        def _():
            pl.semaphore_signal(
                go_sem, inc=1, device_id=place(relay_peer), device_id_type=MESH
            )

        spread(level)

        @pl.loop(1, levels)
        def _(hop):
            level_copy(hop).wait_recv()
            spread(lax.rem(level + levels - hop, levels))

        @pl.loop(1, cuts)
        def _(hop):
            @pl.loop(0, levels)
            def _(item):
                @pl.when(cut >= hop)
                def _():
                    right_copy(cut - hop, item).wait_recv()

                    @pl.when(after)
                    def _():
                        right_copy(cut - hop, item).start()

                    core_copy(cut - hop, item).start()

                @pl.when(cut + hop < cuts)
                def _():
                    left_copy(cut + hop, item).wait_recv()

                    @pl.when(before)
                    def _():
                        left_copy(cut + hop, item).start()

                    core_copy(cut + hop, item).start()

    @pl.when(~hub)
    def _():
        @pl.when(((seat == 3) & above) | ((seat == 0) & below))
        def _():
            pl.semaphore_wait(go_sem, 1)

        @pl.when(ends_after | ends_before)
        def _():
            @pl.loop(0, chunks * 3 // 4)
            def _(step):
                lend_copy(step).wait_send()

        send_slow(False)

        @pl.loop(0, borrowed)
        def _(step):
            lend_copy(step).wait_recv()
            relay_copy(step).start()

        @pl.loop(0, cuts)
        def _(owner):
            @pl.loop(0, levels)
            def _(item):
                core_copy(owner, item).wait_recv()

    for load in loads[2:]:
        load.wait()

    for part in range(2):
        for block in range(blocks):
            for entry in range(listed):
                name = index_ref[block, entry]
                tile = pool[name // blocks, part, lax.rem(name, blocks)]
                far[part, block, pl.ds(entry * heads, heads), :] = tile.astype(jnp.float32)

    scale = 1.0 / jnp.sqrt(jnp.float32(HEAD))
    contract = (((1,), (1,)), ((), ()))
    total_blocks = count * blocks

    def far_rows(part, block, head):
        return far[part, block, pl.ds(head, listed, stride=heads), :].astype(jnp.bfloat16)

    fast_copy(kbuf, 0).wait_recv()

    @pl.loop(0, chunks)
    def _(step):
        for start, length in key_pieces:
            @pl.when(has_slow & (step == start))
            def _():
                slow_copy(kbuf, k_send, k_recv, start, length).wait_recv()

        for inner in range(CHUNK_HEADS):
            head = step * CHUNK_HEADS + inner
            columns = pl.ds(pl.multiple_of(head * HEAD, HEAD), HEAD)
            for block in range(blocks):
                query = qbuf[block * BLOCK : (block + 1) * BLOCK, columns]
                near_keys = kbuf[pl.ds(block * BLOCK, span), columns]
                scores = lax.dot_general(
                    query, near_keys, contract, preferred_element_type=jnp.float32
                )
                far_scores = lax.dot_general(
                    query, far_rows(0, block, head), contract,
                    preferred_element_type=jnp.float32,
                )
                own = me * blocks + block
                pieces = []
                for place_of in range(2 * REACH + 1):
                    offset = place_of - REACH
                    piece = scores[:, place_of * BLOCK : (place_of + 1) * BLOCK]
                    if offset:
                        other = own + offset
                        allowed = (
                            (window_ref[block] >= abs(offset))
                            & (other >= 0)
                            & (other < total_blocks)
                        )
                        piece = jnp.where(allowed, piece, -1e30)
                    pieces.append(piece)
                tallest = functools.reduce(jnp.maximum, pieces)
                top = jnp.maximum(
                    jnp.max(tallest, axis=1, keepdims=True),
                    jnp.max(far_scores, axis=1, keepdims=True),
                )
                weights = [jnp.exp((piece - top) * scale) for piece in pieces]
                far_weights = jnp.exp((far_scores - top) * scale)
                total = jnp.sum(
                    functools.reduce(jnp.add, weights), axis=1, keepdims=True
                ) + jnp.sum(far_weights, axis=1, keepdims=True)
                for place_of, weight in enumerate(weights):
                    wbuf[head, block, :, place_of * BLOCK : (place_of + 1) * BLOCK] = (
                        weight.astype(jnp.bfloat16)
                    )
                fwbuf[head, block] = far_weights.astype(jnp.bfloat16)
                inv[head, block] = 1.0 / total

        @pl.when(hub & (step < borrowed))
        def _():
            lend_copy(step).wait_recv()
            relay_copy(step).start()

        @pl.when(hub & (step == borrowed))
        def _():
            @pl.loop(0, passed)
            def _(number):
                take_part(number).wait_recv()
                relay_part(number).start()

    fast_copy(kbuf, 0).wait_send()
    fast_copy(vbuf, 1).wait_send()

    @pl.when(~hub)
    def _():
        own_copy(1, across).wait_send()
        own_copy(2, fast_peer).wait_send()

    @pl.when(hub)
    def _():
        own_copy(0, slow_peer).wait_send()

        @pl.loop(1, levels)
        def _(hop):
            level_copy(hop).wait_send()

        @pl.loop(0, levels)
        def _(item):
            @pl.loop(0, cuts)
            def _(owner):
                core_copy(owner, item).wait_send()

            @pl.when(after)
            def _():
                @pl.loop(0, cut + 1)
                def _(owner):
                    right_copy(owner, item).wait_send()

            @pl.when(before)
            def _():
                @pl.loop(cut, cuts)
                def _(owner):
                    left_copy(owner, item).wait_send()

    fast_copy(vbuf, 1).wait_recv()

    def arrive(step):
        for start, length in value_pieces:
            @pl.when(hub & has_slow & (step == start))
            def _():
                slow_copy(vbuf, v_send, v_recv, start, length).wait_recv()

        @pl.when(~hub & has_slow)
        def _():
            slow_copy(vbuf, v_send, v_recv, step).wait_recv()

    def far_mixed(block, head):
        return jnp.dot(
            fwbuf[head, block], far_rows(1, block, head),
            preferred_element_type=jnp.float32,
        )

    @pl.loop(0, chunks - 1)
    def _(step):
        arrive(step)
        for inner in range(CHUNK_HEADS):
            head = step * CHUNK_HEADS + inner
            columns = pl.ds(pl.multiple_of(head * HEAD, HEAD), HEAD)
            for block in range(blocks):
                near_values = vbuf[pl.ds(block * BLOCK, span), columns]
                mixed = jnp.dot(
                    wbuf[head, block], near_values, preferred_element_type=jnp.float32
                ) + far_mixed(block, head)
                out_ref[block * BLOCK : (block + 1) * BLOCK, columns] = (
                    mixed * inv[head, block]
                ).astype(out_ref.dtype)

    final = [
        (chunks * CHUNK_HEADS - CHUNK_HEADS + inner, block)
        for inner in range(CHUNK_HEADS)
        for block in range(blocks)
    ]

    def final_dot(head, block, first, stop):
        first, stop = max(first, block * BLOCK), min(stop, block * BLOCK + span)
        return jnp.dot(
            wbuf[head, block, :, first - block * BLOCK : stop - block * BLOCK],
            vbuf[first:stop, head * HEAD : (head + 1) * HEAD],
            preferred_element_type=jnp.float32,
        )

    def final_near(first, stop):
        for n, (head, block) in enumerate(final):
            early[n] = final_dot(head, block, first, stop) + far_mixed(block, head)

    def final_slow(first, stop):
        for n, (head, block) in enumerate(final):
            mixed = early[n] + final_dot(head, block, first, stop)
            out_ref[
                block * BLOCK : (block + 1) * BLOCK, head * HEAD : (head + 1) * HEAD
            ] = (mixed * inv[head, block]).astype(out_ref.dtype)

    pl.when(odd)(lambda: final_near(0, edge))
    pl.when(~odd)(lambda: final_near(halo, edge + halo))

    @pl.when(has_slow)
    def _():
        for start, length in key_pieces:
            slow_copy(kbuf, k_send, k_recv, start, length).wait_send()

    @pl.when(hub)
    def _():
        @pl.loop(0, borrowed)
        def _(item):
            relay_copy(item).wait_send()

        @pl.loop(0, passed)
        def _(number):
            relay_part(number).wait_send()

    @pl.when(hub & has_slow)
    def _():
        for start, length in value_pieces[:-1]:
            slow_copy(vbuf, v_send, v_recv, start, length).wait_send()

    arrive(chunks - 1)
    pl.when(odd)(lambda: final_slow(edge, edge + halo))
    pl.when(~odd)(lambda: final_slow(0, halo))

    @pl.when(~hub)
    def _():
        @pl.loop(0, borrowed)
        def _(step):
            relay_copy(step).wait_send()

    @pl.when(hub & has_slow)
    def _():
        start, length = value_pieces[-1]
        slow_copy(vbuf, v_send, v_recv, start, length).wait_send()

    @pl.when(ends_after | ends_before)
    def _():
        @pl.loop(chunks * 3 // 4, chunks)
        def _(step):
            lend_copy(step).wait_send()

    @pl.when(~hub & has_slow & ~(ends_after | ends_before))
    def _():
        @pl.loop(0, lent)
        def _(step):
            slow_copy(vbuf, v_send, v_recv, step).wait_send()

        @pl.when(rest > 0)
        def _():
            @pl.loop(0, QUARTERS)
            def _(number):
                slow_part(number).wait_send()

        @pl.loop(lent + jnp.where(rest > 0, 1, 0), chunks)
        def _(step):
            slow_copy(vbuf, v_send, v_recv, step).wait_send()


def shards(cuts, group, queries, keys, values, window, summary_index):
    rows, width = queries.shape
    blocks = rows // BLOCK
    heads = width // HEAD
    listed = summary_index.shape[1]
    count = cuts * group
    levels = group // SEATS
    chunk = CHUNK_HEADS * HEAD
    chunks = width // chunk
    halo = REACH * BLOCK
    held = rows + 2 * halo
    span = (2 * REACH + 1) * BLOCK
    dma = pltpu.SemaphoreType.DMA
    return pl.pallas_call(
        functools.partial(kernel, cuts, group),
        out_shape=jax.ShapeDtypeStruct((rows, width), jnp.bfloat16),
        in_specs=[pl.BlockSpec(memory_space=pltpu.HBM)] * 5,
        out_specs=pl.BlockSpec(memory_space=pltpu.VMEM),
        scratch_shapes=[
            pltpu.VMEM((rows, width), jnp.bfloat16),
            pltpu.VMEM((held, width), jnp.bfloat16),
            pltpu.VMEM((held, width), jnp.bfloat16),
            pltpu.VMEM((chunks, halo, chunk), jnp.bfloat16),
            pltpu.SMEM(window.shape, jnp.int32),
            pltpu.SMEM(summary_index.shape, jnp.int32),
            pltpu.VMEM((2, blocks, heads, HEAD), jnp.bfloat16),
            pltpu.VMEM((count, 2, blocks, heads, HEAD), jnp.bfloat16),
            pltpu.VMEM((2, blocks, listed * heads, HEAD), jnp.float32),
            pltpu.VMEM((heads, blocks, BLOCK, span), jnp.bfloat16),
            pltpu.VMEM((heads, blocks, BLOCK, listed), jnp.bfloat16),
            pltpu.VMEM((heads, blocks, BLOCK, 1), jnp.float32),
            pltpu.VMEM((CHUNK_HEADS * blocks, BLOCK, HEAD), jnp.float32),
            dma((5,)),
            *[dma((chunks,))] * 4,
            *[dma((2,))] * 2,
            *[dma((chunks,))] * 2,
            *[dma((QUARTERS,))] * 3,
            *[dma((3,))] * 2,
            *[dma((cuts, levels))] * 2,
            *[dma((levels,))] * 2,
            *[dma((cuts, levels))] * 4,
            *[pltpu.SemaphoreType.REGULAR] * 2,
        ],
        compiler_params=pltpu.CompilerParams(
            collective_id=0, has_side_effects=True, vmem_limit_bytes=48 * 1024 * 1024
        ),
    )(
        *(
            pltpu.with_memory_space_constraint(operand, pltpu.HBM)
            for operand in (queries, keys, values, window, summary_index)
        )
    )


def solution(mesh):
    return jax.shard_map(
        functools.partial(shards, mesh.shape["cuts"], mesh.shape["group"]),
        mesh=mesh,
        in_specs=(
            P(("cuts", "group"), None),
            P(("cuts", "group"), None),
            P(("cuts", "group"), None),
            P(("cuts", "group")),
            P(("cuts", "group"), None),
        ),
        out_specs=P(("cuts", "group"), None),
        check_vma=False,
    )
```

```python
import functools

import jax
import jax.numpy as jnp
from jax import lax
from jax.experimental import pallas as pl
from jax.experimental.pallas import tpu as pltpu
from jax.sharding import PartitionSpec as P

HEAD = 128
BLOCK = 128
REACH = 2
CHUNK_HEADS = 2
SEATS = 4
QUARTERS = 4
MESH = pl.DeviceIdType.MESH


def pieces_of(chunks, most):
    if most == 2:
        tail = chunks - chunks // 2
        lengths = [1, chunks // 2 - 1, tail // 2, tail // 4, tail - tail // 2 - tail // 4]
    else:
        rest = chunks - 2
        lengths = [rest - rest // 2, rest // 2, 1, 1]
    pieces, start = [], 0
    for length in lengths:
        if length:
            pieces.append((start, length))
            start += length
    return pieces


def kernel(
    cuts, group,
    q_hbm, k_hbm, v_hbm, window_hbm, index_hbm, out_ref,
    qbuf, kbuf, vbuf, relay, window_ref, index_ref, own, pool, far, wbuf, fwbuf, inv, early,
    local_sem, k_send, k_recv, v_send, v_recv, fast_send, fast_recv,
    relay_send, relay_recv, part_send, part_recv, pass_send, own_send, own_recv, core_send, core_recv,
    level_send, level_recv,
    right_send, right_recv, left_send, left_recv, go_sem, far_sem,
):
    count = cuts * group
    rows, width = q_hbm.shape
    blocks = rows // BLOCK
    heads = width // HEAD
    halo = REACH * BLOCK
    span = (2 * REACH + 1) * BLOCK
    chunk = CHUNK_HEADS * HEAD
    chunks = width // chunk
    listed = index_ref.shape[1]
    levels = group // SEATS
    top = levels - 1

    cut = lax.axis_index("cuts")
    spot = lax.axis_index("group")
    me = cut * group + spot
    seat = lax.rem(spot, SEATS)
    level = spot // SEATS
    odd = lax.rem(seat, 2) == 1
    hub = (seat == 1) | (seat == 2)
    below, above = level > 0, level < top
    before, after = cut > 0, cut < cuts - 1

    fast_peer = jnp.where(odd, me - 1, me + 1)
    slow_peer = jnp.where(odd, me + 1, me - 1)
    has_slow = (slow_peer >= 0) & (slow_peer < count)
    across = jnp.where(seat < 2, me + 2, me - 2)

    trim = jnp.where(cut == 0, jnp.maximum(2 - level, 0), 0)
    upward = jnp.maximum((top - level) * chunks * QUARTERS // levels - trim, 0)
    downward = level * chunks // levels * QUARTERS
    quarters = jnp.where(
        seat == 3,
        jnp.where(above, upward, chunks * QUARTERS),
        jnp.where(seat == 0, jnp.where(below, downward, chunks * QUARTERS), 0),
    )
    quarters = jnp.where(has_slow, quarters, 0)
    lent = quarters // QUARTERS
    rest = quarters - lent * QUARTERS
    lend_peer = jnp.where(
        seat == 3,
        jnp.where(above, me - 2, me + SEATS),
        jnp.where(below, me + 2, me - SEATS),
    )
    relay_up = (seat == 1) & above
    relay_down = (seat == 2) & below
    ends_after = (seat == 3) & (level == top) & after
    ends_before = (seat == 0) & (level == 0) & before
    relay_after = (seat == 3) & (level == 0) & before
    relay_before = (seat == 0) & (level == top) & after
    taken = jnp.where(
        relay_up,
        upward,
        jnp.where(
            relay_down,
            downward,
            jnp.where(relay_after | relay_before, chunks * QUARTERS, 0),
        ),
    )
    borrowed = taken // QUARTERS
    passed = taken - borrowed * QUARTERS
    relay_peer = jnp.where(
        relay_up | relay_before, me + (SEATS - 1), me - (SEATS - 1)
    )

    def place(device):
        return (device // group, lax.rem(device, group))

    barrier = pltpu.get_barrier_semaphore()

    def greet(device, present=None):
        def signal():
            pl.semaphore_signal(
                barrier, inc=1, device_id=place(device), device_id_type=MESH
            )

        if present is None:
            signal()
        else:
            pl.when(present)(signal)

    greet(slow_peer, has_slow)
    greet(fast_peer)
    greet(across, hub)
    @pl.when(hub)
    def _():
        @pl.loop(1, levels)
        def _(hop):
            greet(cut * group + lax.rem(fast_peer - cut * group + hop * SEATS, group))

    greet(fast_peer - group, hub & before)
    greet(fast_peer + group, hub & after)
    greet(me - SEATS, relay_after)
    greet(me + SEATS, relay_before)
    greet(me - SEATS, (seat == 0) & below)
    greet(me + SEATS, (seat == 3) & above)
    greet(me - (SEATS - 1), ends_after)
    greet(me + (SEATS - 1), ends_before)
    expected = 1 + jnp.where(hub, 0, levels - 1)
    for present in (
        has_slow, ~hub, ~hub & before, ~hub & after,
        (seat == 0) & above, (seat == 3) & below,
        relay_after, relay_before, ends_after, ends_before,
    ):
        expected = expected + jnp.where(present, 1, 0)

    loads = [
        pltpu.make_async_copy(k_hbm, kbuf.at[pl.ds(halo, rows)], local_sem.at[0]),
        pltpu.make_async_copy(v_hbm, vbuf.at[pl.ds(halo, rows)], local_sem.at[1]),
        pltpu.make_async_copy(q_hbm, qbuf, local_sem.at[2]),
        pltpu.make_async_copy(window_hbm, window_ref, local_sem.at[3]),
        pltpu.make_async_copy(index_hbm, index_ref, local_sem.at[4]),
    ]
    for load in loads:
        load.start()

    def remote(source, target, send, recv, device):
        return pltpu.make_async_remote_copy(
            src_ref=source, dst_ref=target, send_sem=send, recv_sem=recv,
            device_id=place(device), device_id_type=MESH,
        )

    def columns_of(step):
        return pl.ds(pl.multiple_of(step * chunk, chunk), chunk)

    key_pieces = pieces_of(chunks, 2)
    value_pieces = pieces_of(chunks, 4)
    edge = halo + rows
    slow_from = pl.ds(pl.multiple_of(jnp.where(odd, rows, halo), BLOCK), halo)
    first_from = pl.ds(pl.multiple_of(jnp.where(odd, rows - halo, 0), BLOCK), halo)
    slow_to = pl.ds(pl.multiple_of(jnp.where(odd, 0, edge), BLOCK), halo)
    fast_from = pl.ds(pl.multiple_of(jnp.where(odd, halo, rows), BLOCK), halo)
    fast_to = pl.ds(pl.multiple_of(jnp.where(odd, edge, 0), BLOCK), halo)
    relay_to = pl.ds(
        pl.multiple_of(jnp.where(relay_up | relay_after, 0, edge), BLOCK), halo
    )

    def slow_copy(buffer, send, recv, step, length=1):
        columns = pl.ds(pl.multiple_of(step * chunk, chunk), length * chunk)
        return remote(
            buffer.at[slow_from, columns], buffer.at[slow_to, columns],
            send.at[step], recv.at[step], slow_peer,
        )

    piece = halo // QUARTERS

    def rows_of(start, number):
        return pl.ds(pl.multiple_of(start + number * piece, piece), piece)

    def slow_part(number):
        return remote(
            vbuf.at[rows_of(jnp.where(odd, rows, halo), number), columns_of(lent)],
            vbuf.at[rows_of(jnp.where(odd, 0, edge), number), columns_of(lent)],
            part_send.at[number], v_recv.at[lent], slow_peer,
        )

    def lend_part(number):
        return remote(
            vbuf.at[rows_of(jnp.where(odd, rows, halo), number), columns_of(lent)],
            relay.at[lent, rows_of(0, number)],
            part_send.at[number], part_recv.at[number], lend_peer,
        )

    def relay_part(number):
        return remote(
            relay.at[borrowed, rows_of(0, number)],
            vbuf.at[
                rows_of(jnp.where(relay_up | relay_after, 0, edge), number),
                columns_of(borrowed),
            ],
            pass_send.at[number], v_recv.at[borrowed], relay_peer,
        )

    def take_part(number):
        return remote(
            vbuf.at[rows_of(halo, number), columns_of(borrowed)],
            relay.at[borrowed, rows_of(0, number)],
            part_send.at[number], part_recv.at[number], lend_peer,
        )

    def fast_copy(buffer, part):
        return remote(
            buffer.at[fast_from], buffer.at[fast_to],
            fast_send.at[part], fast_recv.at[part], fast_peer,
        )

    def lend_copy(step):
        return remote(
            vbuf.at[slow_from, columns_of(step)], relay.at[step],
            v_send.at[step], relay_recv.at[step], lend_peer,
        )

    def relay_copy(step):
        return remote(
            relay.at[step], vbuf.at[relay_to, columns_of(step)],
            relay_send.at[step], v_recv.at[step], relay_peer,
        )

    def own_copy(place_of, device):
        return remote(
            own, pool.at[me], own_send.at[place_of], own_recv.at[place_of], device
        )

    def quad_copy(owner, item, send, recv, device):
        held = pool.at[pl.ds(owner * group + item * SEATS, SEATS)]
        return remote(held, held, send, recv, device)

    def level_copy(hop):
        return quad_copy(
            cut, level, level_send.at[hop], level_recv.at[hop],
            cut * group + lax.rem(spot + hop * SEATS, group),
        )

    def right_copy(owner, item):
        return quad_copy(
            owner, item, right_send.at[owner, item], right_recv.at[owner, item], me + group
        )

    def left_copy(owner, item):
        return quad_copy(
            owner, item, left_send.at[owner, item], left_recv.at[owner, item], me - group
        )

    def core_copy(owner, item):
        return quad_copy(
            owner, item, core_send.at[owner, item], core_recv.at[owner, item], fast_peer
        )

    def first_copy():
        length = key_pieces[0][1] * chunk
        return remote(
            k_hbm.at[first_from, pl.ds(0, length)], kbuf.at[slow_to, pl.ds(0, length)],
            k_send.at[0], k_recv.at[0], slow_peer,
        )

    @pl.when(hub)
    def _():
        pl.semaphore_wait(barrier, expected)

        @pl.when(has_slow)
        def _():
            first_copy().start()

    ones = jnp.ones((heads, BLOCK), jnp.bfloat16)
    row = lax.broadcasted_iota(jnp.int32, (heads, HEAD), 0)
    for part, (buffer, divisor) in enumerate(
        ((kbuf, jnp.sqrt(jnp.float32(BLOCK))), (vbuf, jnp.float32(BLOCK)))
    ):
        loads[part].wait()
        for block in range(blocks):
            pooled = jnp.zeros((heads, HEAD), jnp.float32)
            sums = jnp.dot(
                ones,
                buffer[halo + block * BLOCK : halo + (block + 1) * BLOCK, :],
                preferred_element_type=jnp.float32,
            )
            for head in range(heads):
                pooled = jnp.where(
                    row == head, sums[:, head * HEAD : (head + 1) * HEAD], pooled
                )
            own[part, block] = (pooled / divisor).astype(jnp.bfloat16)
    @pl.when(~hub)
    def _():
        pl.semaphore_wait(barrier, expected)

    @pl.when(hub)
    def _():
        own_copy(0, slow_peer).start()

    @pl.when(~hub)
    def _():
        own_copy(1, across).start()
        own_copy(2, fast_peer).start()
        pl.semaphore_signal(
            far_sem, inc=1, device_id=place(fast_peer), device_id_type=MESH
        )

    def send_slow(whole):
        @pl.when(has_slow)
        def _():
            for start, length in key_pieces[1 if whole else 0 :]:
                slow_copy(kbuf, k_send, k_recv, start, length).start()

            if whole:
                for start, length in value_pieces:
                    slow_copy(vbuf, v_send, v_recv, start, length).start()
            else:
                @pl.when(rest > 0)
                def _():
                    @pl.loop(rest, QUARTERS)
                    def _(number):
                        slow_part(number).start()

                @pl.loop(lent + jnp.where(rest > 0, 1, 0), chunks)
                def _(step):
                    slow_copy(vbuf, v_send, v_recv, step).start()

    @pl.loop(0, lent)
    def _(step):
        lend_copy(step).start()

    @pl.loop(0, rest)
    def _(number):
        lend_part(number).start()

    pl.when(hub)(lambda: send_slow(True))
    fast_copy(kbuf, 0).start()
    fast_copy(vbuf, 1).start()

    @pl.when(me == 0)
    def _():
        kbuf[pl.ds(0, halo), :] = jnp.zeros((halo, width), kbuf.dtype)
        vbuf[pl.ds(0, halo), :] = jnp.zeros((halo, width), vbuf.dtype)

    @pl.when(me == count - 1)
    def _():
        kbuf[pl.ds(edge, halo), :] = jnp.zeros((halo, width), kbuf.dtype)
        vbuf[pl.ds(edge, halo), :] = jnp.zeros((halo, width), vbuf.dtype)

    def spread(item):
        @pl.when(after)
        def _():
            right_copy(cut, item).start()

        @pl.when(before)
        def _():
            left_copy(cut, item).start()

        core_copy(cut, item).start()

    @pl.when(hub)
    def _():
        pool[me] = own[...]
        own_copy(0, slow_peer).wait_recv()
        own_copy(1, across).wait_recv()
        own_copy(2, fast_peer).wait_recv()
        pl.semaphore_wait(far_sem, 1)

        @pl.loop(1, levels)
        def _(hop):
            level_copy(hop).start()

        @pl.when(relay_up | relay_down)
        def _():
            pl.semaphore_signal(
                go_sem, inc=1, device_id=place(relay_peer), device_id_type=MESH
            )

        spread(level)

        @pl.loop(1, levels)
        def _(hop):
            level_copy(hop).wait_recv()
            spread(lax.rem(level + levels - hop, levels))

        @pl.loop(1, cuts)
        def _(hop):
            @pl.loop(0, levels)
            def _(item):
                @pl.when(cut >= hop)
                def _():
                    right_copy(cut - hop, item).wait_recv()

                    @pl.when(after)
                    def _():
                        right_copy(cut - hop, item).start()

                    core_copy(cut - hop, item).start()

                @pl.when(cut + hop < cuts)
                def _():
                    left_copy(cut + hop, item).wait_recv()

                    @pl.when(before)
                    def _():
                        left_copy(cut + hop, item).start()

                    core_copy(cut + hop, item).start()

    @pl.when(~hub)
    def _():
        @pl.when(((seat == 3) & above) | ((seat == 0) & below))
        def _():
            pl.semaphore_wait(go_sem, 1)

        @pl.when(ends_after | ends_before)
        def _():
            @pl.loop(0, chunks // 2)
            def _(step):
                lend_copy(step).wait_send()

        send_slow(False)

        @pl.loop(0, borrowed)
        def _(step):
            lend_copy(step).wait_recv()
            relay_copy(step).start()

        @pl.loop(0, cuts)
        def _(owner):
            @pl.loop(0, levels)
            def _(item):
                core_copy(owner, item).wait_recv()

    for load in loads[2:]:
        load.wait()

    for part in range(2):
        for block in range(blocks):
            for entry in range(listed):
                name = index_ref[block, entry]
                tile = pool[name // blocks, part, lax.rem(name, blocks)]
                far[part, block, pl.ds(entry * heads, heads), :] = tile.astype(jnp.float32)

    scale = 1.0 / jnp.sqrt(jnp.float32(HEAD))
    contract = (((1,), (1,)), ((), ()))
    total_blocks = count * blocks

    def far_rows(part, block, head):
        return far[part, block, pl.ds(head, listed, stride=heads), :].astype(jnp.bfloat16)

    fast_copy(kbuf, 0).wait_recv()

    @pl.loop(0, chunks)
    def _(step):
        for start, length in key_pieces:
            @pl.when(has_slow & (step == start))
            def _():
                slow_copy(kbuf, k_send, k_recv, start, length).wait_recv()

        for inner in range(CHUNK_HEADS):
            head = step * CHUNK_HEADS + inner
            columns = pl.ds(pl.multiple_of(head * HEAD, HEAD), HEAD)
            for block in range(blocks):
                query = qbuf[block * BLOCK : (block + 1) * BLOCK, columns]
                near_keys = kbuf[pl.ds(block * BLOCK, span), columns]
                scores = lax.dot_general(
                    query, near_keys, contract, preferred_element_type=jnp.float32
                )
                far_scores = lax.dot_general(
                    query, far_rows(0, block, head), contract,
                    preferred_element_type=jnp.float32,
                )
                own = me * blocks + block
                pieces = []
                for place_of in range(2 * REACH + 1):
                    offset = place_of - REACH
                    piece = scores[:, place_of * BLOCK : (place_of + 1) * BLOCK]
                    if offset:
                        other = own + offset
                        allowed = (
                            (window_ref[block] >= abs(offset))
                            & (other >= 0)
                            & (other < total_blocks)
                        )
                        piece = jnp.where(allowed, piece, -1e30)
                    pieces.append(piece)
                tallest = functools.reduce(jnp.maximum, pieces)
                top = jnp.maximum(
                    jnp.max(tallest, axis=1, keepdims=True),
                    jnp.max(far_scores, axis=1, keepdims=True),
                )
                weights = [jnp.exp((piece - top) * scale) for piece in pieces]
                far_weights = jnp.exp((far_scores - top) * scale)
                total = jnp.sum(
                    functools.reduce(jnp.add, weights), axis=1, keepdims=True
                ) + jnp.sum(far_weights, axis=1, keepdims=True)
                for place_of, weight in enumerate(weights):
                    wbuf[head, block, :, place_of * BLOCK : (place_of + 1) * BLOCK] = (
                        weight.astype(jnp.bfloat16)
                    )
                fwbuf[head, block] = far_weights.astype(jnp.bfloat16)
                inv[head, block] = 1.0 / total

        @pl.when(hub & (step < borrowed))
        def _():
            lend_copy(step).wait_recv()
            relay_copy(step).start()

        @pl.when(hub & (step == borrowed))
        def _():
            @pl.loop(0, passed)
            def _(number):
                take_part(number).wait_recv()
                relay_part(number).start()

    fast_copy(kbuf, 0).wait_send()
    fast_copy(vbuf, 1).wait_send()

    @pl.when(~hub)
    def _():
        own_copy(1, across).wait_send()
        own_copy(2, fast_peer).wait_send()

    @pl.when(hub)
    def _():
        own_copy(0, slow_peer).wait_send()

        @pl.loop(1, levels)
        def _(hop):
            level_copy(hop).wait_send()

        @pl.loop(0, levels)
        def _(item):
            @pl.loop(0, cuts)
            def _(owner):
                core_copy(owner, item).wait_send()

            @pl.when(after)
            def _():
                @pl.loop(0, cut + 1)
                def _(owner):
                    right_copy(owner, item).wait_send()

            @pl.when(before)
            def _():
                @pl.loop(cut, cuts)
                def _(owner):
                    left_copy(owner, item).wait_send()

    fast_copy(vbuf, 1).wait_recv()

    def arrive(step):
        for start, length in value_pieces:
            @pl.when(hub & has_slow & (step == start))
            def _():
                slow_copy(vbuf, v_send, v_recv, start, length).wait_recv()

        @pl.when(~hub & has_slow)
        def _():
            slow_copy(vbuf, v_send, v_recv, step).wait_recv()

    def far_mixed(block, head):
        return jnp.dot(
            fwbuf[head, block], far_rows(1, block, head),
            preferred_element_type=jnp.float32,
        )

    @pl.loop(0, chunks - 1)
    def _(step):
        arrive(step)
        for inner in range(CHUNK_HEADS):
            head = step * CHUNK_HEADS + inner
            columns = pl.ds(pl.multiple_of(head * HEAD, HEAD), HEAD)
            for block in range(blocks):
                near_values = vbuf[pl.ds(block * BLOCK, span), columns]
                mixed = jnp.dot(
                    wbuf[head, block], near_values, preferred_element_type=jnp.float32
                ) + far_mixed(block, head)
                out_ref[block * BLOCK : (block + 1) * BLOCK, columns] = (
                    mixed * inv[head, block]
                ).astype(out_ref.dtype)

    final = [
        (chunks * CHUNK_HEADS - CHUNK_HEADS + inner, block)
        for inner in range(CHUNK_HEADS)
        for block in range(blocks)
    ]

    def final_dot(head, block, first, stop):
        first, stop = max(first, block * BLOCK), min(stop, block * BLOCK + span)
        return jnp.dot(
            wbuf[head, block, :, first - block * BLOCK : stop - block * BLOCK],
            vbuf[first:stop, head * HEAD : (head + 1) * HEAD],
            preferred_element_type=jnp.float32,
        )

    def final_near(first, stop):
        for n, (head, block) in enumerate(final):
            early[n] = final_dot(head, block, first, stop) + far_mixed(block, head)

    def final_slow(first, stop):
        for n, (head, block) in enumerate(final):
            mixed = early[n] + final_dot(head, block, first, stop)
            out_ref[
                block * BLOCK : (block + 1) * BLOCK, head * HEAD : (head + 1) * HEAD
            ] = (mixed * inv[head, block]).astype(out_ref.dtype)

    pl.when(odd)(lambda: final_near(0, edge))
    pl.when(~odd)(lambda: final_near(halo, edge + halo))

    @pl.when(has_slow)
    def _():
        for start, length in key_pieces:
            slow_copy(kbuf, k_send, k_recv, start, length).wait_send()

    @pl.when(hub)
    def _():
        @pl.loop(0, borrowed)
        def _(item):
            relay_copy(item).wait_send()

        @pl.loop(0, passed)
        def _(number):
            relay_part(number).wait_send()

    @pl.when(hub & has_slow)
    def _():
        for start, length in value_pieces[:-1]:
            slow_copy(vbuf, v_send, v_recv, start, length).wait_send()

    arrive(chunks - 1)
    pl.when(odd)(lambda: final_slow(edge, edge + halo))
    pl.when(~odd)(lambda: final_slow(0, halo))

    @pl.when(~hub)
    def _():
        @pl.loop(0, borrowed)
        def _(step):
            relay_copy(step).wait_send()

    @pl.when(hub & has_slow)
    def _():
        start, length = value_pieces[-1]
        slow_copy(vbuf, v_send, v_recv, start, length).wait_send()

    @pl.when(ends_after | ends_before)
    def _():
        @pl.loop(chunks // 2, chunks)
        def _(step):
            lend_copy(step).wait_send()

    @pl.when(~hub & has_slow & ~(ends_after | ends_before))
    def _():
        @pl.loop(0, lent)
        def _(step):
            slow_copy(vbuf, v_send, v_recv, step).wait_send()

        @pl.when(rest > 0)
        def _():
            @pl.loop(0, QUARTERS)
            def _(number):
                slow_part(number).wait_send()

        @pl.loop(lent + jnp.where(rest > 0, 1, 0), chunks)
        def _(step):
            slow_copy(vbuf, v_send, v_recv, step).wait_send()


def shards(cuts, group, queries, keys, values, window, summary_index):
    rows, width = queries.shape
    blocks = rows // BLOCK
    heads = width // HEAD
    listed = summary_index.shape[1]
    count = cuts * group
    levels = group // SEATS
    chunk = CHUNK_HEADS * HEAD
    chunks = width // chunk
    halo = REACH * BLOCK
    held = rows + 2 * halo
    span = (2 * REACH + 1) * BLOCK
    dma = pltpu.SemaphoreType.DMA
    return pl.pallas_call(
        functools.partial(kernel, cuts, group),
        out_shape=jax.ShapeDtypeStruct((rows, width), jnp.bfloat16),
        in_specs=[pl.BlockSpec(memory_space=pltpu.HBM)] * 5,
        out_specs=pl.BlockSpec(memory_space=pltpu.VMEM),
        scratch_shapes=[
            pltpu.VMEM((rows, width), jnp.bfloat16),
            pltpu.VMEM((held, width), jnp.bfloat16),
            pltpu.VMEM((held, width), jnp.bfloat16),
            pltpu.VMEM((chunks, halo, chunk), jnp.bfloat16),
            pltpu.SMEM(window.shape, jnp.int32),
            pltpu.SMEM(summary_index.shape, jnp.int32),
            pltpu.VMEM((2, blocks, heads, HEAD), jnp.bfloat16),
            pltpu.VMEM((count, 2, blocks, heads, HEAD), jnp.bfloat16),
            pltpu.VMEM((2, blocks, listed * heads, HEAD), jnp.float32),
            pltpu.VMEM((heads, blocks, BLOCK, span), jnp.bfloat16),
            pltpu.VMEM((heads, blocks, BLOCK, listed), jnp.bfloat16),
            pltpu.VMEM((heads, blocks, BLOCK, 1), jnp.float32),
            pltpu.VMEM((CHUNK_HEADS * blocks, BLOCK, HEAD), jnp.float32),
            dma((5,)),
            *[dma((chunks,))] * 4,
            *[dma((2,))] * 2,
            *[dma((chunks,))] * 2,
            *[dma((QUARTERS,))] * 3,
            *[dma((3,))] * 2,
            *[dma((cuts, levels))] * 2,
            *[dma((levels,))] * 2,
            *[dma((cuts, levels))] * 4,
            *[pltpu.SemaphoreType.REGULAR] * 2,
        ],
        compiler_params=pltpu.CompilerParams(
            collective_id=0, has_side_effects=True, vmem_limit_bytes=48 * 1024 * 1024
        ),
    )(
        *(
            pltpu.with_memory_space_constraint(operand, pltpu.HBM)
            for operand in (queries, keys, values, window, summary_index)
        )
    )


def solution(mesh):
    return jax.shard_map(
        functools.partial(shards, mesh.shape["cuts"], mesh.shape["group"]),
        mesh=mesh,
        in_specs=(
            P(("cuts", "group"), None),
            P(("cuts", "group"), None),
            P(("cuts", "group"), None),
            P(("cuts", "group")),
            P(("cuts", "group"), None),
        ),
        out_specs=P(("cuts", "group"), None),
        check_vma=False,
    )
```

```python
import functools

import jax
import jax.numpy as jnp
from jax import lax
from jax.experimental import pallas as pl
from jax.experimental.pallas import tpu as pltpu
from jax.sharding import PartitionSpec as P

HEAD = 128
BLOCK = 128
REACH = 2
CHUNK_HEADS = 2
SEATS = 4
QUARTERS = 4
MESH = pl.DeviceIdType.MESH


def pieces_of(*lengths):
    starts = [sum(lengths[:n]) for n in range(len(lengths))]
    return [(start, length) for start, length in zip(starts, lengths) if length]


def kernel(
    cuts, group,
    q_hbm, k_hbm, v_hbm, window_hbm, index_hbm, out_ref,
    qbuf, kbuf, vbuf, relay, window_ref, index_ref, own, pool, far, wbuf, fwbuf, inv, early,
    local_sem, k_send, k_recv, v_send, v_recv, fast_send, fast_recv,
    relay_send, relay_recv, part_send, part_recv, pass_send, own_send, own_recv, core_send, core_recv,
    level_send, level_recv,
    right_send, right_recv, left_send, left_recv, go_sem, far_sem,
):
    count = cuts * group
    rows, width = q_hbm.shape
    blocks = rows // BLOCK
    heads = width // HEAD
    halo = REACH * BLOCK
    span = (2 * REACH + 1) * BLOCK
    chunk = CHUNK_HEADS * HEAD
    chunks = width // chunk
    listed = index_ref.shape[1]
    levels = group // SEATS
    top = levels - 1

    cut = lax.axis_index("cuts")
    spot = lax.axis_index("group")
    me = cut * group + spot
    seat = lax.rem(spot, SEATS)
    level = spot // SEATS
    odd = lax.rem(seat, 2) == 1
    hub = (seat == 1) | (seat == 2)
    below, above = level > 0, level < top
    before, after = cut > 0, cut < cuts - 1

    fast_peer = jnp.where(odd, me - 1, me + 1)
    slow_peer = jnp.where(odd, me + 1, me - 1)
    has_slow = (slow_peer >= 0) & (slow_peer < count)
    across = jnp.where(seat < 2, me + 2, me - 2)

    trim = jnp.where(cut == 0, jnp.maximum(2 - level, 0), 0)
    upward = jnp.maximum((top - level) * chunks * QUARTERS // levels - trim, 0)
    downward = level * chunks // levels * QUARTERS
    quarters = jnp.where(
        seat == 3,
        jnp.where(above, upward, chunks * QUARTERS),
        jnp.where(seat == 0, jnp.where(below, downward, chunks * QUARTERS), 0),
    )
    quarters = jnp.where(has_slow, quarters, 0)
    lent = quarters // QUARTERS
    rest = quarters - lent * QUARTERS
    lend_peer = jnp.where(
        seat == 3,
        jnp.where(above, me - 2, me + SEATS),
        jnp.where(below, me + 2, me - SEATS),
    )
    relay_up = (seat == 1) & above
    relay_down = (seat == 2) & below
    ends_after = (seat == 3) & (level == top) & after
    ends_before = (seat == 0) & (level == 0) & before
    relay_after = (seat == 3) & (level == 0) & before
    relay_before = (seat == 0) & (level == top) & after
    taken = jnp.where(
        relay_up,
        upward,
        jnp.where(
            relay_down,
            downward,
            jnp.where(relay_after | relay_before, chunks * QUARTERS, 0),
        ),
    )
    borrowed = taken // QUARTERS
    passed = taken - borrowed * QUARTERS
    relay_peer = jnp.where(
        relay_up | relay_before, me + (SEATS - 1), me - (SEATS - 1)
    )

    def place(device):
        return (device // group, lax.rem(device, group))

    barrier = pltpu.get_barrier_semaphore()

    def greet(device, present=None):
        def signal():
            pl.semaphore_signal(
                barrier, inc=1, device_id=place(device), device_id_type=MESH
            )

        if present is None:
            signal()
        else:
            pl.when(present)(signal)

    greet(slow_peer, has_slow)
    greet(fast_peer)
    greet(across, hub)
    @pl.when(hub)
    def _():
        @pl.loop(1, levels)
        def _(hop):
            greet(cut * group + lax.rem(fast_peer - cut * group + hop * SEATS, group))

    greet(fast_peer - group, hub & before)
    greet(fast_peer + group, hub & after)
    greet(me - SEATS, relay_after)
    greet(me + SEATS, relay_before)
    greet(me - SEATS, (seat == 0) & below)
    greet(me + SEATS, (seat == 3) & above)
    greet(me - (SEATS - 1), ends_after)
    greet(me + (SEATS - 1), ends_before)
    expected = 1 + jnp.where(hub, 0, levels - 1)
    for present in (
        has_slow, ~hub, ~hub & before, ~hub & after,
        (seat == 0) & above, (seat == 3) & below,
        relay_after, relay_before, ends_after, ends_before,
    ):
        expected = expected + jnp.where(present, 1, 0)

    loads = [
        pltpu.make_async_copy(k_hbm, kbuf.at[pl.ds(halo, rows)], local_sem.at[0]),
        pltpu.make_async_copy(v_hbm, vbuf.at[pl.ds(halo, rows)], local_sem.at[1]),
        pltpu.make_async_copy(q_hbm, qbuf, local_sem.at[2]),
        pltpu.make_async_copy(window_hbm, window_ref, local_sem.at[3]),
        pltpu.make_async_copy(index_hbm, index_ref, local_sem.at[4]),
    ]
    for load in loads:
        load.start()

    def remote(source, target, send, recv, device):
        return pltpu.make_async_remote_copy(
            src_ref=source, dst_ref=target, send_sem=send, recv_sem=recv,
            device_id=place(device), device_id_type=MESH,
        )

    def columns_of(step):
        return pl.ds(pl.multiple_of(step * chunk, chunk), chunk)

    most = chunks - chunks // 2
    straight_keys = pieces_of(1, chunks // 2 - 1, most)
    other_keys = pieces_of(
        1, chunks // 2 - 1, most // 2, most // 4, most - most // 2 - most // 4
    )
    value_pieces = pieces_of(chunks - 2 - (chunks - 2) // 2, (chunks - 2) // 2, 1, 1)
    edge = halo + rows
    slow_from = pl.ds(pl.multiple_of(jnp.where(odd, rows, halo), BLOCK), halo)
    first_from = pl.ds(pl.multiple_of(jnp.where(odd, rows - halo, 0), BLOCK), halo)
    slow_to = pl.ds(pl.multiple_of(jnp.where(odd, 0, edge), BLOCK), halo)
    fast_from = pl.ds(pl.multiple_of(jnp.where(odd, halo, rows), BLOCK), halo)
    fast_to = pl.ds(pl.multiple_of(jnp.where(odd, edge, 0), BLOCK), halo)
    relay_to = pl.ds(
        pl.multiple_of(jnp.where(relay_up | relay_after, 0, edge), BLOCK), halo
    )

    def slow_copy(buffer, send, recv, step, length=1):
        columns = pl.ds(pl.multiple_of(step * chunk, chunk), length * chunk)
        return remote(
            buffer.at[slow_from, columns], buffer.at[slow_to, columns],
            send.at[step], recv.at[step], slow_peer,
        )

    piece = halo // QUARTERS

    def rows_of(start, number):
        return pl.ds(pl.multiple_of(start + number * piece, piece), piece)

    def slow_part(number):
        return remote(
            vbuf.at[rows_of(jnp.where(odd, rows, halo), number), columns_of(lent)],
            vbuf.at[rows_of(jnp.where(odd, 0, edge), number), columns_of(lent)],
            part_send.at[number], v_recv.at[lent], slow_peer,
        )

    def lend_part(number):
        return remote(
            vbuf.at[rows_of(jnp.where(odd, rows, halo), number), columns_of(lent)],
            relay.at[lent, rows_of(0, number)],
            part_send.at[number], part_recv.at[number], lend_peer,
        )

    def relay_part(number):
        return remote(
            relay.at[borrowed, rows_of(0, number)],
            vbuf.at[
                rows_of(jnp.where(relay_up | relay_after, 0, edge), number),
                columns_of(borrowed),
            ],
            pass_send.at[number], v_recv.at[borrowed], relay_peer,
        )

    def take_part(number):
        return remote(
            vbuf.at[rows_of(halo, number), columns_of(borrowed)],
            relay.at[borrowed, rows_of(0, number)],
            part_send.at[number], part_recv.at[number], lend_peer,
        )

    def fast_copy(buffer, part):
        return remote(
            buffer.at[fast_from], buffer.at[fast_to],
            fast_send.at[part], fast_recv.at[part], fast_peer,
        )

    def lend_copy(step):
        return remote(
            vbuf.at[slow_from, columns_of(step)], relay.at[step],
            v_send.at[step], relay_recv.at[step], lend_peer,
        )

    def relay_copy(step):
        return remote(
            relay.at[step], vbuf.at[relay_to, columns_of(step)],
            relay_send.at[step], v_recv.at[step], relay_peer,
        )

    def own_copy(place_of, device):
        return remote(
            own, pool.at[me], own_send.at[place_of], own_recv.at[place_of], device
        )

    def quad_copy(owner, item, send, recv, device):
        held = pool.at[pl.ds(owner * group + item * SEATS, SEATS)]
        return remote(held, held, send, recv, device)

    def level_copy(hop):
        return quad_copy(
            cut, level, level_send.at[hop], level_recv.at[hop],
            cut * group + lax.rem(spot + hop * SEATS, group),
        )

    def right_copy(owner, item):
        return quad_copy(
            owner, item, right_send.at[owner, item], right_recv.at[owner, item], me + group
        )

    def left_copy(owner, item):
        return quad_copy(
            owner, item, left_send.at[owner, item], left_recv.at[owner, item], me - group
        )

    def core_copy(owner, item):
        return quad_copy(
            owner, item, core_send.at[owner, item], core_recv.at[owner, item], fast_peer
        )

    def first_copy():
        length = straight_keys[0][1] * chunk
        return remote(
            k_hbm.at[first_from, pl.ds(0, length)], kbuf.at[slow_to, pl.ds(0, length)],
            k_send.at[0], k_recv.at[0], slow_peer,
        )

    @pl.when(hub)
    def _():
        pl.semaphore_wait(barrier, expected)

        @pl.when(has_slow)
        def _():
            first_copy().start()

    ones = jnp.ones((heads, BLOCK), jnp.bfloat16)
    row = lax.broadcasted_iota(jnp.int32, (heads, HEAD), 0)
    for part, (buffer, divisor) in enumerate(
        ((kbuf, jnp.sqrt(jnp.float32(BLOCK))), (vbuf, jnp.float32(BLOCK)))
    ):
        loads[part].wait()
        for block in range(blocks):
            pooled = jnp.zeros((heads, HEAD), jnp.float32)
            sums = jnp.dot(
                ones,
                buffer[halo + block * BLOCK : halo + (block + 1) * BLOCK, :],
                preferred_element_type=jnp.float32,
            )
            for head in range(heads):
                pooled = jnp.where(
                    row == head, sums[:, head * HEAD : (head + 1) * HEAD], pooled
                )
            own[part, block] = (pooled / divisor).astype(jnp.bfloat16)
    @pl.when(~hub)
    def _():
        pl.semaphore_wait(barrier, expected)

    @pl.when(hub)
    def _():
        own_copy(0, slow_peer).start()

    @pl.when(~hub)
    def _():
        own_copy(1, across).start()
        own_copy(2, fast_peer).start()
        pl.semaphore_signal(
            far_sem, inc=1, device_id=place(fast_peer), device_id_type=MESH
        )

    def send_slow(whole):
        @pl.when(has_slow)
        def _():
            for start, length in straight_keys[1:] if whole else other_keys:
                slow_copy(kbuf, k_send, k_recv, start, length).start()

            if whole:
                for start, length in value_pieces:
                    slow_copy(vbuf, v_send, v_recv, start, length).start()
            else:
                @pl.when(rest > 0)
                def _():
                    @pl.loop(rest, QUARTERS)
                    def _(number):
                        slow_part(number).start()

                @pl.loop(lent + jnp.where(rest > 0, 1, 0), chunks)
                def _(step):
                    slow_copy(vbuf, v_send, v_recv, step).start()

    @pl.loop(0, lent)
    def _(step):
        lend_copy(step).start()

    @pl.loop(0, rest)
    def _(number):
        lend_part(number).start()

    pl.when(hub)(lambda: send_slow(True))
    fast_copy(kbuf, 0).start()
    fast_copy(vbuf, 1).start()

    @pl.when(me == 0)
    def _():
        kbuf[pl.ds(0, halo), :] = jnp.zeros((halo, width), kbuf.dtype)
        vbuf[pl.ds(0, halo), :] = jnp.zeros((halo, width), vbuf.dtype)

    @pl.when(me == count - 1)
    def _():
        kbuf[pl.ds(edge, halo), :] = jnp.zeros((halo, width), kbuf.dtype)
        vbuf[pl.ds(edge, halo), :] = jnp.zeros((halo, width), vbuf.dtype)

    def spread(item):
        @pl.when(after)
        def _():
            right_copy(cut, item).start()

        @pl.when(before)
        def _():
            left_copy(cut, item).start()

        core_copy(cut, item).start()

    @pl.when(hub)
    def _():
        pool[me] = own[...]
        own_copy(0, slow_peer).wait_recv()
        own_copy(1, across).wait_recv()
        own_copy(2, fast_peer).wait_recv()
        pl.semaphore_wait(far_sem, 1)

        @pl.loop(1, levels)
        def _(hop):
            level_copy(hop).start()

        @pl.when(relay_up | relay_down)
        def _():
            pl.semaphore_signal(
                go_sem, inc=1, device_id=place(relay_peer), device_id_type=MESH
            )

        spread(level)

        @pl.loop(1, levels)
        def _(hop):
            level_copy(hop).wait_recv()
            spread(lax.rem(level + levels - hop, levels))

        @pl.loop(1, cuts)
        def _(hop):
            @pl.loop(0, levels)
            def _(item):
                @pl.when(cut >= hop)
                def _():
                    right_copy(cut - hop, item).wait_recv()

                    @pl.when(after)
                    def _():
                        right_copy(cut - hop, item).start()

                    core_copy(cut - hop, item).start()

                @pl.when(cut + hop < cuts)
                def _():
                    left_copy(cut + hop, item).wait_recv()

                    @pl.when(before)
                    def _():
                        left_copy(cut + hop, item).start()

                    core_copy(cut + hop, item).start()

    @pl.when(~hub)
    def _():
        @pl.when(((seat == 3) & above) | ((seat == 0) & below))
        def _():
            pl.semaphore_wait(go_sem, 1)

        @pl.when(ends_after | ends_before)
        def _():
            @pl.loop(0, chunks // 2)
            def _(step):
                lend_copy(step).wait_send()

        send_slow(False)

        @pl.loop(0, borrowed)
        def _(step):
            lend_copy(step).wait_recv()
            relay_copy(step).start()

        @pl.loop(0, cuts)
        def _(owner):
            @pl.loop(0, levels)
            def _(item):
                core_copy(owner, item).wait_recv()

    for load in loads[2:]:
        load.wait()

    for part in range(2):
        for block in range(blocks):
            for entry in range(listed):
                name = index_ref[block, entry]
                tile = pool[name // blocks, part, lax.rem(name, blocks)]
                far[part, block, pl.ds(entry * heads, heads), :] = tile.astype(jnp.float32)

    scale = 1.0 / jnp.sqrt(jnp.float32(HEAD))
    contract = (((1,), (1,)), ((), ()))
    total_blocks = count * blocks

    def far_rows(part, block, head):
        return far[part, block, pl.ds(head, listed, stride=heads), :].astype(jnp.bfloat16)

    fast_copy(kbuf, 0).wait_recv()

    @pl.loop(0, chunks)
    def _(step):
        for mine, pieces in ((hub, straight_keys), (~hub, other_keys)):
            for start, length in pieces:
                @pl.when(mine & has_slow & (step == start))
                def _():
                    slow_copy(kbuf, k_send, k_recv, start, length).wait_recv()

        for inner in range(CHUNK_HEADS):
            head = step * CHUNK_HEADS + inner
            columns = pl.ds(pl.multiple_of(head * HEAD, HEAD), HEAD)
            for block in range(blocks):
                query = qbuf[block * BLOCK : (block + 1) * BLOCK, columns]
                near_keys = kbuf[pl.ds(block * BLOCK, span), columns]
                scores = lax.dot_general(
                    query, near_keys, contract, preferred_element_type=jnp.float32
                )
                far_scores = lax.dot_general(
                    query, far_rows(0, block, head), contract,
                    preferred_element_type=jnp.float32,
                )
                own = me * blocks + block
                pieces = []
                for place_of in range(2 * REACH + 1):
                    offset = place_of - REACH
                    piece = scores[:, place_of * BLOCK : (place_of + 1) * BLOCK]
                    if offset:
                        other = own + offset
                        allowed = (
                            (window_ref[block] >= abs(offset))
                            & (other >= 0)
                            & (other < total_blocks)
                        )
                        piece = jnp.where(allowed, piece, -1e30)
                    pieces.append(piece)
                tallest = functools.reduce(jnp.maximum, pieces)
                top = jnp.maximum(
                    jnp.max(tallest, axis=1, keepdims=True),
                    jnp.max(far_scores, axis=1, keepdims=True),
                )
                weights = [jnp.exp((piece - top) * scale) for piece in pieces]
                far_weights = jnp.exp((far_scores - top) * scale)
                total = jnp.sum(
                    functools.reduce(jnp.add, weights), axis=1, keepdims=True
                ) + jnp.sum(far_weights, axis=1, keepdims=True)
                for place_of, weight in enumerate(weights):
                    wbuf[head, block, :, place_of * BLOCK : (place_of + 1) * BLOCK] = (
                        weight.astype(jnp.bfloat16)
                    )
                fwbuf[head, block] = far_weights.astype(jnp.bfloat16)
                inv[head, block] = 1.0 / total

        @pl.when(hub & (step < borrowed))
        def _():
            lend_copy(step).wait_recv()
            relay_copy(step).start()

        @pl.when(hub & (step == borrowed))
        def _():
            @pl.loop(0, passed)
            def _(number):
                take_part(number).wait_recv()
                relay_part(number).start()

    fast_copy(kbuf, 0).wait_send()
    fast_copy(vbuf, 1).wait_send()

    @pl.when(~hub)
    def _():
        own_copy(1, across).wait_send()
        own_copy(2, fast_peer).wait_send()

    @pl.when(hub)
    def _():
        own_copy(0, slow_peer).wait_send()

        @pl.loop(1, levels)
        def _(hop):
            level_copy(hop).wait_send()

        @pl.loop(0, levels)
        def _(item):
            @pl.loop(0, cuts)
            def _(owner):
                core_copy(owner, item).wait_send()

            @pl.when(after)
            def _():
                @pl.loop(0, cut + 1)
                def _(owner):
                    right_copy(owner, item).wait_send()

            @pl.when(before)
            def _():
                @pl.loop(cut, cuts)
                def _(owner):
                    left_copy(owner, item).wait_send()

    fast_copy(vbuf, 1).wait_recv()

    def arrive(step):
        for start, length in value_pieces:
            @pl.when(hub & has_slow & (step == start))
            def _():
                slow_copy(vbuf, v_send, v_recv, start, length).wait_recv()

        @pl.when(~hub & has_slow)
        def _():
            slow_copy(vbuf, v_send, v_recv, step).wait_recv()

    def far_mixed(block, head):
        return jnp.dot(
            fwbuf[head, block], far_rows(1, block, head),
            preferred_element_type=jnp.float32,
        )

    @pl.loop(0, chunks - 1)
    def _(step):
        arrive(step)
        for inner in range(CHUNK_HEADS):
            head = step * CHUNK_HEADS + inner
            columns = pl.ds(pl.multiple_of(head * HEAD, HEAD), HEAD)
            for block in range(blocks):
                near_values = vbuf[pl.ds(block * BLOCK, span), columns]
                mixed = jnp.dot(
                    wbuf[head, block], near_values, preferred_element_type=jnp.float32
                ) + far_mixed(block, head)
                out_ref[block * BLOCK : (block + 1) * BLOCK, columns] = (
                    mixed * inv[head, block]
                ).astype(out_ref.dtype)

    final = [
        (chunks * CHUNK_HEADS - CHUNK_HEADS + inner, block)
        for inner in range(CHUNK_HEADS)
        for block in range(blocks)
    ]

    def final_dot(head, block, first, stop):
        first, stop = max(first, block * BLOCK), min(stop, block * BLOCK + span)
        return jnp.dot(
            wbuf[head, block, :, first - block * BLOCK : stop - block * BLOCK],
            vbuf[first:stop, head * HEAD : (head + 1) * HEAD],
            preferred_element_type=jnp.float32,
        )

    def final_near(first, stop):
        for n, (head, block) in enumerate(final):
            early[n] = final_dot(head, block, first, stop) + far_mixed(block, head)

    def final_slow(first, stop):
        for n, (head, block) in enumerate(final):
            mixed = early[n] + final_dot(head, block, first, stop)
            out_ref[
                block * BLOCK : (block + 1) * BLOCK, head * HEAD : (head + 1) * HEAD
            ] = (mixed * inv[head, block]).astype(out_ref.dtype)

    pl.when(odd)(lambda: final_near(0, edge))
    pl.when(~odd)(lambda: final_near(halo, edge + halo))

    for mine, pieces in ((hub, straight_keys), (~hub, other_keys)):
        @pl.when(mine & has_slow)
        def _():
            for start, length in pieces:
                slow_copy(kbuf, k_send, k_recv, start, length).wait_send()

    @pl.when(hub)
    def _():
        @pl.loop(0, borrowed)
        def _(item):
            relay_copy(item).wait_send()

        @pl.loop(0, passed)
        def _(number):
            relay_part(number).wait_send()

    @pl.when(hub & has_slow)
    def _():
        for start, length in value_pieces[:-1]:
            slow_copy(vbuf, v_send, v_recv, start, length).wait_send()

    arrive(chunks - 1)
    pl.when(odd)(lambda: final_slow(edge, edge + halo))
    pl.when(~odd)(lambda: final_slow(0, halo))

    @pl.when(~hub)
    def _():
        @pl.loop(0, borrowed)
        def _(step):
            relay_copy(step).wait_send()

    @pl.when(hub & has_slow)
    def _():
        start, length = value_pieces[-1]
        slow_copy(vbuf, v_send, v_recv, start, length).wait_send()

    @pl.when(ends_after | ends_before)
    def _():
        @pl.loop(chunks // 2, chunks)
        def _(step):
            lend_copy(step).wait_send()

    @pl.when(~hub & has_slow & ~(ends_after | ends_before))
    def _():
        @pl.loop(0, lent)
        def _(step):
            slow_copy(vbuf, v_send, v_recv, step).wait_send()

        @pl.when(rest > 0)
        def _():
            @pl.loop(0, QUARTERS)
            def _(number):
                slow_part(number).wait_send()

        @pl.loop(lent + jnp.where(rest > 0, 1, 0), chunks)
        def _(step):
            slow_copy(vbuf, v_send, v_recv, step).wait_send()


def shards(cuts, group, queries, keys, values, window, summary_index):
    rows, width = queries.shape
    blocks = rows // BLOCK
    heads = width // HEAD
    listed = summary_index.shape[1]
    count = cuts * group
    levels = group // SEATS
    chunk = CHUNK_HEADS * HEAD
    chunks = width // chunk
    halo = REACH * BLOCK
    held = rows + 2 * halo
    span = (2 * REACH + 1) * BLOCK
    dma = pltpu.SemaphoreType.DMA
    return pl.pallas_call(
        functools.partial(kernel, cuts, group),
        out_shape=jax.ShapeDtypeStruct((rows, width), jnp.bfloat16),
        in_specs=[pl.BlockSpec(memory_space=pltpu.HBM)] * 5,
        out_specs=pl.BlockSpec(memory_space=pltpu.VMEM),
        scratch_shapes=[
            pltpu.VMEM((rows, width), jnp.bfloat16),
            pltpu.VMEM((held, width), jnp.bfloat16),
            pltpu.VMEM((held, width), jnp.bfloat16),
            pltpu.VMEM((chunks, halo, chunk), jnp.bfloat16),
            pltpu.SMEM(window.shape, jnp.int32),
            pltpu.SMEM(summary_index.shape, jnp.int32),
            pltpu.VMEM((2, blocks, heads, HEAD), jnp.bfloat16),
            pltpu.VMEM((count, 2, blocks, heads, HEAD), jnp.bfloat16),
            pltpu.VMEM((2, blocks, listed * heads, HEAD), jnp.float32),
            pltpu.VMEM((heads, blocks, BLOCK, span), jnp.bfloat16),
            pltpu.VMEM((heads, blocks, BLOCK, listed), jnp.bfloat16),
            pltpu.VMEM((heads, blocks, BLOCK, 1), jnp.float32),
            pltpu.VMEM((CHUNK_HEADS * blocks, BLOCK, HEAD), jnp.float32),
            dma((5,)),
            *[dma((chunks,))] * 4,
            *[dma((2,))] * 2,
            *[dma((chunks,))] * 2,
            *[dma((QUARTERS,))] * 3,
            *[dma((3,))] * 2,
            *[dma((cuts, levels))] * 2,
            *[dma((levels,))] * 2,
            *[dma((cuts, levels))] * 4,
            *[pltpu.SemaphoreType.REGULAR] * 2,
        ],
        compiler_params=pltpu.CompilerParams(
            collective_id=0, has_side_effects=True, vmem_limit_bytes=48 * 1024 * 1024
        ),
    )(
        *(
            pltpu.with_memory_space_constraint(operand, pltpu.HBM)
            for operand in (queries, keys, values, window, summary_index)
        )
    )


def solution(mesh):
    return jax.shard_map(
        functools.partial(shards, mesh.shape["cuts"], mesh.shape["group"]),
        mesh=mesh,
        in_specs=(
            P(("cuts", "group"), None),
            P(("cuts", "group"), None),
            P(("cuts", "group"), None),
            P(("cuts", "group")),
            P(("cuts", "group"), None),
        ),
        out_specs=P(("cuts", "group"), None),
        check_vma=False,
    )
```

```python
import functools

import jax
import jax.numpy as jnp
from jax import lax
from jax.experimental import pallas as pl
from jax.experimental.pallas import tpu as pltpu
from jax.sharding import PartitionSpec as P

HEAD = 128
BLOCK = 128
REACH = 2
CHUNK_HEADS = 2
SEATS = 4
QUARTERS = 4
MESH = pl.DeviceIdType.MESH


def pieces_of(*lengths):
    starts = [sum(lengths[:n]) for n in range(len(lengths))]
    return [(start, length) for start, length in zip(starts, lengths) if length]


def kernel(
    cuts, group,
    q_hbm, k_hbm, v_hbm, window_hbm, index_hbm, out_ref,
    qbuf, kbuf, vbuf, relay, window_ref, index_ref, own, pool, far, wbuf, fwbuf, inv, early,
    local_sem, k_send, k_recv, v_send, v_recv, fast_send, fast_recv,
    relay_send, relay_recv, part_send, part_recv, pass_send, own_send, own_recv, core_send, core_recv,
    level_send, level_recv,
    right_send, right_recv, left_send, left_recv, go_sem, far_sem,
):
    count = cuts * group
    rows, width = q_hbm.shape
    blocks = rows // BLOCK
    heads = width // HEAD
    halo = REACH * BLOCK
    span = (2 * REACH + 1) * BLOCK
    chunk = CHUNK_HEADS * HEAD
    chunks = width // chunk
    listed = index_ref.shape[1]
    levels = group // SEATS
    top = levels - 1

    cut = lax.axis_index("cuts")
    spot = lax.axis_index("group")
    me = cut * group + spot
    seat = lax.rem(spot, SEATS)
    level = spot // SEATS
    odd = lax.rem(seat, 2) == 1
    hub = (seat == 1) | (seat == 2)
    below, above = level > 0, level < top
    before, after = cut > 0, cut < cuts - 1

    fast_peer = jnp.where(odd, me - 1, me + 1)
    slow_peer = jnp.where(odd, me + 1, me - 1)
    has_slow = (slow_peer >= 0) & (slow_peer < count)
    across = jnp.where(seat < 2, me + 2, me - 2)

    trim = jnp.where(cut == 0, jnp.minimum(top - level, 2), 0)
    upward = jnp.maximum((top - level) * chunks * QUARTERS // levels - trim, 0)
    downward = level * chunks // levels * QUARTERS
    quarters = jnp.where(
        seat == 3,
        jnp.where(above, upward, chunks * QUARTERS),
        jnp.where(seat == 0, jnp.where(below, downward, chunks * QUARTERS), 0),
    )
    quarters = jnp.where(has_slow, quarters, 0)
    lent = quarters // QUARTERS
    rest = quarters - lent * QUARTERS
    lend_peer = jnp.where(
        seat == 3,
        jnp.where(above, me - 2, me + SEATS),
        jnp.where(below, me + 2, me - SEATS),
    )
    relay_up = (seat == 1) & above
    relay_down = (seat == 2) & below
    ends_after = (seat == 3) & (level == top) & after
    ends_before = (seat == 0) & (level == 0) & before
    relay_after = (seat == 3) & (level == 0) & before
    relay_before = (seat == 0) & (level == top) & after
    taken = jnp.where(
        relay_up,
        upward,
        jnp.where(
            relay_down,
            downward,
            jnp.where(relay_after | relay_before, chunks * QUARTERS, 0),
        ),
    )
    borrowed = taken // QUARTERS
    passed = taken - borrowed * QUARTERS
    relay_peer = jnp.where(
        relay_up | relay_before, me + (SEATS - 1), me - (SEATS - 1)
    )

    def place(device):
        return (device // group, lax.rem(device, group))

    barrier = pltpu.get_barrier_semaphore()

    def greet(device, present=None):
        def signal():
            pl.semaphore_signal(
                barrier, inc=1, device_id=place(device), device_id_type=MESH
            )

        if present is None:
            signal()
        else:
            pl.when(present)(signal)

    greet(slow_peer, has_slow)
    greet(fast_peer)
    greet(across, hub)
    @pl.when(hub)
    def _():
        @pl.loop(1, levels)
        def _(hop):
            greet(cut * group + lax.rem(fast_peer - cut * group + hop * SEATS, group))

    greet(fast_peer - group, hub & before)
    greet(fast_peer + group, hub & after)
    greet(me - SEATS, relay_after)
    greet(me + SEATS, relay_before)
    greet(me - SEATS, (seat == 0) & below)
    greet(me + SEATS, (seat == 3) & above)
    greet(me - (SEATS - 1), ends_after)
    greet(me + (SEATS - 1), ends_before)
    expected = 1 + jnp.where(hub, 0, levels - 1)
    for present in (
        has_slow, ~hub, ~hub & before, ~hub & after,
        (seat == 0) & above, (seat == 3) & below,
        relay_after, relay_before, ends_after, ends_before,
    ):
        expected = expected + jnp.where(present, 1, 0)

    loads = [
        pltpu.make_async_copy(k_hbm, kbuf.at[pl.ds(halo, rows)], local_sem.at[0]),
        pltpu.make_async_copy(v_hbm, vbuf.at[pl.ds(halo, rows)], local_sem.at[1]),
        pltpu.make_async_copy(q_hbm, qbuf, local_sem.at[2]),
        pltpu.make_async_copy(window_hbm, window_ref, local_sem.at[3]),
        pltpu.make_async_copy(index_hbm, index_ref, local_sem.at[4]),
    ]
    for load in loads:
        load.start()

    def remote(source, target, send, recv, device):
        return pltpu.make_async_remote_copy(
            src_ref=source, dst_ref=target, send_sem=send, recv_sem=recv,
            device_id=place(device), device_id_type=MESH,
        )

    def columns_of(step):
        return pl.ds(pl.multiple_of(step * chunk, chunk), chunk)

    most = chunks - chunks // 2
    straight_keys = pieces_of(1, chunks // 2 - 1, most)
    other_keys = pieces_of(
        1, chunks // 2 - 1, most // 2, most // 4, most - most // 2 - most // 4
    )
    value_pieces = pieces_of(chunks - 2 - (chunks - 2) // 2, (chunks - 2) // 2, 1, 1)
    edge = halo + rows
    slow_from = pl.ds(pl.multiple_of(jnp.where(odd, rows, halo), BLOCK), halo)
    first_from = pl.ds(pl.multiple_of(jnp.where(odd, rows - halo, 0), BLOCK), halo)
    slow_to = pl.ds(pl.multiple_of(jnp.where(odd, 0, edge), BLOCK), halo)
    fast_from = pl.ds(pl.multiple_of(jnp.where(odd, halo, rows), BLOCK), halo)
    fast_to = pl.ds(pl.multiple_of(jnp.where(odd, edge, 0), BLOCK), halo)
    relay_to = pl.ds(
        pl.multiple_of(jnp.where(relay_up | relay_after, 0, edge), BLOCK), halo
    )

    def slow_copy(buffer, send, recv, step, length=1):
        columns = pl.ds(pl.multiple_of(step * chunk, chunk), length * chunk)
        return remote(
            buffer.at[slow_from, columns], buffer.at[slow_to, columns],
            send.at[step], recv.at[step], slow_peer,
        )

    piece = halo // QUARTERS

    def rows_of(start, number):
        return pl.ds(pl.multiple_of(start + number * piece, piece), piece)

    def slow_part(number):
        return remote(
            vbuf.at[rows_of(jnp.where(odd, rows, halo), number), columns_of(lent)],
            vbuf.at[rows_of(jnp.where(odd, 0, edge), number), columns_of(lent)],
            part_send.at[number], v_recv.at[lent], slow_peer,
        )

    def lend_part(number):
        return remote(
            vbuf.at[rows_of(jnp.where(odd, rows, halo), number), columns_of(lent)],
            relay.at[lent, rows_of(0, number)],
            part_send.at[number], part_recv.at[number], lend_peer,
        )

    def relay_part(number):
        return remote(
            relay.at[borrowed, rows_of(0, number)],
            vbuf.at[
                rows_of(jnp.where(relay_up | relay_after, 0, edge), number),
                columns_of(borrowed),
            ],
            pass_send.at[number], v_recv.at[borrowed], relay_peer,
        )

    def take_part(number):
        return remote(
            vbuf.at[rows_of(halo, number), columns_of(borrowed)],
            relay.at[borrowed, rows_of(0, number)],
            part_send.at[number], part_recv.at[number], lend_peer,
        )

    def fast_copy(buffer, part):
        return remote(
            buffer.at[fast_from], buffer.at[fast_to],
            fast_send.at[part], fast_recv.at[part], fast_peer,
        )

    def lend_copy(step):
        return remote(
            vbuf.at[slow_from, columns_of(step)], relay.at[step],
            v_send.at[step], relay_recv.at[step], lend_peer,
        )

    def relay_copy(step):
        return remote(
            relay.at[step], vbuf.at[relay_to, columns_of(step)],
            relay_send.at[step], v_recv.at[step], relay_peer,
        )

    def own_copy(place_of, device):
        return remote(
            own, pool.at[me], own_send.at[place_of], own_recv.at[place_of], device
        )

    def quad_copy(owner, item, send, recv, device):
        held = pool.at[pl.ds(owner * group + item * SEATS, SEATS)]
        return remote(held, held, send, recv, device)

    def level_copy(hop):
        return quad_copy(
            cut, level, level_send.at[hop], level_recv.at[hop],
            cut * group + lax.rem(spot + hop * SEATS, group),
        )

    def right_copy(owner, item):
        return quad_copy(
            owner, item, right_send.at[owner, item], right_recv.at[owner, item], me + group
        )

    def left_copy(owner, item):
        return quad_copy(
            owner, item, left_send.at[owner, item], left_recv.at[owner, item], me - group
        )

    def core_copy(owner, item):
        return quad_copy(
            owner, item, core_send.at[owner, item], core_recv.at[owner, item], fast_peer
        )

    def first_copy():
        length = straight_keys[0][1] * chunk
        return remote(
            k_hbm.at[first_from, pl.ds(0, length)], kbuf.at[slow_to, pl.ds(0, length)],
            k_send.at[0], k_recv.at[0], slow_peer,
        )

    @pl.when(hub)
    def _():
        pl.semaphore_wait(barrier, expected)

        @pl.when(has_slow)
        def _():
            first_copy().start()

    ones = jnp.ones((heads, BLOCK), jnp.bfloat16)
    row = lax.broadcasted_iota(jnp.int32, (heads, HEAD), 0)
    for part, (buffer, divisor) in enumerate(
        ((kbuf, jnp.sqrt(jnp.float32(BLOCK))), (vbuf, jnp.float32(BLOCK)))
    ):
        loads[part].wait()
        for block in range(blocks):
            pooled = jnp.zeros((heads, HEAD), jnp.float32)
            sums = jnp.dot(
                ones,
                buffer[halo + block * BLOCK : halo + (block + 1) * BLOCK, :],
                preferred_element_type=jnp.float32,
            )
            for head in range(heads):
                pooled = jnp.where(
                    row == head, sums[:, head * HEAD : (head + 1) * HEAD], pooled
                )
            own[part, block] = (pooled / divisor).astype(jnp.bfloat16)
    @pl.when(~hub)
    def _():
        pl.semaphore_wait(barrier, expected)

    @pl.when(hub)
    def _():
        own_copy(0, slow_peer).start()

    @pl.when(~hub)
    def _():
        own_copy(1, across).start()
        own_copy(2, fast_peer).start()
        pl.semaphore_signal(
            far_sem, inc=1, device_id=place(fast_peer), device_id_type=MESH
        )

    def send_slow(whole):
        @pl.when(has_slow)
        def _():
            for start, length in straight_keys[1:] if whole else other_keys:
                slow_copy(kbuf, k_send, k_recv, start, length).start()

            if whole:
                for start, length in value_pieces:
                    slow_copy(vbuf, v_send, v_recv, start, length).start()
            else:
                @pl.when(rest > 0)
                def _():
                    @pl.loop(rest, QUARTERS)
                    def _(number):
                        slow_part(number).start()

                @pl.loop(lent + jnp.where(rest > 0, 1, 0), chunks)
                def _(step):
                    slow_copy(vbuf, v_send, v_recv, step).start()

    @pl.loop(0, lent)
    def _(step):
        lend_copy(step).start()

    @pl.loop(0, rest)
    def _(number):
        lend_part(number).start()

    pl.when(hub)(lambda: send_slow(True))
    fast_copy(kbuf, 0).start()
    fast_copy(vbuf, 1).start()

    @pl.when(me == 0)
    def _():
        kbuf[pl.ds(0, halo), :] = jnp.zeros((halo, width), kbuf.dtype)
        vbuf[pl.ds(0, halo), :] = jnp.zeros((halo, width), vbuf.dtype)

    @pl.when(me == count - 1)
    def _():
        kbuf[pl.ds(edge, halo), :] = jnp.zeros((halo, width), kbuf.dtype)
        vbuf[pl.ds(edge, halo), :] = jnp.zeros((halo, width), vbuf.dtype)

    def spread(item):
        @pl.when(after)
        def _():
            right_copy(cut, item).start()

        @pl.when(before)
        def _():
            left_copy(cut, item).start()

        core_copy(cut, item).start()

    @pl.when(hub)
    def _():
        pool[me] = own[...]
        own_copy(0, slow_peer).wait_recv()
        own_copy(1, across).wait_recv()
        own_copy(2, fast_peer).wait_recv()
        pl.semaphore_wait(far_sem, 1)

        @pl.loop(1, levels)
        def _(hop):
            level_copy(hop).start()

        @pl.when(relay_up | relay_down)
        def _():
            pl.semaphore_signal(
                go_sem, inc=1, device_id=place(relay_peer), device_id_type=MESH
            )

        spread(level)

        @pl.loop(1, levels)
        def _(hop):
            level_copy(hop).wait_recv()
            spread(lax.rem(level + levels - hop, levels))

        @pl.loop(1, cuts)
        def _(hop):
            @pl.loop(0, levels)
            def _(item):
                @pl.when(cut >= hop)
                def _():
                    right_copy(cut - hop, item).wait_recv()

                    @pl.when(after)
                    def _():
                        right_copy(cut - hop, item).start()

                    core_copy(cut - hop, item).start()

                @pl.when(cut + hop < cuts)
                def _():
                    left_copy(cut + hop, item).wait_recv()

                    @pl.when(before)
                    def _():
                        left_copy(cut + hop, item).start()

                    core_copy(cut + hop, item).start()

    @pl.when(~hub)
    def _():
        @pl.when(((seat == 3) & above) | ((seat == 0) & below))
        def _():
            pl.semaphore_wait(go_sem, 1)

        @pl.when(ends_after | ends_before)
        def _():
            @pl.loop(0, chunks // 2)
            def _(step):
                lend_copy(step).wait_send()

        send_slow(False)

        @pl.loop(0, borrowed)
        def _(step):
            lend_copy(step).wait_recv()
            relay_copy(step).start()

        @pl.loop(0, cuts)
        def _(owner):
            @pl.loop(0, levels)
            def _(item):
                core_copy(owner, item).wait_recv()

    for load in loads[2:]:
        load.wait()

    for part in range(2):
        for block in range(blocks):
            for entry in range(listed):
                name = index_ref[block, entry]
                tile = pool[name // blocks, part, lax.rem(name, blocks)]
                far[part, block, pl.ds(entry * heads, heads), :] = tile.astype(jnp.float32)

    scale = 1.0 / jnp.sqrt(jnp.float32(HEAD))
    contract = (((1,), (1,)), ((), ()))
    total_blocks = count * blocks

    def far_rows(part, block, head):
        return far[part, block, pl.ds(head, listed, stride=heads), :].astype(jnp.bfloat16)

    fast_copy(kbuf, 0).wait_recv()

    @pl.loop(0, chunks)
    def _(step):
        for mine, pieces in ((hub, straight_keys), (~hub, other_keys)):
            for start, length in pieces:
                @pl.when(mine & has_slow & (step == start))
                def _():
                    slow_copy(kbuf, k_send, k_recv, start, length).wait_recv()

        for inner in range(CHUNK_HEADS):
            head = step * CHUNK_HEADS + inner
            columns = pl.ds(pl.multiple_of(head * HEAD, HEAD), HEAD)
            for block in range(blocks):
                query = qbuf[block * BLOCK : (block + 1) * BLOCK, columns]
                near_keys = kbuf[pl.ds(block * BLOCK, span), columns]
                scores = lax.dot_general(
                    query, near_keys, contract, preferred_element_type=jnp.float32
                )
                far_scores = lax.dot_general(
                    query, far_rows(0, block, head), contract,
                    preferred_element_type=jnp.float32,
                )
                own = me * blocks + block
                pieces = []
                for place_of in range(2 * REACH + 1):
                    offset = place_of - REACH
                    piece = scores[:, place_of * BLOCK : (place_of + 1) * BLOCK]
                    if offset:
                        other = own + offset
                        allowed = (
                            (window_ref[block] >= abs(offset))
                            & (other >= 0)
                            & (other < total_blocks)
                        )
                        piece = jnp.where(allowed, piece, -1e30)
                    pieces.append(piece)
                tallest = functools.reduce(jnp.maximum, pieces)
                top = jnp.maximum(
                    jnp.max(tallest, axis=1, keepdims=True),
                    jnp.max(far_scores, axis=1, keepdims=True),
                )
                weights = [jnp.exp((piece - top) * scale) for piece in pieces]
                far_weights = jnp.exp((far_scores - top) * scale)
                total = jnp.sum(
                    functools.reduce(jnp.add, weights), axis=1, keepdims=True
                ) + jnp.sum(far_weights, axis=1, keepdims=True)
                for place_of, weight in enumerate(weights):
                    wbuf[head, block, :, place_of * BLOCK : (place_of + 1) * BLOCK] = (
                        weight.astype(jnp.bfloat16)
                    )
                fwbuf[head, block] = far_weights.astype(jnp.bfloat16)
                inv[head, block] = 1.0 / total

        @pl.when(hub & (step < borrowed))
        def _():
            lend_copy(step).wait_recv()
            relay_copy(step).start()

        @pl.when(hub & (step == borrowed))
        def _():
            @pl.loop(0, passed)
            def _(number):
                take_part(number).wait_recv()
                relay_part(number).start()

    fast_copy(kbuf, 0).wait_send()
    fast_copy(vbuf, 1).wait_send()

    @pl.when(~hub)
    def _():
        own_copy(1, across).wait_send()
        own_copy(2, fast_peer).wait_send()

    @pl.when(hub)
    def _():
        own_copy(0, slow_peer).wait_send()

        @pl.loop(1, levels)
        def _(hop):
            level_copy(hop).wait_send()

        @pl.loop(0, levels)
        def _(item):
            @pl.loop(0, cuts)
            def _(owner):
                core_copy(owner, item).wait_send()

            @pl.when(after)
            def _():
                @pl.loop(0, cut + 1)
                def _(owner):
                    right_copy(owner, item).wait_send()

            @pl.when(before)
            def _():
                @pl.loop(cut, cuts)
                def _(owner):
                    left_copy(owner, item).wait_send()

    fast_copy(vbuf, 1).wait_recv()

    def arrive(step):
        for start, length in value_pieces:
            @pl.when(hub & has_slow & (step == start))
            def _():
                slow_copy(vbuf, v_send, v_recv, start, length).wait_recv()

        @pl.when(~hub & has_slow)
        def _():
            slow_copy(vbuf, v_send, v_recv, step).wait_recv()

    def far_mixed(block, head):
        return jnp.dot(
            fwbuf[head, block], far_rows(1, block, head),
            preferred_element_type=jnp.float32,
        )

    @pl.loop(0, chunks - 1)
    def _(step):
        arrive(step)
        for inner in range(CHUNK_HEADS):
            head = step * CHUNK_HEADS + inner
            columns = pl.ds(pl.multiple_of(head * HEAD, HEAD), HEAD)
            for block in range(blocks):
                near_values = vbuf[pl.ds(block * BLOCK, span), columns]
                mixed = jnp.dot(
                    wbuf[head, block], near_values, preferred_element_type=jnp.float32
                ) + far_mixed(block, head)
                out_ref[block * BLOCK : (block + 1) * BLOCK, columns] = (
                    mixed * inv[head, block]
                ).astype(out_ref.dtype)

    final = [
        (chunks * CHUNK_HEADS - CHUNK_HEADS + inner, block)
        for inner in range(CHUNK_HEADS)
        for block in range(blocks)
    ]

    def final_dot(head, block, first, stop):
        first, stop = max(first, block * BLOCK), min(stop, block * BLOCK + span)
        return jnp.dot(
            wbuf[head, block, :, first - block * BLOCK : stop - block * BLOCK],
            vbuf[first:stop, head * HEAD : (head + 1) * HEAD],
            preferred_element_type=jnp.float32,
        )

    def final_near(first, stop):
        for n, (head, block) in enumerate(final):
            early[n] = final_dot(head, block, first, stop) + far_mixed(block, head)

    def final_slow(first, stop):
        for n, (head, block) in enumerate(final):
            mixed = early[n] + final_dot(head, block, first, stop)
            out_ref[
                block * BLOCK : (block + 1) * BLOCK, head * HEAD : (head + 1) * HEAD
            ] = (mixed * inv[head, block]).astype(out_ref.dtype)

    pl.when(odd)(lambda: final_near(0, edge))
    pl.when(~odd)(lambda: final_near(halo, edge + halo))

    for mine, pieces in ((hub, straight_keys), (~hub, other_keys)):
        @pl.when(mine & has_slow)
        def _():
            for start, length in pieces:
                slow_copy(kbuf, k_send, k_recv, start, length).wait_send()

    @pl.when(hub)
    def _():
        @pl.loop(0, borrowed)
        def _(item):
            relay_copy(item).wait_send()

        @pl.loop(0, passed)
        def _(number):
            relay_part(number).wait_send()

    @pl.when(hub & has_slow)
    def _():
        for start, length in value_pieces[:-1]:
            slow_copy(vbuf, v_send, v_recv, start, length).wait_send()

    arrive(chunks - 1)
    pl.when(odd)(lambda: final_slow(edge, edge + halo))
    pl.when(~odd)(lambda: final_slow(0, halo))

    @pl.when(~hub)
    def _():
        @pl.loop(0, borrowed)
        def _(step):
            relay_copy(step).wait_send()

    @pl.when(hub & has_slow)
    def _():
        start, length = value_pieces[-1]
        slow_copy(vbuf, v_send, v_recv, start, length).wait_send()

    @pl.when(ends_after | ends_before)
    def _():
        @pl.loop(chunks // 2, chunks)
        def _(step):
            lend_copy(step).wait_send()

    @pl.when(~hub & has_slow & ~(ends_after | ends_before))
    def _():
        @pl.loop(0, lent)
        def _(step):
            slow_copy(vbuf, v_send, v_recv, step).wait_send()

        @pl.when(rest > 0)
        def _():
            @pl.loop(0, QUARTERS)
            def _(number):
                slow_part(number).wait_send()

        @pl.loop(lent + jnp.where(rest > 0, 1, 0), chunks)
        def _(step):
            slow_copy(vbuf, v_send, v_recv, step).wait_send()


def shards(cuts, group, queries, keys, values, window, summary_index):
    rows, width = queries.shape
    blocks = rows // BLOCK
    heads = width // HEAD
    listed = summary_index.shape[1]
    count = cuts * group
    levels = group // SEATS
    chunk = CHUNK_HEADS * HEAD
    chunks = width // chunk
    halo = REACH * BLOCK
    held = rows + 2 * halo
    span = (2 * REACH + 1) * BLOCK
    dma = pltpu.SemaphoreType.DMA
    return pl.pallas_call(
        functools.partial(kernel, cuts, group),
        out_shape=jax.ShapeDtypeStruct((rows, width), jnp.bfloat16),
        in_specs=[pl.BlockSpec(memory_space=pltpu.HBM)] * 5,
        out_specs=pl.BlockSpec(memory_space=pltpu.VMEM),
        scratch_shapes=[
            pltpu.VMEM((rows, width), jnp.bfloat16),
            pltpu.VMEM((held, width), jnp.bfloat16),
            pltpu.VMEM((held, width), jnp.bfloat16),
            pltpu.VMEM((chunks, halo, chunk), jnp.bfloat16),
            pltpu.SMEM(window.shape, jnp.int32),
            pltpu.SMEM(summary_index.shape, jnp.int32),
            pltpu.VMEM((2, blocks, heads, HEAD), jnp.bfloat16),
            pltpu.VMEM((count, 2, blocks, heads, HEAD), jnp.bfloat16),
            pltpu.VMEM((2, blocks, listed * heads, HEAD), jnp.float32),
            pltpu.VMEM((heads, blocks, BLOCK, span), jnp.bfloat16),
            pltpu.VMEM((heads, blocks, BLOCK, listed), jnp.bfloat16),
            pltpu.VMEM((heads, blocks, BLOCK, 1), jnp.float32),
            pltpu.VMEM((CHUNK_HEADS * blocks, BLOCK, HEAD), jnp.float32),
            dma((5,)),
            *[dma((chunks,))] * 4,
            *[dma((2,))] * 2,
            *[dma((chunks,))] * 2,
            *[dma((QUARTERS,))] * 3,
            *[dma((3,))] * 2,
            *[dma((cuts, levels))] * 2,
            *[dma((levels,))] * 2,
            *[dma((cuts, levels))] * 4,
            *[pltpu.SemaphoreType.REGULAR] * 2,
        ],
        compiler_params=pltpu.CompilerParams(
            collective_id=0, has_side_effects=True, vmem_limit_bytes=48 * 1024 * 1024
        ),
    )(
        *(
            pltpu.with_memory_space_constraint(operand, pltpu.HBM)
            for operand in (queries, keys, values, window, summary_index)
        )
    )


def solution(mesh):
    return jax.shard_map(
        functools.partial(shards, mesh.shape["cuts"], mesh.shape["group"]),
        mesh=mesh,
        in_specs=(
            P(("cuts", "group"), None),
            P(("cuts", "group"), None),
            P(("cuts", "group"), None),
            P(("cuts", "group")),
            P(("cuts", "group"), None),
        ),
        out_specs=P(("cuts", "group"), None),
        check_vma=False,
    )
```

```python
import functools

import jax
import jax.numpy as jnp
from jax import lax
from jax.experimental import pallas as pl
from jax.experimental.pallas import tpu as pltpu
from jax.sharding import PartitionSpec as P

HEAD = 128
BLOCK = 128
REACH = 2
CHUNK_HEADS = 2
SEATS = 4
QUARTERS = 4
MESH = pl.DeviceIdType.MESH


def pieces_of(*lengths):
    starts = [sum(lengths[:n]) for n in range(len(lengths))]
    return [(start, length) for start, length in zip(starts, lengths) if length]


def kernel(
    cuts, group,
    q_hbm, k_hbm, v_hbm, window_hbm, index_hbm, out_ref,
    qbuf, kbuf, vbuf, relay, window_ref, index_ref, own, pool, far, wbuf, fwbuf, inv, early,
    local_sem, k_send, k_recv, v_send, v_recv, fast_send, fast_recv,
    relay_send, relay_recv, part_send, part_recv, pass_send, own_send, own_recv, core_send, core_recv,
    level_send, level_recv,
    right_send, right_recv, left_send, left_recv, go_sem, far_sem,
):
    count = cuts * group
    rows, width = q_hbm.shape
    blocks = rows // BLOCK
    heads = width // HEAD
    halo = REACH * BLOCK
    span = (2 * REACH + 1) * BLOCK
    chunk = CHUNK_HEADS * HEAD
    chunks = width // chunk
    listed = index_ref.shape[1]
    levels = group // SEATS
    top = levels - 1

    cut = lax.axis_index("cuts")
    spot = lax.axis_index("group")
    me = cut * group + spot
    seat = lax.rem(spot, SEATS)
    level = spot // SEATS
    odd = lax.rem(seat, 2) == 1
    hub = (seat == 1) | (seat == 2)
    below, above = level > 0, level < top
    before, after = cut > 0, cut < cuts - 1

    fast_peer = jnp.where(odd, me - 1, me + 1)
    slow_peer = jnp.where(odd, me + 1, me - 1)
    has_slow = (slow_peer >= 0) & (slow_peer < count)
    across = jnp.where(seat < 2, me + 2, me - 2)

    trim = jnp.minimum(top - level, jnp.where(cut == 0, 2, 1))
    upward = jnp.maximum((top - level) * chunks * QUARTERS // levels - trim, 0)
    downward = level * chunks // levels * QUARTERS
    quarters = jnp.where(
        seat == 3,
        jnp.where(above, upward, chunks * QUARTERS),
        jnp.where(seat == 0, jnp.where(below, downward, chunks * QUARTERS), 0),
    )
    quarters = jnp.where(has_slow, quarters, 0)
    lent = quarters // QUARTERS
    rest = quarters - lent * QUARTERS
    lend_peer = jnp.where(
        seat == 3,
        jnp.where(above, me - 2, me + SEATS),
        jnp.where(below, me + 2, me - SEATS),
    )
    relay_up = (seat == 1) & above
    relay_down = (seat == 2) & below
    ends_after = (seat == 3) & (level == top) & after
    ends_before = (seat == 0) & (level == 0) & before
    relay_after = (seat == 3) & (level == 0) & before
    relay_before = (seat == 0) & (level == top) & after
    taken = jnp.where(
        relay_up,
        upward,
        jnp.where(
            relay_down,
            downward,
            jnp.where(relay_after | relay_before, chunks * QUARTERS, 0),
        ),
    )
    borrowed = taken // QUARTERS
    passed = taken - borrowed * QUARTERS
    relay_peer = jnp.where(
        relay_up | relay_before, me + (SEATS - 1), me - (SEATS - 1)
    )

    def place(device):
        return (device // group, lax.rem(device, group))

    barrier = pltpu.get_barrier_semaphore()

    def greet(device, present=None):
        def signal():
            pl.semaphore_signal(
                barrier, inc=1, device_id=place(device), device_id_type=MESH
            )

        if present is None:
            signal()
        else:
            pl.when(present)(signal)

    greet(slow_peer, has_slow)
    greet(fast_peer)
    greet(across, hub)
    @pl.when(hub)
    def _():
        @pl.loop(1, levels)
        def _(hop):
            greet(cut * group + lax.rem(fast_peer - cut * group + hop * SEATS, group))

    greet(fast_peer - group, hub & before)
    greet(fast_peer + group, hub & after)
    greet(me - SEATS, relay_after)
    greet(me + SEATS, relay_before)
    greet(me - SEATS, (seat == 0) & below)
    greet(me + SEATS, (seat == 3) & above)
    greet(me - (SEATS - 1), ends_after)
    greet(me + (SEATS - 1), ends_before)
    expected = 1 + jnp.where(hub, 0, levels - 1)
    for present in (
        has_slow, ~hub, ~hub & before, ~hub & after,
        (seat == 0) & above, (seat == 3) & below,
        relay_after, relay_before, ends_after, ends_before,
    ):
        expected = expected + jnp.where(present, 1, 0)

    loads = [
        pltpu.make_async_copy(k_hbm, kbuf.at[pl.ds(halo, rows)], local_sem.at[0]),
        pltpu.make_async_copy(v_hbm, vbuf.at[pl.ds(halo, rows)], local_sem.at[1]),
        pltpu.make_async_copy(q_hbm, qbuf, local_sem.at[2]),
        pltpu.make_async_copy(window_hbm, window_ref, local_sem.at[3]),
        pltpu.make_async_copy(index_hbm, index_ref, local_sem.at[4]),
    ]
    for load in loads:
        load.start()

    def remote(source, target, send, recv, device):
        return pltpu.make_async_remote_copy(
            src_ref=source, dst_ref=target, send_sem=send, recv_sem=recv,
            device_id=place(device), device_id_type=MESH,
        )

    def columns_of(step):
        return pl.ds(pl.multiple_of(step * chunk, chunk), chunk)

    most = chunks - chunks // 2
    straight_keys = pieces_of(1, chunks // 2 - 1, most)
    other_keys = pieces_of(
        1, chunks // 2 - 1, most // 2, most // 4, most - most // 2 - most // 4
    )
    value_pieces = pieces_of(chunks - 2 - (chunks - 2) // 2, (chunks - 2) // 2, 1, 1)
    edge = halo + rows
    slow_from = pl.ds(pl.multiple_of(jnp.where(odd, rows, halo), BLOCK), halo)
    first_from = pl.ds(pl.multiple_of(jnp.where(odd, rows - halo, 0), BLOCK), halo)
    slow_to = pl.ds(pl.multiple_of(jnp.where(odd, 0, edge), BLOCK), halo)
    fast_from = pl.ds(pl.multiple_of(jnp.where(odd, halo, rows), BLOCK), halo)
    fast_to = pl.ds(pl.multiple_of(jnp.where(odd, edge, 0), BLOCK), halo)
    relay_to = pl.ds(
        pl.multiple_of(jnp.where(relay_up | relay_after, 0, edge), BLOCK), halo
    )

    def slow_copy(buffer, send, recv, step, length=1):
        columns = pl.ds(pl.multiple_of(step * chunk, chunk), length * chunk)
        return remote(
            buffer.at[slow_from, columns], buffer.at[slow_to, columns],
            send.at[step], recv.at[step], slow_peer,
        )

    piece = halo // QUARTERS

    def rows_of(start, number):
        return pl.ds(pl.multiple_of(start + number * piece, piece), piece)

    def slow_part(number):
        return remote(
            vbuf.at[rows_of(jnp.where(odd, rows, halo), number), columns_of(lent)],
            vbuf.at[rows_of(jnp.where(odd, 0, edge), number), columns_of(lent)],
            part_send.at[number], v_recv.at[lent], slow_peer,
        )

    def lend_part(number):
        return remote(
            vbuf.at[rows_of(jnp.where(odd, rows, halo), number), columns_of(lent)],
            relay.at[lent, rows_of(0, number)],
            part_send.at[number], part_recv.at[number], lend_peer,
        )

    def relay_part(number):
        return remote(
            relay.at[borrowed, rows_of(0, number)],
            vbuf.at[
                rows_of(jnp.where(relay_up | relay_after, 0, edge), number),
                columns_of(borrowed),
            ],
            pass_send.at[number], v_recv.at[borrowed], relay_peer,
        )

    def take_part(number):
        return remote(
            vbuf.at[rows_of(halo, number), columns_of(borrowed)],
            relay.at[borrowed, rows_of(0, number)],
            part_send.at[number], part_recv.at[number], lend_peer,
        )

    def fast_copy(buffer, part):
        return remote(
            buffer.at[fast_from], buffer.at[fast_to],
            fast_send.at[part], fast_recv.at[part], fast_peer,
        )

    def lend_copy(step):
        return remote(
            vbuf.at[slow_from, columns_of(step)], relay.at[step],
            v_send.at[step], relay_recv.at[step], lend_peer,
        )

    def relay_copy(step):
        return remote(
            relay.at[step], vbuf.at[relay_to, columns_of(step)],
            relay_send.at[step], v_recv.at[step], relay_peer,
        )

    def own_copy(place_of, device):
        return remote(
            own, pool.at[me], own_send.at[place_of], own_recv.at[place_of], device
        )

    def quad_copy(owner, item, send, recv, device):
        held = pool.at[pl.ds(owner * group + item * SEATS, SEATS)]
        return remote(held, held, send, recv, device)

    def level_copy(hop):
        return quad_copy(
            cut, level, level_send.at[hop], level_recv.at[hop],
            cut * group + lax.rem(spot + hop * SEATS, group),
        )

    def right_copy(owner, item):
        return quad_copy(
            owner, item, right_send.at[owner, item], right_recv.at[owner, item], me + group
        )

    def left_copy(owner, item):
        return quad_copy(
            owner, item, left_send.at[owner, item], left_recv.at[owner, item], me - group
        )

    def core_copy(owner, item):
        return quad_copy(
            owner, item, core_send.at[owner, item], core_recv.at[owner, item], fast_peer
        )

    def first_copy():
        length = straight_keys[0][1] * chunk
        return remote(
            k_hbm.at[first_from, pl.ds(0, length)], kbuf.at[slow_to, pl.ds(0, length)],
            k_send.at[0], k_recv.at[0], slow_peer,
        )

    @pl.when(hub)
    def _():
        pl.semaphore_wait(barrier, expected)

        @pl.when(has_slow)
        def _():
            first_copy().start()

    ones = jnp.ones((heads, BLOCK), jnp.bfloat16)
    row = lax.broadcasted_iota(jnp.int32, (heads, HEAD), 0)
    for part, (buffer, divisor) in enumerate(
        ((kbuf, jnp.sqrt(jnp.float32(BLOCK))), (vbuf, jnp.float32(BLOCK)))
    ):
        loads[part].wait()
        for block in range(blocks):
            pooled = jnp.zeros((heads, HEAD), jnp.float32)
            sums = jnp.dot(
                ones,
                buffer[halo + block * BLOCK : halo + (block + 1) * BLOCK, :],
                preferred_element_type=jnp.float32,
            )
            for head in range(heads):
                pooled = jnp.where(
                    row == head, sums[:, head * HEAD : (head + 1) * HEAD], pooled
                )
            own[part, block] = (pooled / divisor).astype(jnp.bfloat16)
    @pl.when(~hub)
    def _():
        pl.semaphore_wait(barrier, expected)

    @pl.when(hub)
    def _():
        own_copy(0, slow_peer).start()

    @pl.when(~hub)
    def _():
        own_copy(1, across).start()
        own_copy(2, fast_peer).start()
        pl.semaphore_signal(
            far_sem, inc=1, device_id=place(fast_peer), device_id_type=MESH
        )

    def send_slow(whole):
        @pl.when(has_slow)
        def _():
            for start, length in straight_keys[1:] if whole else other_keys:
                slow_copy(kbuf, k_send, k_recv, start, length).start()

            if whole:
                for start, length in value_pieces:
                    slow_copy(vbuf, v_send, v_recv, start, length).start()
            else:
                @pl.when(rest > 0)
                def _():
                    @pl.loop(rest, QUARTERS)
                    def _(number):
                        slow_part(number).start()

                @pl.loop(lent + jnp.where(rest > 0, 1, 0), chunks)
                def _(step):
                    slow_copy(vbuf, v_send, v_recv, step).start()

    @pl.loop(0, lent)
    def _(step):
        lend_copy(step).start()

    @pl.loop(0, rest)
    def _(number):
        lend_part(number).start()

    pl.when(hub)(lambda: send_slow(True))
    fast_copy(kbuf, 0).start()
    fast_copy(vbuf, 1).start()

    @pl.when(me == 0)
    def _():
        kbuf[pl.ds(0, halo), :] = jnp.zeros((halo, width), kbuf.dtype)
        vbuf[pl.ds(0, halo), :] = jnp.zeros((halo, width), vbuf.dtype)

    @pl.when(me == count - 1)
    def _():
        kbuf[pl.ds(edge, halo), :] = jnp.zeros((halo, width), kbuf.dtype)
        vbuf[pl.ds(edge, halo), :] = jnp.zeros((halo, width), vbuf.dtype)

    def spread(item):
        @pl.when(after)
        def _():
            right_copy(cut, item).start()

        @pl.when(before)
        def _():
            left_copy(cut, item).start()

        core_copy(cut, item).start()

    @pl.when(hub)
    def _():
        pool[me] = own[...]
        own_copy(0, slow_peer).wait_recv()
        own_copy(1, across).wait_recv()
        own_copy(2, fast_peer).wait_recv()
        pl.semaphore_wait(far_sem, 1)

        @pl.loop(1, levels)
        def _(hop):
            level_copy(hop).start()

        @pl.when(relay_up | relay_down)
        def _():
            pl.semaphore_signal(
                go_sem, inc=1, device_id=place(relay_peer), device_id_type=MESH
            )

        spread(level)

        @pl.loop(1, levels)
        def _(hop):
            level_copy(hop).wait_recv()
            spread(lax.rem(level + levels - hop, levels))

        @pl.loop(1, cuts)
        def _(hop):
            @pl.loop(0, levels)
            def _(item):
                @pl.when(cut >= hop)
                def _():
                    right_copy(cut - hop, item).wait_recv()

                    @pl.when(after)
                    def _():
                        right_copy(cut - hop, item).start()

                    core_copy(cut - hop, item).start()

                @pl.when(cut + hop < cuts)
                def _():
                    left_copy(cut + hop, item).wait_recv()

                    @pl.when(before)
                    def _():
                        left_copy(cut + hop, item).start()

                    core_copy(cut + hop, item).start()

    @pl.when(~hub)
    def _():
        @pl.when(((seat == 3) & above) | ((seat == 0) & below))
        def _():
            pl.semaphore_wait(go_sem, 1)

        @pl.when(ends_after | ends_before)
        def _():
            @pl.loop(0, chunks // 2)
            def _(step):
                lend_copy(step).wait_send()

        send_slow(False)

        @pl.loop(0, borrowed)
        def _(step):
            lend_copy(step).wait_recv()
            relay_copy(step).start()

        @pl.loop(0, cuts)
        def _(owner):
            @pl.loop(0, levels)
            def _(item):
                core_copy(owner, item).wait_recv()

    for load in loads[2:]:
        load.wait()

    for part in range(2):
        for block in range(blocks):
            for entry in range(listed):
                name = index_ref[block, entry]
                tile = pool[name // blocks, part, lax.rem(name, blocks)]
                far[part, block, pl.ds(entry * heads, heads), :] = tile.astype(jnp.float32)

    scale = 1.0 / jnp.sqrt(jnp.float32(HEAD))
    contract = (((1,), (1,)), ((), ()))
    total_blocks = count * blocks

    def far_rows(part, block, head):
        return far[part, block, pl.ds(head, listed, stride=heads), :].astype(jnp.bfloat16)

    fast_copy(kbuf, 0).wait_recv()

    @pl.loop(0, chunks)
    def _(step):
        for mine, pieces in ((hub, straight_keys), (~hub, other_keys)):
            for start, length in pieces:
                @pl.when(mine & has_slow & (step == start))
                def _():
                    slow_copy(kbuf, k_send, k_recv, start, length).wait_recv()

        for inner in range(CHUNK_HEADS):
            head = step * CHUNK_HEADS + inner
            columns = pl.ds(pl.multiple_of(head * HEAD, HEAD), HEAD)
            for block in range(blocks):
                query = qbuf[block * BLOCK : (block + 1) * BLOCK, columns]
                near_keys = kbuf[pl.ds(block * BLOCK, span), columns]
                scores = lax.dot_general(
                    query, near_keys, contract, preferred_element_type=jnp.float32
                )
                far_scores = lax.dot_general(
                    query, far_rows(0, block, head), contract,
                    preferred_element_type=jnp.float32,
                )
                own = me * blocks + block
                pieces = []
                for place_of in range(2 * REACH + 1):
                    offset = place_of - REACH
                    piece = scores[:, place_of * BLOCK : (place_of + 1) * BLOCK]
                    if offset:
                        other = own + offset
                        allowed = (
                            (window_ref[block] >= abs(offset))
                            & (other >= 0)
                            & (other < total_blocks)
                        )
                        piece = jnp.where(allowed, piece, -1e30)
                    pieces.append(piece)
                tallest = functools.reduce(jnp.maximum, pieces)
                top = jnp.maximum(
                    jnp.max(tallest, axis=1, keepdims=True),
                    jnp.max(far_scores, axis=1, keepdims=True),
                )
                weights = [jnp.exp((piece - top) * scale) for piece in pieces]
                far_weights = jnp.exp((far_scores - top) * scale)
                total = jnp.sum(
                    functools.reduce(jnp.add, weights), axis=1, keepdims=True
                ) + jnp.sum(far_weights, axis=1, keepdims=True)
                for place_of, weight in enumerate(weights):
                    wbuf[head, block, :, place_of * BLOCK : (place_of + 1) * BLOCK] = (
                        weight.astype(jnp.bfloat16)
                    )
                fwbuf[head, block] = far_weights.astype(jnp.bfloat16)
                inv[head, block] = 1.0 / total

        @pl.when(hub & (step < borrowed))
        def _():
            lend_copy(step).wait_recv()
            relay_copy(step).start()

        @pl.when(hub & (step == borrowed))
        def _():
            @pl.loop(0, passed)
            def _(number):
                take_part(number).wait_recv()
                relay_part(number).start()

    fast_copy(kbuf, 0).wait_send()
    fast_copy(vbuf, 1).wait_send()

    @pl.when(~hub)
    def _():
        own_copy(1, across).wait_send()
        own_copy(2, fast_peer).wait_send()

    @pl.when(hub)
    def _():
        own_copy(0, slow_peer).wait_send()

        @pl.loop(1, levels)
        def _(hop):
            level_copy(hop).wait_send()

        @pl.loop(0, levels)
        def _(item):
            @pl.loop(0, cuts)
            def _(owner):
                core_copy(owner, item).wait_send()

            @pl.when(after)
            def _():
                @pl.loop(0, cut + 1)
                def _(owner):
                    right_copy(owner, item).wait_send()

            @pl.when(before)
            def _():
                @pl.loop(cut, cuts)
                def _(owner):
                    left_copy(owner, item).wait_send()

    fast_copy(vbuf, 1).wait_recv()

    def arrive(step):
        for start, length in value_pieces:
            @pl.when(hub & has_slow & (step == start))
            def _():
                slow_copy(vbuf, v_send, v_recv, start, length).wait_recv()

        @pl.when(~hub & has_slow)
        def _():
            slow_copy(vbuf, v_send, v_recv, step).wait_recv()

    def far_mixed(block, head):
        return jnp.dot(
            fwbuf[head, block], far_rows(1, block, head),
            preferred_element_type=jnp.float32,
        )

    @pl.loop(0, chunks - 1)
    def _(step):
        arrive(step)
        for inner in range(CHUNK_HEADS):
            head = step * CHUNK_HEADS + inner
            columns = pl.ds(pl.multiple_of(head * HEAD, HEAD), HEAD)
            for block in range(blocks):
                near_values = vbuf[pl.ds(block * BLOCK, span), columns]
                mixed = jnp.dot(
                    wbuf[head, block], near_values, preferred_element_type=jnp.float32
                ) + far_mixed(block, head)
                out_ref[block * BLOCK : (block + 1) * BLOCK, columns] = (
                    mixed * inv[head, block]
                ).astype(out_ref.dtype)

    final = [
        (chunks * CHUNK_HEADS - CHUNK_HEADS + inner, block)
        for inner in range(CHUNK_HEADS)
        for block in range(blocks)
    ]

    def final_dot(head, block, first, stop):
        first, stop = max(first, block * BLOCK), min(stop, block * BLOCK + span)
        return jnp.dot(
            wbuf[head, block, :, first - block * BLOCK : stop - block * BLOCK],
            vbuf[first:stop, head * HEAD : (head + 1) * HEAD],
            preferred_element_type=jnp.float32,
        )

    def final_near(first, stop):
        for n, (head, block) in enumerate(final):
            early[n] = final_dot(head, block, first, stop) + far_mixed(block, head)

    def final_slow(first, stop):
        for n, (head, block) in enumerate(final):
            mixed = early[n] + final_dot(head, block, first, stop)
            out_ref[
                block * BLOCK : (block + 1) * BLOCK, head * HEAD : (head + 1) * HEAD
            ] = (mixed * inv[head, block]).astype(out_ref.dtype)

    pl.when(odd)(lambda: final_near(0, edge))
    pl.when(~odd)(lambda: final_near(halo, edge + halo))

    for mine, pieces in ((hub, straight_keys), (~hub, other_keys)):
        @pl.when(mine & has_slow)
        def _():
            for start, length in pieces:
                slow_copy(kbuf, k_send, k_recv, start, length).wait_send()

    @pl.when(hub)
    def _():
        @pl.loop(0, borrowed)
        def _(item):
            relay_copy(item).wait_send()

        @pl.loop(0, passed)
        def _(number):
            relay_part(number).wait_send()

    @pl.when(hub & has_slow)
    def _():
        for start, length in value_pieces[:-1]:
            slow_copy(vbuf, v_send, v_recv, start, length).wait_send()

    arrive(chunks - 1)
    pl.when(odd)(lambda: final_slow(edge, edge + halo))
    pl.when(~odd)(lambda: final_slow(0, halo))

    @pl.when(~hub)
    def _():
        @pl.loop(0, borrowed)
        def _(step):
            relay_copy(step).wait_send()

    @pl.when(hub & has_slow)
    def _():
        start, length = value_pieces[-1]
        slow_copy(vbuf, v_send, v_recv, start, length).wait_send()

    @pl.when(ends_after | ends_before)
    def _():
        @pl.loop(chunks // 2, chunks)
        def _(step):
            lend_copy(step).wait_send()

    @pl.when(~hub & has_slow & ~(ends_after | ends_before))
    def _():
        @pl.loop(0, lent)
        def _(step):
            slow_copy(vbuf, v_send, v_recv, step).wait_send()

        @pl.when(rest > 0)
        def _():
            @pl.loop(0, QUARTERS)
            def _(number):
                slow_part(number).wait_send()

        @pl.loop(lent + jnp.where(rest > 0, 1, 0), chunks)
        def _(step):
            slow_copy(vbuf, v_send, v_recv, step).wait_send()


def shards(cuts, group, queries, keys, values, window, summary_index):
    rows, width = queries.shape
    blocks = rows // BLOCK
    heads = width // HEAD
    listed = summary_index.shape[1]
    count = cuts * group
    levels = group // SEATS
    chunk = CHUNK_HEADS * HEAD
    chunks = width // chunk
    halo = REACH * BLOCK
    held = rows + 2 * halo
    span = (2 * REACH + 1) * BLOCK
    dma = pltpu.SemaphoreType.DMA
    return pl.pallas_call(
        functools.partial(kernel, cuts, group),
        out_shape=jax.ShapeDtypeStruct((rows, width), jnp.bfloat16),
        in_specs=[pl.BlockSpec(memory_space=pltpu.HBM)] * 5,
        out_specs=pl.BlockSpec(memory_space=pltpu.VMEM),
        scratch_shapes=[
            pltpu.VMEM((rows, width), jnp.bfloat16),
            pltpu.VMEM((held, width), jnp.bfloat16),
            pltpu.VMEM((held, width), jnp.bfloat16),
            pltpu.VMEM((chunks, halo, chunk), jnp.bfloat16),
            pltpu.SMEM(window.shape, jnp.int32),
            pltpu.SMEM(summary_index.shape, jnp.int32),
            pltpu.VMEM((2, blocks, heads, HEAD), jnp.bfloat16),
            pltpu.VMEM((count, 2, blocks, heads, HEAD), jnp.bfloat16),
            pltpu.VMEM((2, blocks, listed * heads, HEAD), jnp.float32),
            pltpu.VMEM((heads, blocks, BLOCK, span), jnp.bfloat16),
            pltpu.VMEM((heads, blocks, BLOCK, listed), jnp.bfloat16),
            pltpu.VMEM((heads, blocks, BLOCK, 1), jnp.float32),
            pltpu.VMEM((CHUNK_HEADS * blocks, BLOCK, HEAD), jnp.float32),
            dma((5,)),
            *[dma((chunks,))] * 4,
            *[dma((2,))] * 2,
            *[dma((chunks,))] * 2,
            *[dma((QUARTERS,))] * 3,
            *[dma((3,))] * 2,
            *[dma((cuts, levels))] * 2,
            *[dma((levels,))] * 2,
            *[dma((cuts, levels))] * 4,
            *[pltpu.SemaphoreType.REGULAR] * 2,
        ],
        compiler_params=pltpu.CompilerParams(
            collective_id=0, has_side_effects=True, vmem_limit_bytes=48 * 1024 * 1024
        ),
    )(
        *(
            pltpu.with_memory_space_constraint(operand, pltpu.HBM)
            for operand in (queries, keys, values, window, summary_index)
        )
    )


def solution(mesh):
    return jax.shard_map(
        functools.partial(shards, mesh.shape["cuts"], mesh.shape["group"]),
        mesh=mesh,
        in_specs=(
            P(("cuts", "group"), None),
            P(("cuts", "group"), None),
            P(("cuts", "group"), None),
            P(("cuts", "group")),
            P(("cuts", "group"), None),
        ),
        out_specs=P(("cuts", "group"), None),
        check_vma=False,
    )
```

```python
import functools

import jax
import jax.numpy as jnp
from jax import lax
from jax.experimental import pallas as pl
from jax.experimental.pallas import tpu as pltpu
from jax.sharding import PartitionSpec as P

HEAD = 128
BLOCK = 128
REACH = 2
CHUNK_HEADS = 2
SEATS = 4
QUARTERS = 4
MESH = pl.DeviceIdType.MESH


def pieces_of(*lengths):
    starts = [sum(lengths[:n]) for n in range(len(lengths))]
    return [(start, length) for start, length in zip(starts, lengths) if length]


def kernel(
    cuts, group,
    q_hbm, k_hbm, v_hbm, window_hbm, index_hbm, out_ref,
    qbuf, kbuf, vbuf, relay, window_ref, index_ref, own, pool, far, wbuf, fwbuf, inv, early,
    local_sem, k_send, k_recv, v_send, v_recv, fast_send, fast_recv,
    relay_send, relay_recv, part_send, part_recv, pass_send, own_send, own_recv, core_send, core_recv,
    level_send, level_recv,
    right_send, right_recv, left_send, left_recv, go_sem, far_sem,
):
    count = cuts * group
    rows, width = q_hbm.shape
    blocks = rows // BLOCK
    heads = width // HEAD
    halo = REACH * BLOCK
    span = (2 * REACH + 1) * BLOCK
    chunk = CHUNK_HEADS * HEAD
    chunks = width // chunk
    listed = index_ref.shape[1]
    levels = group // SEATS
    top = levels - 1

    cut = lax.axis_index("cuts")
    spot = lax.axis_index("group")
    me = cut * group + spot
    seat = lax.rem(spot, SEATS)
    level = spot // SEATS
    odd = lax.rem(seat, 2) == 1
    hub = (seat == 1) | (seat == 2)
    below, above = level > 0, level < top
    before, after = cut > 0, cut < cuts - 1

    fast_peer = jnp.where(odd, me - 1, me + 1)
    slow_peer = jnp.where(odd, me + 1, me - 1)
    has_slow = (slow_peer >= 0) & (slow_peer < count)
    across = jnp.where(seat < 2, me + 2, me - 2)

    trim = jnp.where(cut == 0, jnp.minimum(top - level, 2), 0)
    upward = jnp.maximum((top - level) * chunks * QUARTERS // levels - trim, 0)
    downward = level * chunks // levels * QUARTERS
    quarters = jnp.where(
        seat == 3,
        jnp.where(above, upward, chunks * QUARTERS),
        jnp.where(seat == 0, jnp.where(below, downward, chunks * QUARTERS), 0),
    )
    quarters = jnp.where(has_slow, quarters, 0)
    lent = quarters // QUARTERS
    rest = quarters - lent * QUARTERS
    lend_peer = jnp.where(
        seat == 3,
        jnp.where(above, me - 2, me + SEATS),
        jnp.where(below, me + 2, me - SEATS),
    )
    relay_up = (seat == 1) & above
    relay_down = (seat == 2) & below
    ends_after = (seat == 3) & (level == top) & after
    ends_before = (seat == 0) & (level == 0) & before
    relay_after = (seat == 3) & (level == 0) & before
    relay_before = (seat == 0) & (level == top) & after
    taken = jnp.where(
        relay_up,
        upward,
        jnp.where(
            relay_down,
            downward,
            jnp.where(relay_after | relay_before, chunks * QUARTERS, 0),
        ),
    )
    borrowed = taken // QUARTERS
    passed = taken - borrowed * QUARTERS
    relay_peer = jnp.where(
        relay_up | relay_before, me + (SEATS - 1), me - (SEATS - 1)
    )

    def place(device):
        return (device // group, lax.rem(device, group))

    barrier = pltpu.get_barrier_semaphore()

    def greet(device, present=None):
        def signal():
            pl.semaphore_signal(
                barrier, inc=1, device_id=place(device), device_id_type=MESH
            )

        if present is None:
            signal()
        else:
            pl.when(present)(signal)

    greet(slow_peer, has_slow)
    greet(fast_peer)
    greet(across, hub)
    @pl.when(hub)
    def _():
        @pl.loop(1, levels)
        def _(hop):
            greet(cut * group + lax.rem(fast_peer - cut * group + hop * SEATS, group))

    greet(fast_peer - group, hub & before)
    greet(fast_peer + group, hub & after)
    greet(me - SEATS, relay_after)
    greet(me + SEATS, relay_before)
    greet(me - SEATS, (seat == 0) & below)
    greet(me + SEATS, (seat == 3) & above)
    greet(me - (SEATS - 1), ends_after)
    greet(me + (SEATS - 1), ends_before)
    expected = 1 + jnp.where(hub, 0, levels - 1)
    for present in (
        has_slow, ~hub, ~hub & before, ~hub & after,
        (seat == 0) & above, (seat == 3) & below,
        relay_after, relay_before, ends_after, ends_before,
    ):
        expected = expected + jnp.where(present, 1, 0)

    loads = [
        pltpu.make_async_copy(k_hbm, kbuf.at[pl.ds(halo, rows)], local_sem.at[0]),
        pltpu.make_async_copy(v_hbm, vbuf.at[pl.ds(halo, rows)], local_sem.at[1]),
        pltpu.make_async_copy(q_hbm, qbuf, local_sem.at[2]),
        pltpu.make_async_copy(window_hbm, window_ref, local_sem.at[3]),
        pltpu.make_async_copy(index_hbm, index_ref, local_sem.at[4]),
    ]
    for load in loads:
        load.start()

    def remote(source, target, send, recv, device):
        return pltpu.make_async_remote_copy(
            src_ref=source, dst_ref=target, send_sem=send, recv_sem=recv,
            device_id=place(device), device_id_type=MESH,
        )

    def columns_of(step):
        return pl.ds(pl.multiple_of(step * chunk, chunk), chunk)

    most = chunks - chunks // 2
    straight_keys = pieces_of(1, chunks - 1)
    other_keys = pieces_of(
        1, chunks // 2 - 1, most // 2, most // 4, most - most // 2 - most // 4
    )
    value_pieces = pieces_of(chunks - 2 - (chunks - 2) // 2, (chunks - 2) // 2, 1, 1)
    edge = halo + rows
    slow_from = pl.ds(pl.multiple_of(jnp.where(odd, rows, halo), BLOCK), halo)
    first_from = pl.ds(pl.multiple_of(jnp.where(odd, rows - halo, 0), BLOCK), halo)
    slow_to = pl.ds(pl.multiple_of(jnp.where(odd, 0, edge), BLOCK), halo)
    fast_from = pl.ds(pl.multiple_of(jnp.where(odd, halo, rows), BLOCK), halo)
    fast_to = pl.ds(pl.multiple_of(jnp.where(odd, edge, 0), BLOCK), halo)
    relay_to = pl.ds(
        pl.multiple_of(jnp.where(relay_up | relay_after, 0, edge), BLOCK), halo
    )

    def slow_copy(buffer, send, recv, step, length=1):
        columns = pl.ds(pl.multiple_of(step * chunk, chunk), length * chunk)
        return remote(
            buffer.at[slow_from, columns], buffer.at[slow_to, columns],
            send.at[step], recv.at[step], slow_peer,
        )

    piece = halo // QUARTERS

    def rows_of(start, number):
        return pl.ds(pl.multiple_of(start + number * piece, piece), piece)

    def slow_part(number):
        return remote(
            vbuf.at[rows_of(jnp.where(odd, rows, halo), number), columns_of(lent)],
            vbuf.at[rows_of(jnp.where(odd, 0, edge), number), columns_of(lent)],
            part_send.at[number], v_recv.at[lent], slow_peer,
        )

    def lend_part(number):
        return remote(
            vbuf.at[rows_of(jnp.where(odd, rows, halo), number), columns_of(lent)],
            relay.at[lent, rows_of(0, number)],
            part_send.at[number], part_recv.at[number], lend_peer,
        )

    def relay_part(number):
        return remote(
            relay.at[borrowed, rows_of(0, number)],
            vbuf.at[
                rows_of(jnp.where(relay_up | relay_after, 0, edge), number),
                columns_of(borrowed),
            ],
            pass_send.at[number], v_recv.at[borrowed], relay_peer,
        )

    def take_part(number):
        return remote(
            vbuf.at[rows_of(halo, number), columns_of(borrowed)],
            relay.at[borrowed, rows_of(0, number)],
            part_send.at[number], part_recv.at[number], lend_peer,
        )

    def fast_copy(buffer, part):
        return remote(
            buffer.at[fast_from], buffer.at[fast_to],
            fast_send.at[part], fast_recv.at[part], fast_peer,
        )

    def lend_copy(step):
        return remote(
            vbuf.at[slow_from, columns_of(step)], relay.at[step],
            v_send.at[step], relay_recv.at[step], lend_peer,
        )

    def relay_copy(step):
        return remote(
            relay.at[step], vbuf.at[relay_to, columns_of(step)],
            relay_send.at[step], v_recv.at[step], relay_peer,
        )

    def own_copy(place_of, device):
        return remote(
            own, pool.at[me], own_send.at[place_of], own_recv.at[place_of], device
        )

    def quad_copy(owner, item, send, recv, device):
        held = pool.at[pl.ds(owner * group + item * SEATS, SEATS)]
        return remote(held, held, send, recv, device)

    def level_copy(hop):
        return quad_copy(
            cut, level, level_send.at[hop], level_recv.at[hop],
            cut * group + lax.rem(spot + hop * SEATS, group),
        )

    def right_copy(owner, item):
        return quad_copy(
            owner, item, right_send.at[owner, item], right_recv.at[owner, item], me + group
        )

    def left_copy(owner, item):
        return quad_copy(
            owner, item, left_send.at[owner, item], left_recv.at[owner, item], me - group
        )

    def core_copy(owner, item):
        return quad_copy(
            owner, item, core_send.at[owner, item], core_recv.at[owner, item], fast_peer
        )

    def first_copy():
        length = straight_keys[0][1] * chunk
        return remote(
            k_hbm.at[first_from, pl.ds(0, length)], kbuf.at[slow_to, pl.ds(0, length)],
            k_send.at[0], k_recv.at[0], slow_peer,
        )

    @pl.when(hub)
    def _():
        pl.semaphore_wait(barrier, expected)

        @pl.when(has_slow)
        def _():
            first_copy().start()

    ones = jnp.ones((heads, BLOCK), jnp.bfloat16)
    row = lax.broadcasted_iota(jnp.int32, (heads, HEAD), 0)
    for part, (buffer, divisor) in enumerate(
        ((kbuf, jnp.sqrt(jnp.float32(BLOCK))), (vbuf, jnp.float32(BLOCK)))
    ):
        loads[part].wait()
        for block in range(blocks):
            pooled = jnp.zeros((heads, HEAD), jnp.float32)
            sums = jnp.dot(
                ones,
                buffer[halo + block * BLOCK : halo + (block + 1) * BLOCK, :],
                preferred_element_type=jnp.float32,
            )
            for head in range(heads):
                pooled = jnp.where(
                    row == head, sums[:, head * HEAD : (head + 1) * HEAD], pooled
                )
            own[part, block] = (pooled / divisor).astype(jnp.bfloat16)
    @pl.when(~hub)
    def _():
        pl.semaphore_wait(barrier, expected)

    @pl.when(hub)
    def _():
        own_copy(0, slow_peer).start()

    @pl.when(~hub)
    def _():
        own_copy(1, across).start()
        own_copy(2, fast_peer).start()
        pl.semaphore_signal(
            far_sem, inc=1, device_id=place(fast_peer), device_id_type=MESH
        )

    def send_slow(whole):
        @pl.when(has_slow)
        def _():
            for start, length in straight_keys[1:] if whole else other_keys:
                slow_copy(kbuf, k_send, k_recv, start, length).start()

            if whole:
                for start, length in value_pieces:
                    slow_copy(vbuf, v_send, v_recv, start, length).start()
            else:
                @pl.when(rest > 0)
                def _():
                    @pl.loop(rest, QUARTERS)
                    def _(number):
                        slow_part(number).start()

                @pl.loop(lent + jnp.where(rest > 0, 1, 0), chunks)
                def _(step):
                    slow_copy(vbuf, v_send, v_recv, step).start()

    @pl.loop(0, lent)
    def _(step):
        lend_copy(step).start()

    @pl.loop(0, rest)
    def _(number):
        lend_part(number).start()

    pl.when(hub)(lambda: send_slow(True))
    fast_copy(kbuf, 0).start()
    fast_copy(vbuf, 1).start()

    @pl.when(me == 0)
    def _():
        kbuf[pl.ds(0, halo), :] = jnp.zeros((halo, width), kbuf.dtype)
        vbuf[pl.ds(0, halo), :] = jnp.zeros((halo, width), vbuf.dtype)

    @pl.when(me == count - 1)
    def _():
        kbuf[pl.ds(edge, halo), :] = jnp.zeros((halo, width), kbuf.dtype)
        vbuf[pl.ds(edge, halo), :] = jnp.zeros((halo, width), vbuf.dtype)

    def spread(item):
        @pl.when(after)
        def _():
            right_copy(cut, item).start()

        @pl.when(before)
        def _():
            left_copy(cut, item).start()

        core_copy(cut, item).start()

    @pl.when(hub)
    def _():
        pool[me] = own[...]
        own_copy(0, slow_peer).wait_recv()
        own_copy(1, across).wait_recv()
        own_copy(2, fast_peer).wait_recv()
        pl.semaphore_wait(far_sem, 1)

        @pl.loop(1, levels)
        def _(hop):
            level_copy(hop).start()

        @pl.when(relay_up | relay_down)
        def _():
            pl.semaphore_signal(
                go_sem, inc=1, device_id=place(relay_peer), device_id_type=MESH
            )

        spread(level)

        @pl.loop(1, levels)
        def _(hop):
            level_copy(hop).wait_recv()
            spread(lax.rem(level + levels - hop, levels))

        @pl.loop(1, cuts)
        def _(hop):
            @pl.loop(0, levels)
            def _(item):
                @pl.when(cut >= hop)
                def _():
                    right_copy(cut - hop, item).wait_recv()

                    @pl.when(after)
                    def _():
                        right_copy(cut - hop, item).start()

                    core_copy(cut - hop, item).start()

                @pl.when(cut + hop < cuts)
                def _():
                    left_copy(cut + hop, item).wait_recv()

                    @pl.when(before)
                    def _():
                        left_copy(cut + hop, item).start()

                    core_copy(cut + hop, item).start()

    @pl.when(~hub)
    def _():
        @pl.when(((seat == 3) & above) | ((seat == 0) & below))
        def _():
            pl.semaphore_wait(go_sem, 1)

        @pl.when(ends_after | ends_before)
        def _():
            @pl.loop(0, chunks // 2)
            def _(step):
                lend_copy(step).wait_send()

        send_slow(False)

        @pl.loop(0, borrowed)
        def _(step):
            lend_copy(step).wait_recv()
            relay_copy(step).start()

        @pl.loop(0, cuts)
        def _(owner):
            @pl.loop(0, levels)
            def _(item):
                core_copy(owner, item).wait_recv()

    for load in loads[2:]:
        load.wait()

    for part in range(2):
        for block in range(blocks):
            for entry in range(listed):
                name = index_ref[block, entry]
                tile = pool[name // blocks, part, lax.rem(name, blocks)]
                far[part, block, pl.ds(entry * heads, heads), :] = tile.astype(jnp.float32)

    scale = 1.0 / jnp.sqrt(jnp.float32(HEAD))
    contract = (((1,), (1,)), ((), ()))
    total_blocks = count * blocks

    def far_rows(part, block, head):
        return far[part, block, pl.ds(head, listed, stride=heads), :].astype(jnp.bfloat16)

    fast_copy(kbuf, 0).wait_recv()

    @pl.loop(0, chunks)
    def _(step):
        for mine, pieces in ((hub, straight_keys), (~hub, other_keys)):
            for start, length in pieces:
                @pl.when(mine & has_slow & (step == start))
                def _():
                    slow_copy(kbuf, k_send, k_recv, start, length).wait_recv()

        for inner in range(CHUNK_HEADS):
            head = step * CHUNK_HEADS + inner
            columns = pl.ds(pl.multiple_of(head * HEAD, HEAD), HEAD)
            for block in range(blocks):
                query = qbuf[block * BLOCK : (block + 1) * BLOCK, columns]
                near_keys = kbuf[pl.ds(block * BLOCK, span), columns]
                scores = lax.dot_general(
                    query, near_keys, contract, preferred_element_type=jnp.float32
                )
                far_scores = lax.dot_general(
                    query, far_rows(0, block, head), contract,
                    preferred_element_type=jnp.float32,
                )
                own = me * blocks + block
                pieces = []
                for place_of in range(2 * REACH + 1):
                    offset = place_of - REACH
                    piece = scores[:, place_of * BLOCK : (place_of + 1) * BLOCK]
                    if offset:
                        other = own + offset
                        allowed = (
                            (window_ref[block] >= abs(offset))
                            & (other >= 0)
                            & (other < total_blocks)
                        )
                        piece = jnp.where(allowed, piece, -1e30)
                    pieces.append(piece)
                tallest = functools.reduce(jnp.maximum, pieces)
                top = jnp.maximum(
                    jnp.max(tallest, axis=1, keepdims=True),
                    jnp.max(far_scores, axis=1, keepdims=True),
                )
                weights = [jnp.exp((piece - top) * scale) for piece in pieces]
                far_weights = jnp.exp((far_scores - top) * scale)
                total = jnp.sum(
                    functools.reduce(jnp.add, weights), axis=1, keepdims=True
                ) + jnp.sum(far_weights, axis=1, keepdims=True)
                for place_of, weight in enumerate(weights):
                    wbuf[head, block, :, place_of * BLOCK : (place_of + 1) * BLOCK] = (
                        weight.astype(jnp.bfloat16)
                    )
                fwbuf[head, block] = far_weights.astype(jnp.bfloat16)
                inv[head, block] = 1.0 / total

        @pl.when(hub & (step < borrowed))
        def _():
            lend_copy(step).wait_recv()
            relay_copy(step).start()

        @pl.when(hub & (step == borrowed))
        def _():
            @pl.loop(0, passed)
            def _(number):
                take_part(number).wait_recv()
                relay_part(number).start()

    fast_copy(kbuf, 0).wait_send()
    fast_copy(vbuf, 1).wait_send()

    @pl.when(~hub)
    def _():
        own_copy(1, across).wait_send()
        own_copy(2, fast_peer).wait_send()

    @pl.when(hub)
    def _():
        own_copy(0, slow_peer).wait_send()

        @pl.loop(1, levels)
        def _(hop):
            level_copy(hop).wait_send()

        @pl.loop(0, levels)
        def _(item):
            @pl.loop(0, cuts)
            def _(owner):
                core_copy(owner, item).wait_send()

            @pl.when(after)
            def _():
                @pl.loop(0, cut + 1)
                def _(owner):
                    right_copy(owner, item).wait_send()

            @pl.when(before)
            def _():
                @pl.loop(cut, cuts)
                def _(owner):
                    left_copy(owner, item).wait_send()

    fast_copy(vbuf, 1).wait_recv()

    def arrive(step):
        for start, length in value_pieces:
            @pl.when(hub & has_slow & (step == start))
            def _():
                slow_copy(vbuf, v_send, v_recv, start, length).wait_recv()

        @pl.when(~hub & has_slow)
        def _():
            slow_copy(vbuf, v_send, v_recv, step).wait_recv()

    def far_mixed(block, head):
        return jnp.dot(
            fwbuf[head, block], far_rows(1, block, head),
            preferred_element_type=jnp.float32,
        )

    @pl.loop(0, chunks - 1)
    def _(step):
        arrive(step)
        for inner in range(CHUNK_HEADS):
            head = step * CHUNK_HEADS + inner
            columns = pl.ds(pl.multiple_of(head * HEAD, HEAD), HEAD)
            for block in range(blocks):
                near_values = vbuf[pl.ds(block * BLOCK, span), columns]
                mixed = jnp.dot(
                    wbuf[head, block], near_values, preferred_element_type=jnp.float32
                ) + far_mixed(block, head)
                out_ref[block * BLOCK : (block + 1) * BLOCK, columns] = (
                    mixed * inv[head, block]
                ).astype(out_ref.dtype)

    final = [
        (chunks * CHUNK_HEADS - CHUNK_HEADS + inner, block)
        for inner in range(CHUNK_HEADS)
        for block in range(blocks)
    ]

    def final_dot(head, block, first, stop):
        first, stop = max(first, block * BLOCK), min(stop, block * BLOCK + span)
        return jnp.dot(
            wbuf[head, block, :, first - block * BLOCK : stop - block * BLOCK],
            vbuf[first:stop, head * HEAD : (head + 1) * HEAD],
            preferred_element_type=jnp.float32,
        )

    def final_near(first, stop):
        for n, (head, block) in enumerate(final):
            early[n] = final_dot(head, block, first, stop) + far_mixed(block, head)

    def final_slow(first, stop):
        for n, (head, block) in enumerate(final):
            mixed = early[n] + final_dot(head, block, first, stop)
            out_ref[
                block * BLOCK : (block + 1) * BLOCK, head * HEAD : (head + 1) * HEAD
            ] = (mixed * inv[head, block]).astype(out_ref.dtype)

    pl.when(odd)(lambda: final_near(0, edge))
    pl.when(~odd)(lambda: final_near(halo, edge + halo))

    for mine, pieces in ((hub, straight_keys), (~hub, other_keys)):
        @pl.when(mine & has_slow)
        def _():
            for start, length in pieces:
                slow_copy(kbuf, k_send, k_recv, start, length).wait_send()

    @pl.when(hub)
    def _():
        @pl.loop(0, borrowed)
        def _(item):
            relay_copy(item).wait_send()

        @pl.loop(0, passed)
        def _(number):
            relay_part(number).wait_send()

    @pl.when(hub & has_slow)
    def _():
        for start, length in value_pieces[:-1]:
            slow_copy(vbuf, v_send, v_recv, start, length).wait_send()

    arrive(chunks - 1)
    pl.when(odd)(lambda: final_slow(edge, edge + halo))
    pl.when(~odd)(lambda: final_slow(0, halo))

    @pl.when(~hub)
    def _():
        @pl.loop(0, borrowed)
        def _(step):
            relay_copy(step).wait_send()

    @pl.when(hub & has_slow)
    def _():
        start, length = value_pieces[-1]
        slow_copy(vbuf, v_send, v_recv, start, length).wait_send()

    @pl.when(ends_after | ends_before)
    def _():
        @pl.loop(chunks // 2, chunks)
        def _(step):
            lend_copy(step).wait_send()

    @pl.when(~hub & has_slow & ~(ends_after | ends_before))
    def _():
        @pl.loop(0, lent)
        def _(step):
            slow_copy(vbuf, v_send, v_recv, step).wait_send()

        @pl.when(rest > 0)
        def _():
            @pl.loop(0, QUARTERS)
            def _(number):
                slow_part(number).wait_send()

        @pl.loop(lent + jnp.where(rest > 0, 1, 0), chunks)
        def _(step):
            slow_copy(vbuf, v_send, v_recv, step).wait_send()


def shards(cuts, group, queries, keys, values, window, summary_index):
    rows, width = queries.shape
    blocks = rows // BLOCK
    heads = width // HEAD
    listed = summary_index.shape[1]
    count = cuts * group
    levels = group // SEATS
    chunk = CHUNK_HEADS * HEAD
    chunks = width // chunk
    halo = REACH * BLOCK
    held = rows + 2 * halo
    span = (2 * REACH + 1) * BLOCK
    dma = pltpu.SemaphoreType.DMA
    return pl.pallas_call(
        functools.partial(kernel, cuts, group),
        out_shape=jax.ShapeDtypeStruct((rows, width), jnp.bfloat16),
        in_specs=[pl.BlockSpec(memory_space=pltpu.HBM)] * 5,
        out_specs=pl.BlockSpec(memory_space=pltpu.VMEM),
        scratch_shapes=[
            pltpu.VMEM((rows, width), jnp.bfloat16),
            pltpu.VMEM((held, width), jnp.bfloat16),
            pltpu.VMEM((held, width), jnp.bfloat16),
            pltpu.VMEM((chunks, halo, chunk), jnp.bfloat16),
            pltpu.SMEM(window.shape, jnp.int32),
            pltpu.SMEM(summary_index.shape, jnp.int32),
            pltpu.VMEM((2, blocks, heads, HEAD), jnp.bfloat16),
            pltpu.VMEM((count, 2, blocks, heads, HEAD), jnp.bfloat16),
            pltpu.VMEM((2, blocks, listed * heads, HEAD), jnp.float32),
            pltpu.VMEM((heads, blocks, BLOCK, span), jnp.bfloat16),
            pltpu.VMEM((heads, blocks, BLOCK, listed), jnp.bfloat16),
            pltpu.VMEM((heads, blocks, BLOCK, 1), jnp.float32),
            pltpu.VMEM((CHUNK_HEADS * blocks, BLOCK, HEAD), jnp.float32),
            dma((5,)),
            *[dma((chunks,))] * 4,
            *[dma((2,))] * 2,
            *[dma((chunks,))] * 2,
            *[dma((QUARTERS,))] * 3,
            *[dma((3,))] * 2,
            *[dma((cuts, levels))] * 2,
            *[dma((levels,))] * 2,
            *[dma((cuts, levels))] * 4,
            *[pltpu.SemaphoreType.REGULAR] * 2,
        ],
        compiler_params=pltpu.CompilerParams(
            collective_id=0, has_side_effects=True, vmem_limit_bytes=48 * 1024 * 1024
        ),
    )(
        *(
            pltpu.with_memory_space_constraint(operand, pltpu.HBM)
            for operand in (queries, keys, values, window, summary_index)
        )
    )


def solution(mesh):
    return jax.shard_map(
        functools.partial(shards, mesh.shape["cuts"], mesh.shape["group"]),
        mesh=mesh,
        in_specs=(
            P(("cuts", "group"), None),
            P(("cuts", "group"), None),
            P(("cuts", "group"), None),
            P(("cuts", "group")),
            P(("cuts", "group"), None),
        ),
        out_specs=P(("cuts", "group"), None),
        check_vma=False,
    )
```
